32 devices in a mesh: ctx: 8 (over y, x, core), fsdp: 4 (over z).
Axes of the slice: x: 2, y: 2, z: 4, core: 2. Of those that a mesh axis runs over, the one named last changes fastest.
Arguments:
- hidden: bfloat16 [4096, 1536], P(('fsdp', 'ctx')), may hold values from -6 to 6
- positions: int32 [4096], P('fsdp'), may hold values from 0 to 1023, as said below
- first_gain: bfloat16 [1536], P(('ctx', 'fsdp')), may hold values from 0.099609375 to 1.8984375
- query_weight: bfloat16 [1536, 1536], P(('ctx', 'fsdp')), may hold values from -0.15625 to 0.15625
- key_weight: bfloat16 [1536, 256], P(('ctx', 'fsdp')), may hold values from -0.15625 to 0.15625
- value_weight: bfloat16 [1536, 256], P(('ctx', 'fsdp')), may hold values from -0.15625 to 0.15625
- query_bias: bfloat16 [1536], P(('ctx', 'fsdp')), may hold values from -3 to 3
- key_bias: bfloat16 [256], P(('ctx', 'fsdp')), may hold values from -3 to 3
- value_bias: bfloat16 [256], P(('ctx', 'fsdp')), may hold values from -3 to 3
- output_weight: bfloat16 [1536, 1536], P(('ctx', 'fsdp')), may hold values from -0.625 to 0.625
- second_gain: bfloat16 [1536], P(('ctx', 'fsdp')), may hold values from 0.099609375 to 1.8984375
- gate_weight: bfloat16 [1536, 8960], P(None, ('ctx', 'fsdp')), may hold values from -0.15625 to 0.15625
- up_weight: bfloat16 [1536, 8960], P(None, ('ctx', 'fsdp')), may hold values from -0.15625 to 0.15625
- down_weight: bfloat16 [8960, 1536], P(('ctx', 'fsdp')), may hold values from -0.0625 to 0.0625
- cotangent: bfloat16 [4096, 1536], P(('fsdp', 'ctx')), may hold values from -6 to 6
Outputs:
- layer_output: bfloat16 [4096, 1536], P(('fsdp', 'ctx'))
- input_gradient: float32 [4096, 1536], P(('fsdp', 'ctx'))
- first_gain_gradient: float32 [1536], P(('ctx', 'fsdp'))
- query_weight_gradient: float32 [1536, 1536], P(('ctx', 'fsdp'))
- key_weight_gradient: float32 [1536, 256], P(('ctx', 'fsdp'))
- value_weight_gradient: float32 [1536, 256], P(('ctx', 'fsdp'))
- query_bias_gradient: float32 [1536], P(('ctx', 'fsdp'))
- key_bias_gradient: float32 [256], P(('ctx', 'fsdp'))
- value_bias_gradient: float32 [256], P(('ctx', 'fsdp'))
- output_weight_gradient: float32 [1536, 1536], P(('ctx', 'fsdp'))
- second_gain_gradient: float32 [1536], P(('ctx', 'fsdp'))
- gate_weight_gradient: float32 [1536, 8960], P(None, ('ctx', 'fsdp'))
- up_weight_gradient: float32 [1536, 8960], P(None, ('ctx', 'fsdp'))
- down_weight_gradient: float32 [8960, 1536], P(('ctx', 'fsdp'))
The draws below stay inside these ranges and needn't reach their ends.
Inputs may be any that keep to these rules, and one draw needn't show every extreme that they name: Within each sequence of 1024 tokens, the 128 tokens of each index of ctx are two runs of consecutive positions of 64 each: blocks b and 15 - b of the sequence cut into 16 equal blocks, the earlier block first, where b (0 to 7) may differ for each index of ctx and each sequence; every position of the sequence appears once.
All inputs are finite; a program needn't handle non-finite values.
Results may differ from the reference program's by a relative error of at most 0.035.
Values may be sent and summed in bfloat16 or wider, within the bound.
No kernel may reach another device: no remote copies, remote signals or barrier semaphores. Data moves between devices by JAX's collectives and lax.ppermute only.
A program may use at most 256 MiB of HBM per device.

```python
import jax
import jax.numpy as jnp
from jax import lax

D = 1536
FF = 8960
H = 12
KV = 2
HD = 128
TOK_DEV = 128
SEQ = 1024
TOKENS = 4096
N_CTX = 8
N_FSDP = 4


def draw_positions(key, part):
    block_size = TOK_DEV // 2

    def sequence_positions(sequence):
        shuffled = jax.random.permutation(jax.random.fold_in(key, sequence), N_CTX)
        offsets = jnp.arange(block_size)[None, :]
        early_rows = shuffled[:, None] * block_size + offsets
        late_rows = (2 * N_CTX - 1 - shuffled)[:, None] * block_size + offsets
        return jnp.concatenate([early_rows, late_rows], axis=1).reshape(-1)
    return jax.vmap(sequence_positions)(jnp.arange(N_FSDP)).reshape(-1).astype(jnp.int32)


def block_levels(stream_key, extent, cuts, smallest, high):
    level, own = 1.0, jax.random.fold_in(stream_key, 6)
    for dim, parts in cuts:
        heights = jnp.exp(jax.random.uniform(jax.random.fold_in(own, dim), (parts,), jnp.float32, smallest / len(cuts), high / len(cuts)))
        level = level * jnp.repeat(heights, extent[dim] // parts).reshape([-1 if axis == dim else 1 for axis in range(len(extent))])
    return level


def noise(stream_key, dims, width, reach, cuts=(), held_as=jnp.bfloat16):
    values = width * jax.random.normal(stream_key, dims, jnp.float32)
    if cuts:
        values = values * block_levels(stream_key, dims, cuts, -0.22, 0.18)
    return jnp.clip(values, -reach, reach).astype(held_as)


def setup_inputs(seed: int = 0) -> dict:
    key_list = jax.random.split(jax.random.key(seed), 16)
    hidden = noise(key_list[0], (TOKENS, D), 1.0, 6.0, ((0, 32),))
    positions = draw_positions(jax.random.fold_in(key_list[15], 71), 0)
    first_gain = jnp.clip(1.0 + 0.18 * jax.random.normal(key_list[2], (D,), jnp.float32), 0.099609375, 1.8984375).astype(jnp.bfloat16)
    query_weight = noise(key_list[3], (D, H * HD), D ** -0.5, 0.15625, ((0, 32),))
    key_weight = noise(key_list[4], (D, KV * HD), D ** -0.5, 0.15625, ((0, 32),))
    value_weight = noise(key_list[5], (D, KV * HD), D ** -0.5, 0.15625, ((0, 32),))
    query_bias = noise(key_list[6], (H * HD,), 0.5, 3.0, ((0, 32),))
    key_bias = noise(key_list[7], (KV * HD,), 0.5, 3.0, ((0, 32),))
    value_bias = noise(key_list[8], (KV * HD,), 0.5, 3.0, ((0, 32),))
    output_weight = noise(key_list[9], (H * HD, D), (D // 16) ** -0.5, 0.625, ((0, 32),))
    second_gain = jnp.clip(1.0 + 0.18 * jax.random.normal(key_list[10], (D,), jnp.float32), 0.099609375, 1.8984375).astype(jnp.bfloat16)
    gate_weight = noise(key_list[11], (D, FF), D ** -0.5, 0.15625, ((1, 32),))
    up_weight = noise(key_list[12], (D, FF), D ** -0.5, 0.15625, ((1, 32),))
    down_weight = noise(key_list[13], (FF, D), FF ** -0.5, 0.0625, ((0, 32),))
    cotangent = noise(key_list[14], (TOKENS, D), 1.0, 6.0, ((0, 32),))
    return dict(hidden=hidden, positions=positions, first_gain=first_gain, query_weight=query_weight, key_weight=key_weight, value_weight=value_weight, query_bias=query_bias, key_bias=key_bias, value_bias=value_bias, output_weight=output_weight, second_gain=second_gain, gate_weight=gate_weight, up_weight=up_weight, down_weight=down_weight, cotangent=cotangent)


@jax.custom_vjp
def low(v):
    return lax.optimization_barrier(v.astype(jnp.bfloat16)).astype(jnp.float32)

@jax.custom_vjp
def low_back(v):
    return v

def low_keep(v):
    return (low(v), None)

def low_pass(kept, grad):
    return (grad,)

def back_keep(v):
    return (v, None)

def back_low(kept, grad):
    return (low(grad),)
low.defvjp(low_keep, low_pass)
low_back.defvjp(back_keep, back_low)
epsilon = 1e-06
rope_base = 1000000.0
neg_large = -1e+30
highest = lax.Precision.HIGHEST

def rms_norm(values, norm_gain):
    return values * lax.rsqrt(lax.optimization_barrier(jnp.mean(values * values, axis=-1, keepdims=True)) + epsilon) * norm_gain

def rotate(values, places):
    half_width = values.shape[-1] // 2
    frequency = rope_base ** (-2.0 * jnp.arange(half_width, dtype=jnp.float32) / values.shape[-1])
    angles = places.astype(jnp.float32)[:, None] * frequency[None, :]
    cosine = jnp.cos(angles)[:, None, :]
    sine_table = jnp.sin(angles)[:, None, :]
    leading = values[..., :half_width]
    trailing = values[..., half_width:]
    return jnp.concatenate([leading * cosine - trailing * sine_table, trailing * cosine + leading * sine_table], axis=-1)

def layer(inputs, places, first_gain, query_weight, key_weight, value_weight, query_bias, key_bias, value_bias, output_weight, second_gain, gate_weight, up_weight, down_weight):
    length = inputs.shape[0]
    group_size = H // KV
    normed = low(rms_norm(inputs, first_gain))
    query_lin = low_back(jnp.dot(normed, query_weight, precision=highest) + query_bias)
    key_lin = low_back(jnp.dot(normed, key_weight, precision=highest) + key_bias)
    value_all = low(low_back(jnp.dot(normed, value_weight, precision=highest) + value_bias)).reshape(length, KV, HD)
    queries = low(rotate(query_lin.reshape(length, H, HD), places)).reshape(length, KV, group_size, HD)
    keys_all = low(rotate(key_lin.reshape(length, KV, HD), places))
    block_rows = min(512, length)
    blocks = length // block_rows

    def attend(pieces):
        query_block, place_block = pieces
        scores = low_back(jnp.einsum('tgjd,sgd->gjts', query_block, keys_all, precision=highest) * HD ** (-0.5))
        allowed = places[None, None, None, :] <= place_block[None, None, :, None]
        scores = jnp.where(allowed, scores, neg_large)
        weights = low(jax.nn.softmax(scores, axis=-1))
        return jnp.einsum('gjts,sgd->tgjd', weights, value_all, precision=highest)
    mixture = lax.map(jax.checkpoint(attend), (queries.reshape(blocks, block_rows, KV, group_size, HD), places.reshape(blocks, block_rows)))
    mixture = low(low_back(mixture.reshape(length, H * HD)))
    attention = low_back(jnp.dot(mixture, output_weight, precision=highest))
    middle = inputs + attention
    normed_two = low(rms_norm(middle, second_gain))
    gate_lin = low_back(jnp.dot(normed_two, gate_weight, precision=highest))
    up_lin = low_back(jnp.dot(normed_two, up_weight, precision=highest))
    activated = low(low_back(jax.nn.silu(gate_lin) * up_lin))
    return middle + low_back(jnp.dot(activated, down_weight, precision=highest))

def reference(hidden, positions, first_gain, query_weight, key_weight, value_weight, query_bias, key_bias, value_bias, output_weight, second_gain, gate_weight, up_weight, down_weight, cotangent):
    floats = tuple((entry.astype(jnp.float32) for entry in (first_gain, query_weight, key_weight, value_weight, query_bias, key_bias, value_bias, output_weight, second_gain, gate_weight, up_weight, down_weight)))

    def whole(inputs, params):

        def per_sequence(pieces):
            return layer(pieces[0], pieces[1], *params)
        results = lax.map(per_sequence, (inputs.reshape(N_FSDP, SEQ, D), positions.reshape(N_FSDP, SEQ)))
        return results.reshape(TOKENS, D)
    result, pullback = jax.vjp(whole, hidden.astype(jnp.float32), floats)
    input_delta, param_deltas = pullback(cotangent.astype(jnp.float32))
    return (result.astype(jnp.bfloat16), input_delta, param_deltas[0], param_deltas[1], param_deltas[2], param_deltas[3], param_deltas[4], param_deltas[5], param_deltas[6], param_deltas[7], param_deltas[8], param_deltas[9], param_deltas[10], param_deltas[11])
```

```python
import jax
import jax.numpy as jnp
from jax import lax
from jax.sharding import Mesh
from jax.sharding import PartitionSpec as P

H = 12
KV = 2
HD = 128

epsilon = 1e-06
rope_base = 1000000.0
neg_large = -1e30

EVERY = ("grp", "core", "fsdp")
SEQ_AXES = ("grp", "core")
TP_AXES = ("fsdp", "core")


def rms_scale(values):
    return lax.rsqrt(jnp.mean(values * values, axis=-1, keepdims=True) + epsilon)


def rope_tables(places):
    half_width = HD // 2
    frequency = rope_base ** (-2.0 * jnp.arange(half_width, dtype=jnp.float32) / HD)
    angles = places.astype(jnp.float32)[:, None] * frequency[None, :]
    return jnp.cos(angles)[:, None, :], jnp.sin(angles)[:, None, :]


def rotate(values, cosine, sine):
    half_width = values.shape[-1] // 2
    leading = values[..., :half_width]
    trailing = values[..., half_width:]
    return jnp.concatenate(
        [leading * cosine - trailing * sine, trailing * cosine + leading * sine], axis=-1
    )


def matmul(left, right):
    return jnp.dot(left, right, preferred_element_type=jnp.float32)


def matmul_nt(left, right):
    return lax.dot_general(
        left, right, (((1,), (1,)), ((), ())), preferred_element_type=jnp.float32
    )


def inner(left, right):
    return lax.dot_general(
        left, right, (((0,), (0,)), ((), ())), preferred_element_type=jnp.float32
    )


def low(values):
    return values.astype(jnp.bfloat16)


def exchange(values, bit):
    count = lax.axis_size("grp")
    return lax.ppermute(values, "grp", [(i, i ^ bit) for i in range(count)])


def gather_group(block):
    count = lax.axis_size("grp")
    if count != 4:
        return lax.all_gather(block, "grp", axis=0, tiled=True)
    half = block.shape[1] // 2
    from_x = exchange(block, 1)
    from_y = exchange(block, 2)
    left = exchange(from_x[:, :half], 2)
    right = exchange(from_y[:, half:], 1)
    corner = jnp.concatenate([left, right], axis=1)
    return jnp.concatenate([block, from_x, from_y, corner], axis=0)


def scatter_group(parts):
    count = lax.axis_size("grp")
    if count != 4:
        return lax.psum_scatter(low(parts), "grp", scatter_dimension=0, tiled=True).astype(
            jnp.float32
        )
    rows = parts.shape[0] // 4
    half = parts.shape[1] // 2
    own, for_x, for_y, corner = (parts[i * rows : (i + 1) * rows] for i in range(4))
    corner = low(corner)
    from_x = exchange(corner[:, :half], 1).astype(jnp.float32)
    from_y = exchange(corner[:, half:], 2).astype(jnp.float32)
    for_y = jnp.concatenate([for_y[:, :half] + from_x, for_y[:, half:]], axis=1)
    for_x = jnp.concatenate([for_x[:, :half], for_x[:, half:] + from_y], axis=1)
    return (
        own
        + exchange(low(for_x), 1).astype(jnp.float32)
        + exchange(low(for_y), 2).astype(jnp.float32)
    )


def local(
    hidden,
    positions,
    first_gain,
    query_weight,
    key_weight,
    value_weight,
    query_bias,
    key_bias,
    value_bias,
    output_weight,
    second_gain,
    gate_weight,
    up_weight,
    down_weight,
    cotangent,
):
    rows = hidden.shape[0]
    width = hidden.shape[1]
    group_size = H // KV
    score_scale = HD ** (-0.5)
    ctx_here = lax.axis_index("grp") * lax.axis_size("core") + lax.axis_index("core")
    own_places = lax.dynamic_slice_in_dim(positions, ctx_here * rows, rows)
    q_width, k_width = H * HD, KV * HD

    projections = jnp.concatenate([query_weight, key_weight, value_weight], axis=1)
    weight_qkv = lax.all_gather(projections, EVERY, axis=0, tiled=True)
    small = jnp.concatenate([first_gain, second_gain, query_bias, key_bias, value_bias])
    small_all = lax.all_gather(small, EVERY, axis=0, tiled=False).astype(jnp.float32)
    own = width // small_all.shape[0]
    kv_own = k_width // small_all.shape[0]
    gain_one = small_all[:, :own].reshape(width)
    gain_two = small_all[:, own : 2 * own].reshape(width)
    bias_qkv = jnp.concatenate(
        [
            small_all[:, 2 * own : 3 * own].reshape(q_width),
            small_all[:, 3 * own : 3 * own + kv_own].reshape(k_width),
            small_all[:, 3 * own + kv_own :].reshape(k_width),
        ]
    )
    weight_output = lax.all_gather(output_weight, EVERY, axis=0, tiled=True)
    gate_rows = gather_group(gate_weight.T)
    up_rows = gather_group(up_weight.T)
    down_rows = gather_group(down_weight)
    cotangent_all = lax.all_gather(cotangent, TP_AXES, axis=0, tiled=True)

    inputs = hidden.astype(jnp.float32)
    unit_one = inputs * rms_scale(inputs)
    normed = low(unit_one * gain_one)
    lin = matmul(normed, weight_qkv) + bias_qkv
    cosine, sine = rope_tables(own_places)
    queries = low(rotate(lin[:, :q_width].reshape(rows, H, HD), cosine, sine)).reshape(
        rows, KV, group_size, HD
    )
    keys_local = low(
        rotate(lin[:, q_width : q_width + k_width].reshape(rows, KV, HD), cosine, sine)
    ).reshape(rows, k_width)
    values_local = low(lin[:, q_width + k_width :])
    kv_all = lax.all_gather(
        jnp.concatenate([keys_local, values_local], axis=1), SEQ_AXES, axis=0, tiled=True
    )
    length = kv_all.shape[0]
    keys = kv_all[:, :k_width].reshape(length, KV, HD)
    values = kv_all[:, k_width:].reshape(length, KV, HD)
    allowed = (positions[None, :] <= own_places[:, None])[None, None]

    scores = jnp.einsum("tgjd,sgd->gjts", queries, keys, preferred_element_type=jnp.float32)
    scores = jnp.where(allowed, scores * score_scale, neg_large)
    top = jnp.max(scores, axis=-1, keepdims=True)
    log_sum = top + jnp.log(jnp.sum(jnp.exp(scores - top), axis=-1, keepdims=True))
    probs = jnp.where(allowed, jnp.exp(scores - log_sum), 0.0)
    probs_low = low(probs)
    mixture = jnp.einsum("gjts,sgd->tgjd", probs_low, values, preferred_element_type=jnp.float32)
    mixed_low = low(mixture.reshape(rows, q_width))
    middle = inputs + matmul(mixed_low, weight_output)
    scale_two = rms_scale(middle)
    unit_two = middle * scale_two
    normed_two = low(unit_two * gain_two)

    normed_all = lax.all_gather(normed_two, TP_AXES, axis=0, tiled=True)
    gate = matmul_nt(normed_all, gate_rows)
    upward = matmul_nt(normed_all, up_rows)
    active_delta = low(matmul_nt(cotangent_all, down_rows)).astype(jnp.float32)
    sigmoid = 1.0 / (1.0 + jnp.exp(-gate))
    silu = gate * sigmoid
    active = low(silu * upward)
    gate_delta = low(active_delta * upward * (sigmoid * (1.0 + gate * (1.0 - sigmoid))))
    up_delta = low(active_delta * silu)
    normed_two_part = matmul(gate_delta, gate_rows) + matmul(up_delta, up_rows)
    normed_two_delta = lax.psum_scatter(
        low(normed_two_part), TP_AXES, scatter_dimension=0, tiled=True
    ).astype(jnp.float32)
    out_part = matmul(active, down_rows)
    out_sum = lax.psum_scatter(low(out_part), TP_AXES, scatter_dimension=0, tiled=True)
    layer_out = low(middle + out_sum.astype(jnp.float32))
    gate_grad = scatter_group(inner(gate_delta, normed_all)).T
    up_grad = scatter_group(inner(up_delta, normed_all)).T
    down_grad = scatter_group(inner(active, cotangent_all))

    second_gain_part = jnp.sum(normed_two_delta * unit_two, axis=0)
    scaled = normed_two_delta * gain_two
    middle_delta = cotangent.astype(jnp.float32) + scale_two * (
        scaled - unit_two * jnp.mean(scaled * unit_two, axis=-1, keepdims=True)
    )

    attention_low = low(middle_delta)
    output_grad = lax.psum_scatter(
        low(inner(mixed_low, attention_low)), EVERY, scatter_dimension=0, tiled=True
    ).astype(jnp.float32)
    mixed_delta = low(matmul_nt(attention_low, weight_output)).reshape(rows, KV, group_size, HD)
    row_dots = jnp.transpose(jnp.sum(mixed_delta.astype(jnp.float32) * mixture, axis=-1), (1, 2, 0))
    value_part = jnp.einsum(
        "gjts,tgjd->sgd", probs_low, mixed_delta, preferred_element_type=jnp.float32
    )
    prob_delta = jnp.einsum(
        "tgjd,sgd->gjts", mixed_delta, values, preferred_element_type=jnp.float32
    )
    score_delta = low(probs * (prob_delta - row_dots[..., None]))
    query_rot_delta = (
        jnp.einsum("gjts,sgd->tgjd", score_delta, keys, preferred_element_type=jnp.float32)
        * score_scale
    )
    key_part = (
        jnp.einsum("gjts,tgjd->sgd", score_delta, queries, preferred_element_type=jnp.float32)
        * score_scale
    )
    kv_part = jnp.concatenate(
        [key_part.reshape(length, k_width), value_part.reshape(length, k_width)], axis=1
    )
    kv_delta = lax.psum_scatter(low(kv_part), SEQ_AXES, scatter_dimension=0, tiled=True)
    key_lin_delta = low(
        rotate(
            kv_delta[:, :k_width].astype(jnp.float32).reshape(rows, KV, HD), cosine, -sine
        ).reshape(rows, k_width)
    )
    query_lin_delta = low(
        rotate(query_rot_delta.reshape(rows, H, HD), cosine, -sine).reshape(rows, q_width)
    )
    lin_delta = jnp.concatenate([query_lin_delta, key_lin_delta, kv_delta[:, k_width:]], axis=1)
    qkv_grad = lax.psum_scatter(
        low(inner(normed, lin_delta)), EVERY, scatter_dimension=0, tiled=True
    ).astype(jnp.float32)
    normed_delta = matmul_nt(lin_delta, weight_qkv)
    scale_one = rms_scale(inputs)
    first_gain_part = jnp.sum(normed_delta * unit_one, axis=0)
    scaled_one = normed_delta * gain_one
    input_delta = middle_delta + scale_one * (
        scaled_one - unit_one * jnp.mean(scaled_one * unit_one, axis=-1, keepdims=True)
    )

    bias_part = jnp.sum(lin_delta.astype(jnp.float32), axis=0)
    devices = small_all.shape[0]
    small_part = jnp.concatenate(
        [
            first_gain_part.reshape(devices, own),
            second_gain_part.reshape(devices, own),
            bias_part[:q_width].reshape(devices, own),
            bias_part[q_width : q_width + k_width].reshape(devices, kv_own),
            bias_part[q_width + k_width :].reshape(devices, kv_own),
        ],
        axis=1,
    )
    small_grad = lax.psum_scatter(small_part.reshape(-1), EVERY, scatter_dimension=0, tiled=True)
    return (
        layer_out,
        input_delta,
        small_grad[:own],
        qkv_grad[:, :q_width],
        qkv_grad[:, q_width : q_width + k_width],
        qkv_grad[:, q_width + k_width :],
        small_grad[2 * own : 3 * own],
        small_grad[3 * own : 3 * own + kv_own],
        small_grad[3 * own + kv_own :],
        output_grad,
        small_grad[own : 2 * own],
        gate_grad,
        up_grad,
        down_grad,
    )


def solution(mesh):
    cores = 2
    ctx, fsdp = mesh.shape["ctx"], mesh.shape["fsdp"]
    split = Mesh(mesh.devices.reshape(ctx // cores, cores, fsdp), EVERY)
    tokens = P(("fsdp", "grp", "core"), None)
    in_specs = (
        tokens,
        P("fsdp"),
        P(EVERY),
        P(EVERY, None),
        P(EVERY, None),
        P(EVERY, None),
        P(EVERY),
        P(EVERY),
        P(EVERY),
        P(EVERY, None),
        P(EVERY),
        P(None, EVERY),
        P(None, EVERY),
        P(EVERY, None),
        tokens,
    )
    out_specs = (
        tokens,
        tokens,
        P(EVERY),
        P(EVERY, None),
        P(EVERY, None),
        P(EVERY, None),
        P(EVERY),
        P(EVERY),
        P(EVERY),
        P(EVERY, None),
        P(EVERY),
        P(None, EVERY),
        P(None, EVERY),
        P(EVERY, None),
    )
    return jax.shard_map(local, mesh=split, in_specs=in_specs, out_specs=out_specs, check_vma=False)
```

```python
import jax
import jax.numpy as jnp
from jax import lax
from jax.sharding import Mesh
from jax.sharding import PartitionSpec as P

H = 12
KV = 2
HD = 128

epsilon = 1e-06
rope_base = 1000000.0
neg_large = -1e30

EVERY = ("grp", "core", "fsdp")
SEQ_AXES = ("grp", "core")
TP_AXES = ("fsdp", "core")


def rms_scale(values):
    return lax.rsqrt(jnp.mean(values * values, axis=-1, keepdims=True) + epsilon)


def rope_tables(places):
    half_width = HD // 2
    frequency = rope_base ** (-2.0 * jnp.arange(half_width, dtype=jnp.float32) / HD)
    angles = places.astype(jnp.float32)[:, None] * frequency[None, :]
    return jnp.cos(angles)[:, None, :], jnp.sin(angles)[:, None, :]


def rotate(values, cosine, sine):
    half_width = values.shape[-1] // 2
    leading = values[..., :half_width]
    trailing = values[..., half_width:]
    return jnp.concatenate(
        [leading * cosine - trailing * sine, trailing * cosine + leading * sine], axis=-1
    )


def matmul(left, right):
    return jnp.dot(left, right, preferred_element_type=jnp.float32)


def matmul_nt(left, right):
    return lax.dot_general(
        left, right, (((1,), (1,)), ((), ())), preferred_element_type=jnp.float32
    )


def inner(left, right):
    return lax.dot_general(
        left, right, (((0,), (0,)), ((), ())), preferred_element_type=jnp.float32
    )


def low(values):
    return values.astype(jnp.bfloat16)


def after(values, *others):
    return lax.optimization_barrier((values, others))[0]


def exchange(values, bit):
    count = lax.axis_size("grp")
    return lax.ppermute(values, "grp", [(i, i ^ bit) for i in range(count)])


def other_core(values):
    return lax.ppermute(values, "core", [(0, 1), (1, 0)])


def gather_group(block):
    count = lax.axis_size("grp")
    if count != 4:
        bit = 1
        while bit < count:
            block = jnp.concatenate([block, exchange(block, bit)], axis=0)
            bit *= 2
        return block
    half = block.shape[1] // 2
    from_x = exchange(block, 1)
    from_y = exchange(block, 2)
    left = exchange(from_x[:, :half], 2)
    right = exchange(from_y[:, half:], 1)
    corner = jnp.concatenate([left, right], axis=1)
    return jnp.concatenate([block, from_x, from_y, corner], axis=0)


def scatter_group(parts, *before):
    count = lax.axis_size("grp")
    rows = parts.shape[0] // count
    if count != 4:
        bit = count // 2
        parts = parts.astype(jnp.float32)
        while bit:
            keep, give = parts[: bit * rows], parts[bit * rows :]
            parts = keep + exchange(low(give), bit).astype(jnp.float32)
            bit //= 2
        return after(parts, *before)
    half = parts.shape[1] // 2
    own, for_x, for_y, corner = (
        parts[i * rows : (i + 1) * rows].astype(jnp.float32) for i in range(4)
    )
    corner = low(corner)
    from_x = exchange(corner[:, :half], 1).astype(jnp.float32)
    from_y = exchange(corner[:, half:], 2).astype(jnp.float32)
    for_y = jnp.concatenate([for_y[:, :half] + from_x, for_y[:, half:]], axis=1)
    for_x = jnp.concatenate([for_x[:, :half], for_x[:, half:] + from_y], axis=1)
    from_x = after(exchange(low(for_x), 1), *before).astype(jnp.float32)
    from_y = after(exchange(low(for_y), 2), *before).astype(jnp.float32)
    return own + from_x + from_y


def gather_sequence(block):
    mine = gather_group(block)
    return jnp.concatenate([mine, other_core(mine)], axis=0)


def scatter_sequence(parts):
    half = parts.shape[0] // 2
    return scatter_group(
        parts[:half].astype(jnp.float32) + other_core(low(parts[half:])).astype(jnp.float32)
    )


def sequence_order(values):
    count = lax.axis_size("grp")
    ctx = lax.axis_index("grp") * 2 + lax.axis_index("core")
    rows = values.shape[0] // (2 * count)
    return jnp.concatenate(
        [
            lax.dynamic_slice_in_dim(values, (ctx ^ (2 * i + j)) * rows, rows)
            for j in range(2)
            for i in range(count)
        ]
    )


def swap_groups(values):
    count = lax.axis_size("grp")
    if count == 1:
        return values
    width = values.shape[1] // count
    grp = lax.axis_index("grp")
    return jnp.concatenate(
        [lax.dynamic_slice_in_dim(values, (grp ^ i) * width, width, 1) for i in range(count)],
        axis=1,
    )


def swap_halves(values):
    half = values.shape[1] // 2
    first = lax.axis_index("core") == 0
    left, right = values[:, :half], values[:, half:]
    return jnp.where(first, left, right), jnp.where(first, right, left)


def gather_weight(block, *before):
    rows = after(lax.all_gather(block, ("core", "fsdp"), axis=0, tiled=True), *before)
    half = rows.shape[1] // 2
    mine = gather_group(lax.dynamic_slice_in_dim(rows, lax.axis_index("core") * half, half, 1))
    return mine, other_core(mine)


def sum_everywhere(values):
    for axis in ("core", "grp", "fsdp"):
        count = lax.axis_size(axis)
        bit = 1
        while bit < count:
            values = values + lax.ppermute(values, axis, [(i, i ^ bit) for i in range(count)])
            bit *= 2
    return values


def local(
    hidden,
    positions,
    first_gain,
    query_weight,
    key_weight,
    value_weight,
    query_bias,
    key_bias,
    value_bias,
    output_weight,
    second_gain,
    gate_weight,
    up_weight,
    down_weight,
    cotangent,
):
    rows = hidden.shape[0]
    width = hidden.shape[1]
    group_size = H // KV
    score_scale = HD ** (-0.5)
    ctx_here = lax.axis_index("grp") * lax.axis_size("core") + lax.axis_index("core")
    own_places = lax.dynamic_slice_in_dim(positions, ctx_here * rows, rows)
    q_width, k_width = H * HD, KV * HD

    projections = jnp.concatenate([query_weight, key_weight, value_weight], axis=1)
    small = jnp.concatenate([first_gain, second_gain, query_bias, key_bias, value_bias])
    devices = lax.axis_size(EVERY)
    device_here = lax.axis_index(EVERY)
    small_all = sum_everywhere(
        lax.dynamic_update_slice_in_dim(
            jnp.zeros((devices, small.shape[0]), jnp.float32),
            small.astype(jnp.float32)[None],
            device_here,
            0,
        )
    )
    down_rows = gather_group(down_weight)
    qkv_mine, qkv_other = gather_weight(projections, small_all, down_rows)
    own = width // devices
    kv_own = k_width // devices
    gain_one = small_all[:, :own].reshape(width)
    gain_two = small_all[:, own : 2 * own].reshape(width)
    bias_qkv = jnp.concatenate(
        [
            small_all[:, 2 * own : 3 * own].reshape(q_width),
            small_all[:, 3 * own : 3 * own + kv_own].reshape(k_width),
            small_all[:, 3 * own + kv_own :].reshape(k_width),
        ]
    )
    output_mine, output_other = gather_weight(output_weight)
    gate_rows = gather_group(gate_weight.T)
    up_rows = gather_group(up_weight.T)
    cotangent_all = lax.all_gather(cotangent, TP_AXES, axis=0, tiled=True)

    inputs = hidden.astype(jnp.float32)
    unit_one = inputs * rms_scale(inputs)
    normed = low(unit_one * gain_one)
    normed_swapped = swap_groups(normed)
    lin_halves = jnp.concatenate(
        [matmul(normed_swapped, qkv_mine), matmul(normed_swapped, qkv_other)], axis=1
    )
    lin = jnp.concatenate(swap_halves(lin_halves), axis=1) + bias_qkv
    cosine, sine = rope_tables(own_places)
    queries = low(rotate(lin[:, :q_width].reshape(rows, H, HD), cosine, sine)).reshape(
        rows, KV, group_size, HD
    )
    keys_local = low(
        rotate(lin[:, q_width : q_width + k_width].reshape(rows, KV, HD), cosine, sine)
    ).reshape(rows, k_width)
    values_local = low(lin[:, q_width + k_width :])
    kv_all = gather_sequence(jnp.concatenate([keys_local, values_local], axis=1))
    length = kv_all.shape[0]
    places = positions.reshape(-1, rows)
    steps = jnp.arange(places.shape[0], dtype=jnp.int32)
    from_ctx = ctx_here ^ jnp.concatenate([steps[0::2], steps[1::2]])
    matches = from_ctx[:, None] == jnp.arange(places.shape[0], dtype=jnp.int32)[None, :]
    key_places = jnp.sum(jnp.where(matches[:, :, None], places[None], 0), axis=1).reshape(length)
    keys = kv_all[:, :k_width].reshape(length, KV, HD)
    values = kv_all[:, k_width:].reshape(length, KV, HD)
    allowed = (key_places[None, :] <= own_places[:, None])[None, None]

    scores = jnp.einsum("tgjd,sgd->gjts", queries, keys, preferred_element_type=jnp.float32)
    scores = jnp.where(allowed, scores * score_scale, neg_large)
    top = jnp.max(scores, axis=-1, keepdims=True)
    log_sum = top + jnp.log(jnp.sum(jnp.exp(scores - top), axis=-1, keepdims=True))
    probs = jnp.where(allowed, jnp.exp(scores - log_sum), 0.0)
    probs_low = low(probs)
    mixture = jnp.einsum("gjts,sgd->tgjd", probs_low, values, preferred_element_type=jnp.float32)
    mixed_low = low(mixture.reshape(rows, q_width))
    mixed_swapped = swap_groups(mixed_low)
    attention_halves = jnp.concatenate(
        [matmul(mixed_swapped, output_mine), matmul(mixed_swapped, output_other)], axis=1
    )
    middle = inputs + jnp.concatenate(swap_halves(attention_halves), axis=1)
    scale_two = rms_scale(middle)
    unit_two = middle * scale_two
    normed_two = low(unit_two * gain_two)

    normed_all = lax.all_gather(normed_two, TP_AXES, axis=0, tiled=True)
    gate = matmul_nt(normed_all, gate_rows)
    upward = matmul_nt(normed_all, up_rows)
    active_delta = low(matmul_nt(cotangent_all, down_rows)).astype(jnp.float32)
    sigmoid = 1.0 / (1.0 + jnp.exp(-gate))
    silu = gate * sigmoid
    active = low(silu * upward)
    gate_delta = low(active_delta * upward * (sigmoid * (1.0 + gate * (1.0 - sigmoid))))
    up_delta = low(active_delta * silu)
    normed_two_part = matmul(gate_delta, gate_rows) + matmul(up_delta, up_rows)
    normed_two_delta = lax.psum_scatter(
        low(normed_two_part), TP_AXES, scatter_dimension=0, tiled=True
    ).astype(jnp.float32)
    out_part = matmul(active, down_rows)
    out_sum = lax.psum_scatter(low(out_part), TP_AXES, scatter_dimension=0, tiled=True)
    gate_grad_sums = inner(gate_delta, normed_all)
    up_grad_sums = inner(up_delta, normed_all)
    down_grad_sums = inner(active, cotangent_all)

    second_gain_part = jnp.sum(normed_two_delta * unit_two, axis=0)
    scaled = normed_two_delta * gain_two
    middle_delta = cotangent.astype(jnp.float32) + scale_two * (
        scaled - unit_two * jnp.mean(scaled * unit_two, axis=-1, keepdims=True)
    )

    attention_low = low(middle_delta)
    low_mine, low_other = swap_halves(attention_low)
    mixed_delta = low(
        swap_groups(matmul_nt(low_mine, output_mine) + matmul_nt(low_other, output_other))
    ).reshape(rows, KV, group_size, HD)
    row_dots = jnp.transpose(jnp.sum(mixed_delta.astype(jnp.float32) * mixture, axis=-1), (1, 2, 0))
    value_part = jnp.einsum(
        "gjts,tgjd->sgd", probs_low, mixed_delta, preferred_element_type=jnp.float32
    )
    prob_delta = jnp.einsum(
        "tgjd,sgd->gjts", mixed_delta, values, preferred_element_type=jnp.float32
    )
    score_delta = low(probs * (prob_delta - row_dots[..., None]))
    query_rot_delta = (
        jnp.einsum("gjts,sgd->tgjd", score_delta, keys, preferred_element_type=jnp.float32)
        * score_scale
    )
    key_part = (
        jnp.einsum("gjts,tgjd->sgd", score_delta, queries, preferred_element_type=jnp.float32)
        * score_scale
    )
    kv_part = jnp.concatenate(
        [key_part.reshape(length, k_width), value_part.reshape(length, k_width)], axis=1
    )
    kv_delta = low(scatter_sequence(kv_part))
    key_lin_delta = low(
        rotate(
            kv_delta[:, :k_width].astype(jnp.float32).reshape(rows, KV, HD), cosine, -sine
        ).reshape(rows, k_width)
    )
    query_lin_delta = low(
        rotate(query_rot_delta.reshape(rows, H, HD), cosine, -sine).reshape(rows, q_width)
    )
    lin_delta = jnp.concatenate([query_lin_delta, key_lin_delta, kv_delta[:, k_width:]], axis=1)
    delta_mine, delta_other = swap_halves(lin_delta)
    normed_delta = swap_groups(
        matmul_nt(delta_mine, qkv_mine) + matmul_nt(delta_other, qkv_other)
    )
    scale_one = rms_scale(inputs)
    scaled_one = normed_delta * gain_one
    input_delta = middle_delta + scale_one * (
        scaled_one - unit_one * jnp.mean(scaled_one * unit_one, axis=-1, keepdims=True)
    )

    def columns(values):
        return sequence_order(
            lax.all_to_all(values, SEQ_AXES, split_axis=1, concat_axis=0, tiled=True)
        )

    output_grad = lax.psum_scatter(
        low(inner(columns(mixed_low), gather_sequence(attention_low))),
        "fsdp",
        scatter_dimension=0,
        tiled=True,
    ).astype(jnp.float32)
    qkv_grad = lax.psum_scatter(
        low(inner(columns(normed), gather_sequence(lin_delta))),
        "fsdp",
        scatter_dimension=0,
        tiled=True,
    ).astype(jnp.float32)
    first_gain_grad = jnp.sum(
        qkv_grad * projections.astype(jnp.float32), axis=1
    ) / first_gain.astype(jnp.float32)

    gate_grad = scatter_group(gate_grad_sums, lin_delta).T
    up_grad = scatter_group(up_grad_sums, lin_delta).T
    down_grad = scatter_group(down_grad_sums, lin_delta)
    layer_out = low(middle + after(out_sum, lin_delta).astype(jnp.float32))

    bias_part = jnp.sum(lin_delta.astype(jnp.float32), axis=0)
    small_part = jnp.concatenate(
        [
            second_gain_part.reshape(devices, own),
            bias_part[:q_width].reshape(devices, own),
            bias_part[q_width : q_width + k_width].reshape(devices, kv_own),
            bias_part[q_width + k_width :].reshape(devices, kv_own),
        ],
        axis=1,
    )
    small_grad = lax.dynamic_slice_in_dim(sum_everywhere(small_part), device_here, 1, 0)[0]
    return (
        layer_out,
        input_delta,
        first_gain_grad,
        qkv_grad[:, :q_width],
        qkv_grad[:, q_width : q_width + k_width],
        qkv_grad[:, q_width + k_width :],
        small_grad[own : 2 * own],
        small_grad[2 * own : 2 * own + kv_own],
        small_grad[2 * own + kv_own :],
        output_grad,
        small_grad[:own],
        gate_grad,
        up_grad,
        down_grad,
    )


def solution(mesh):
    cores = 2
    ctx, fsdp = mesh.shape["ctx"], mesh.shape["fsdp"]
    split = Mesh(mesh.devices.reshape(ctx // cores, cores, fsdp), EVERY)
    tokens = P(("fsdp", "grp", "core"), None)
    in_specs = (
        tokens,
        P("fsdp"),
        P(EVERY),
        P(EVERY, None),
        P(EVERY, None),
        P(EVERY, None),
        P(EVERY),
        P(EVERY),
        P(EVERY),
        P(EVERY, None),
        P(EVERY),
        P(None, EVERY),
        P(None, EVERY),
        P(EVERY, None),
        tokens,
    )
    out_specs = (
        tokens,
        tokens,
        P(EVERY),
        P(EVERY, None),
        P(EVERY, None),
        P(EVERY, None),
        P(EVERY),
        P(EVERY),
        P(EVERY),
        P(EVERY, None),
        P(EVERY),
        P(None, EVERY),
        P(None, EVERY),
        P(EVERY, None),
    )
    return jax.shard_map(local, mesh=split, in_specs=in_specs, out_specs=out_specs, check_vma=False)
```

```python
import jax
import jax.numpy as jnp
from jax import lax
from jax.experimental import pallas as pl
from jax.experimental.pallas import tpu as pltpu
from jax.sharding import Mesh
from jax.sharding import PartitionSpec as P

H = 12
KV = 2
HD = 128

epsilon = 1e-06
rope_base = 1000000.0
neg_large = -1e30

bf16 = jnp.bfloat16
f32 = jnp.float32
VMEM_BYTES = 56 * 2**20

EVERY = ("grp", "core", "fsdp")
SEQ_AXES = ("grp", "core")
TP_AXES = ("fsdp", "core")


def rms_scale(values):
    return lax.rsqrt(jnp.mean(values * values, axis=-1, keepdims=True) + epsilon)


def rope_tables(places):
    half_width = HD // 2
    frequency = rope_base ** (-2.0 * jnp.arange(half_width, dtype=jnp.float32) / HD)
    angles = places.astype(jnp.float32)[:, None] * frequency[None, :]
    cosine, sine = jnp.cos(angles), jnp.sin(angles)
    return jnp.concatenate([cosine, cosine], axis=1), jnp.concatenate([-sine, sine], axis=1)


def matmul(left, right):
    return jnp.dot(left, right, preferred_element_type=jnp.float32)


def matmul_nt(left, right):
    return lax.dot_general(
        left, right, (((1,), (1,)), ((), ())), preferred_element_type=jnp.float32
    )


def inner(left, right):
    return lax.dot_general(
        left, right, (((0,), (0,)), ((), ())), preferred_element_type=jnp.float32
    )


def low(values):
    return values.astype(jnp.bfloat16)


def after(values, *others):
    return lax.optimization_barrier((values, others))[0]


def exchange(values, bit):
    count = lax.axis_size("grp")
    return lax.ppermute(values, "grp", [(i, i ^ bit) for i in range(count)])


def other_core(values):
    return lax.ppermute(values, "core", [(0, 1), (1, 0)])


def gather_group(block):
    count = lax.axis_size("grp")
    if count != 4:
        bit = 1
        while bit < count:
            block = jnp.concatenate([block, exchange(block, bit)], axis=0)
            bit *= 2
        return block
    half = block.shape[1] // 2
    from_x = exchange(block, 1)
    from_y = exchange(block, 2)
    left = exchange(from_x[:, :half], 2)
    right = exchange(from_y[:, half:], 1)
    corner = jnp.concatenate([left, right], axis=1)
    return jnp.concatenate([block, from_x, from_y, corner], axis=0)


def gather_near(block):
    return exchange(block, 1), exchange(block, 2)


def gather_far(block, near):
    from_x, from_y = near
    half = block.shape[1] // 2
    left = exchange(from_x[:, :half], 2)
    right = exchange(from_y[:, half:], 1)
    return block, from_x, from_y, left, right


def join(pieces):
    rows, width = pieces[0].shape
    spare = jnp.zeros((-rows % 16, width), bf16)
    corner = jnp.concatenate(pieces[3:], axis=1)
    slots = []
    for piece in (*pieces[:3], corner):
        slots += [piece, spare]
    return jnp.concatenate(slots, axis=0)


def scatter_group(parts, rows, *before):
    count = lax.axis_size("grp")
    slot = parts.shape[0] // count
    if count != 4:
        bit = count // 2
        parts = parts.astype(jnp.float32)
        while bit:
            keep, give = parts[: bit * rows], parts[bit * rows :]
            parts = keep + exchange(low(give), bit).astype(jnp.float32)
            bit //= 2
        return after(parts, *before)
    half = parts.shape[1] // 2
    own, for_x, for_y, corner = (
        parts[i * slot : i * slot + rows].astype(jnp.float32) for i in range(4)
    )
    corner = low(corner)
    from_x = exchange(corner[:, :half], 1).astype(jnp.float32)
    from_y = exchange(corner[:, half:], 2).astype(jnp.float32)
    for_y = jnp.concatenate([for_y[:, :half] + from_x, for_y[:, half:]], axis=1)
    for_x = jnp.concatenate([for_x[:, :half], for_x[:, half:] + from_y], axis=1)
    from_x = exchange(after(low(for_x), *before), 1).astype(jnp.float32)
    from_y = exchange(after(low(for_y), *before), 2).astype(jnp.float32)
    return own + from_x + from_y


def gather_small(block):
    count = lax.axis_size("grp")
    mine = [block] + [exchange(block, step) for step in range(1, count)]
    return mine + [other_core(piece) for piece in mine]


def sequence_order(values):
    count = lax.axis_size("grp")
    ctx = lax.axis_index("grp") * 2 + lax.axis_index("core")
    rows = values.shape[0] // (2 * count)
    return jnp.concatenate(
        [
            lax.dynamic_slice_in_dim(values, (ctx ^ (2 * i + j)) * rows, rows)
            for j in range(2)
            for i in range(count)
        ]
    )


def plane_spots(pieces):
    count = lax.axis_size("grp")
    if len(pieces) > 2 * count:
        return (0, 0), (1, 0), (2, 0), (3, 0), (3, pieces[3].shape[1])
    return tuple((i, 0) for i in range(count))


def gather_plane(block):
    count = lax.axis_size("grp")
    if count == 4:
        part = block.shape[1] // 2
        from_x, from_y = exchange(block, 1), exchange(block, 2)
        left = exchange(from_x[:, :part], 2)
        right = exchange(from_y[:, part:], 1)
        mine = [block, from_x, from_y, left, right]
    else:
        mine = [block] + [exchange(block, i) for i in range(1, count)]
    return mine + [other_core(piece) for piece in mine]


def gather_rows(block, *before):
    return lax.all_gather(after(block, *before), ("core", "fsdp"), axis=0, tiled=True)


def gather_weight(rows):
    count = lax.axis_size("grp")
    height, half = rows.shape[0], rows.shape[1] // 2
    own = lax.dynamic_slice_in_dim(rows, lax.axis_index("core") * half, half, 1)
    if count == 4:
        part = half // 2
        from_x = exchange(own, 1)
        from_y = exchange(own, 2)
        left = exchange(from_x[:, :part], 2)
        right = exchange(from_y[:, part:], 1)
        spots = ((1, 0), (2, 0), (3, 0), (3, part))
        mine = (from_x, from_y, left, right)
    else:
        blocks = gather_group(own)
        spots = tuple((i, 0) for i in range(1, count))
        mine = tuple(blocks[i * height : (i + 1) * height] for i in range(1, count))
    return spots, rows, mine, tuple(other_core(piece) for piece in mine)


def assemble(spots, own_ref, mine_refs, other_refs, full_ref, sems):
    grp, core = lax.axis_index("grp"), lax.axis_index("core")
    height, half = own_ref.shape[0], full_ref.shape[1] // 2

    def rows_of(step):
        return pl.ds(pl.multiple_of((grp ^ step) * height, height), height)

    copies = [pltpu.make_async_copy(own_ref, full_ref.at[rows_of(0), :], sems.at[0])]
    for place, (step, offset) in enumerate(spots):
        for side, refs in ((core, mine_refs), (1 - core, other_refs)):
            width = refs[place].shape[1]
            start = pl.multiple_of(side * half + offset, 128)
            copies.append(
                pltpu.make_async_copy(
                    refs[place],
                    full_ref.at[rows_of(step), pl.ds(start, width)],
                    sems.at[len(copies)],
                )
            )
    for copy in copies:
        copy.start()
    return copies


def call(kernel, outs, ins, anys=(), scratch=()):
    whole = pl.BlockSpec(memory_space=pltpu.VMEM)
    left = pl.BlockSpec(memory_space=pl.ANY)
    return pl.pallas_call(
        kernel,
        out_shape=[jax.ShapeDtypeStruct(shape, dtype) for shape, dtype in outs],
        in_specs=[whole] * len(ins) + [left] * len(anys),
        out_specs=[whole] * len(outs),
        scratch_shapes=list(scratch),
        compiler_params=pltpu.CompilerParams(vmem_limit_bytes=VMEM_BYTES),
    )(*ins, *anys)


def weight_scratch(gathered, shape):
    spots, own, mine, other = gathered
    return [
        pltpu.VMEM(shape, bf16),
        pltpu.SemaphoreType.DMA((1 + 2 * len(mine),)),
    ]


def weight_args(gathered):
    spots, own, mine, other = gathered
    return [own, *mine, *other]


def weight_refs(gathered, refs):
    count = len(gathered[2])
    return gathered[0], refs[0], refs[1 : 1 + count], refs[1 + count : 1 + 2 * count]


def rope(values, cosine, sine):
    return values * cosine + pltpu.roll(values, HD // 2, 1) * sine


def project_kernel(gathered, refs):
    hidden, gain, bias, cosine, sine = refs[:5]
    count = 1 + 2 * len(gathered[2])
    pieces = refs[5 : 5 + count]
    normed, queries, pairs, weight, sems = refs[5 + count :]
    copies = assemble(*weight_refs(gathered, pieces), weight, sems)
    inputs = hidden[...].astype(f32)
    normed[...] = low(inputs * rms_scale(inputs) * gain[...])
    for copy in copies:
        copy.wait()
    rows = hidden.shape[0]
    half = weight.shape[1] // 2
    heads_half = half // HD
    for side in range(2):
        lin = (
            matmul(normed[...], weight[:, side * half : (side + 1) * half])
            + bias[:, side * half : (side + 1) * half]
        )
        for spot in range(heads_half):
            head = side * heads_half + spot
            part = lin[:, spot * HD : (spot + 1) * HD]
            if head < H + KV:
                part = rope(part, cosine[...], sine[...])
            if head < H:
                queries[head * rows : (head + 1) * rows, :] = low(part)
            else:
                pairs[:, (head - H) * HD : (head - H + 1) * HD] = low(part)


def fetch_pairs(refs, full_ref, sems):
    rows = refs[0].shape[0]
    copies = [
        pltpu.make_async_copy(ref, full_ref.at[pl.ds(i * rows, rows), :], sems.at[i])
        for i, ref in enumerate(refs)
    ]
    for copy in copies:
        copy.start()
    return copies


def attend_kernel(blocks, refs):
    queries, key_places, own_places = refs[:3]
    pair_refs = refs[3 : 3 + blocks]
    mixed, log_sums, pairs, pair_sems = refs[3 + blocks :]
    for copy in fetch_pairs(pair_refs, pairs, pair_sems):
        copy.wait()
    rows = own_places.shape[0]
    allowed = key_places[...] <= own_places[...]
    scale = HD ** (-0.5)
    for head in range(H):
        group = head // (H // KV)
        keys = pairs[:, group * HD : (group + 1) * HD]
        values = pairs[:, (KV + group) * HD : (KV + group + 1) * HD]
        span = slice(head * rows, (head + 1) * rows)
        scores = jnp.where(allowed, matmul_nt(queries[span, :], keys) * scale, neg_large)
        top = jnp.max(scores, axis=1, keepdims=True)
        terms = jnp.exp(scores - top)
        total = jnp.sum(terms, axis=1, keepdims=True)
        log_sums[span, :] = top + jnp.log(total)
        probs = low(terms * (1.0 / total))
        mixed[:, head * HD : (head + 1) * HD] = low(matmul(probs, values))


def output_kernel(gathered, refs):
    mixed, hidden, gain = refs[:3]
    count = 1 + 2 * len(gathered[2])
    pieces = refs[3 : 3 + count]
    middle, normed_two, weight, sems = refs[3 + count :]
    for copy in assemble(*weight_refs(gathered, pieces), weight, sems):
        copy.wait()
    result = hidden[...].astype(f32) + matmul(mixed[...], weight[...])
    middle[...] = result
    normed_two[...] = low(result * rms_scale(result) * gain[...])


def norm_back(delta, values, gain):
    scale = rms_scale(values)
    unit = values * scale
    scaled = delta * gain
    return scale * (scaled - unit * jnp.mean(scaled * unit, axis=-1, keepdims=True)), unit


def middle_kernel(gathered, refs):
    normed_delta, middle, cotangent, gain = refs[:4]
    count = 1 + 2 * len(gathered[2])
    pieces = refs[4 : 4 + count]
    middle_delta, attention_low, mixed_delta, gain_part, weight, sems = refs[4 + count :]
    copies = assemble(*weight_refs(gathered, pieces), weight, sems)
    delta = normed_delta[...].astype(f32)
    term, unit = norm_back(delta, middle[...], gain[...])
    gain_part[...] = jnp.sum(delta * unit, axis=0, keepdims=True)
    result = cotangent[...].astype(f32) + term
    middle_delta[...] = result
    attention_low[...] = low(result)
    for copy in copies:
        copy.wait()
    rows = middle.shape[0]
    mixed = matmul_nt(low(result), weight[...])
    for head in range(H):
        mixed_delta[head * rows : (head + 1) * rows, :] = low(mixed[:, head * HD : (head + 1) * HD])


def attend_back_kernel(blocks, refs):
    queries, mixed_delta, log_sums, key_places, own_places, cosine, sine = refs[:7]
    pair_refs = refs[7 : 7 + blocks]
    query_delta, bias_part, pair_mine, pair_other, pairs, pair_sems = refs[7 + blocks :]
    for copy in fetch_pairs(pair_refs, pairs, pair_sems):
        copy.wait()
    rows = own_places.shape[0]
    half = pair_mine.shape[0]
    allowed = key_places[...] <= own_places[...]
    scale = HD ** (-0.5)
    group_size = H // KV
    for group in range(KV):
        key_span = slice(group * HD, (group + 1) * HD)
        value_span = slice((KV + group) * HD, (KV + group + 1) * HD)
        keys, values = pairs[:, key_span], pairs[:, value_span]
        key_sum = value_sum = None
        for head in range(group * group_size, (group + 1) * group_size):
            span = slice(head * rows, (head + 1) * rows)
            query = queries[span, :]
            mixed = mixed_delta[span, :]
            scores = matmul_nt(query, keys) * scale
            probs = jnp.where(allowed, jnp.exp(scores - log_sums[span, :]), 0.0)
            prob_delta = matmul_nt(mixed, values)
            dots = jnp.sum(probs * prob_delta, axis=1, keepdims=True)
            score_delta = low(probs * (prob_delta - dots))
            turned = low(rope(matmul(score_delta, keys) * scale, cosine[...], sine[...]))
            query_delta[:, head * HD : (head + 1) * HD] = turned
            bias_part[:, head * HD : (head + 1) * HD] = jnp.sum(
                turned.astype(f32), axis=0, keepdims=True
            )
            key_part = inner(score_delta, query)
            value_part = inner(low(probs), mixed)
            key_sum = key_part if key_sum is None else key_sum + key_part
            value_sum = value_part if value_sum is None else value_sum + value_part
        key_sum = key_sum * scale
        pair_mine[:, key_span] = key_sum[:half]
        pair_mine[:, value_span] = value_sum[:half]
        pair_other[:, key_span] = low(key_sum[half:])
        pair_other[:, value_span] = low(value_sum[half:])


def pair_split_kernel(refs):
    mine, received, own = refs[:3]
    rows = own.shape[0]
    own[...] = mine[:rows] + received[:rows].astype(f32)
    for place, part in enumerate(refs[3:], 1):
        span = slice(place * rows, (place + 1) * rows)
        part[...] = low(mine[span] + received[span].astype(f32))


def pair_sum_kernel(parts, refs):
    own = refs[0]
    cosine, sine, pair_delta, bias_part = refs[1 + parts :]
    total = own[...]
    for part in refs[1 : 1 + parts]:
        total = total + part[...].astype(f32)
    for spot in range(2 * KV):
        span = slice(spot * HD, (spot + 1) * HD)
        part = total[:, span]
        if spot < KV:
            part = rope(part, cosine[...], sine[...])
        part = low(part)
        pair_delta[:, span] = part
        bias_part[:, span] = jnp.sum(part.astype(f32), axis=0, keepdims=True)


def weight_grad_kernel(places, refs):
    columns = refs[0]
    pieces = refs[1 : 1 + len(places)]
    result, deltas, sems = refs[1 + len(places) :]
    copies = []
    for place, piece in enumerate(pieces):
        row, start = places[place]
        rows, width = piece.shape
        copies.append(
            pltpu.make_async_copy(
                piece, deltas.at[pl.ds(row, rows), pl.ds(start, width)], sems.at[place]
            )
        )
    for copy in copies:
        copy.start()
    for copy in copies:
        copy.wait()
    result[...] = low(inner(columns[...], deltas[...]))


def weight_grad(values, *gathered):
    count = lax.axis_size("grp")
    places, pieces, start = [], [], 0
    for group in gathered:
        rows, width = group[0].shape
        spots = plane_spots(group)
        for side in range(2):
            places += [((side * count + step) * rows, start + offset) for step, offset in spots]
        pieces += group
        start += width
    (part,) = call(
        lambda *refs: weight_grad_kernel(places, refs),
        [((values.shape[1], start), bf16)],
        [values],
        pieces,
        [pltpu.VMEM((values.shape[0], start), bf16), pltpu.SemaphoreType.DMA((len(pieces),))],
    )
    return lax.psum_scatter(part, "fsdp", scatter_dimension=0, tiled=True).astype(f32)


def forward_back_kernel(count, refs):
    normed, active_delta = refs[:2]
    pieces = refs[2 : 2 + 2 * (count + 1)]
    active, gate_delta, up_delta, normed_delta, weights, sems = refs[2 + 2 * (count + 1) :]
    rows, width = pieces[0].shape
    slot = weights.shape[1] // count

    @pl.when(pl.program_id(0) == 0)
    def fetch():
        copies = []
        for which in range(2):
            for place in range(count + 1):
                piece = pieces[which * (count + 1) + place]
                step = min(place, count - 1)
                start = width // 2 if place == count else 0
                copies.append(
                    pltpu.make_async_copy(
                        piece,
                        weights.at[which, pl.ds(step * slot, rows), pl.ds(start, piece.shape[1])],
                        sems.at[len(copies)],
                    )
                )
        for copy in copies:
            copy.start()
        for copy in copies:
            copy.wait()
        if slot > rows:
            for which in range(2):
                for step in range(count):
                    spare = slice(step * slot + rows, (step + 1) * slot)
                    weights[which, spare, :] = jnp.zeros((slot - rows, width), bf16)

    gate = matmul_nt(normed[...], weights[0])
    upward = matmul_nt(normed[...], weights[1])
    delta = active_delta[...].astype(f32)
    sigmoid = 1.0 / (1.0 + jnp.exp(-gate))
    silu = gate * sigmoid
    active[...] = low(silu * upward)
    gate_low = low(delta * upward * (sigmoid * (1.0 + gate * (1.0 - sigmoid))))
    up_low = low(delta * silu)
    gate_delta[...] = gate_low
    up_delta[...] = up_low
    normed_delta[...] = low(matmul(gate_low, weights[0]) + matmul(up_low, weights[1]))


def forward_back(normed_all, active_delta, gate_pieces, up_pieces):
    tokens, width = normed_all.shape
    units = active_delta.shape[1]
    tile = 256

    def tiles(columns):
        return pl.BlockSpec((tile, columns), lambda i: (i, 0))

    pieces = list(gate_pieces) + list(up_pieces)
    count = len(gate_pieces) - 1
    return pl.pallas_call(
        lambda *refs: forward_back_kernel(count, refs),
        grid=(tokens // tile,),
        out_shape=[jax.ShapeDtypeStruct((tokens, n), bf16) for n in (units, units, units, width)],
        in_specs=[tiles(width), tiles(units)] + [pl.BlockSpec(memory_space=pl.ANY)] * len(pieces),
        out_specs=[tiles(units), tiles(units), tiles(units), tiles(width)],
        scratch_shapes=[
            pltpu.VMEM((2, units, width), bf16),
            pltpu.SemaphoreType.DMA((len(pieces),)),
        ],
        compiler_params=pltpu.CompilerParams(vmem_limit_bytes=VMEM_BYTES),
    )(normed_all, active_delta, *pieces)


def finish_kernel(gathered, refs):
    query_delta, pair_delta, hidden, middle_delta, gain = refs[:5]
    count = 1 + 2 * len(gathered[2])
    pieces = refs[5 : 5 + count]
    input_delta, weight, sems = refs[5 + count :]
    copies = assemble(*weight_refs(gathered, pieces), weight, sems)
    for copy in copies:
        copy.wait()
    split = query_delta.shape[1]
    delta = matmul_nt(query_delta[...], weight[:, :split]) + matmul_nt(
        pair_delta[...], weight[:, split:]
    )
    term, unit = norm_back(delta, hidden[...].astype(f32), gain[...])
    input_delta[...] = middle_delta[...] + term


def sum_everywhere(values):
    for axis in ("core", "grp", "fsdp"):
        count = lax.axis_size(axis)
        bit = 1
        while bit < count:
            values = values + lax.ppermute(values, axis, [(i, i ^ bit) for i in range(count)])
            bit *= 2
    return values


def local(
    hidden,
    positions,
    first_gain,
    query_weight,
    key_weight,
    value_weight,
    query_bias,
    key_bias,
    value_bias,
    output_weight,
    second_gain,
    gate_weight,
    up_weight,
    down_weight,
    cotangent,
):
    rows = hidden.shape[0]
    width = hidden.shape[1]
    ctx_here = lax.axis_index("grp") * lax.axis_size("core") + lax.axis_index("core")
    own_places = lax.dynamic_slice_in_dim(positions, ctx_here * rows, rows)
    q_width, k_width = H * HD, KV * HD

    near = lax.axis_size("grp") == 4 and gate_weight.shape[1] % 8 == 0
    projections = jnp.concatenate([query_weight, key_weight, value_weight], axis=1)
    qkv_rows = gather_rows(projections)

    def columns(values):
        return sequence_order(
            lax.all_to_all(values, SEQ_AXES, split_axis=1, concat_axis=0, tiled=True)
        )

    inputs = hidden.astype(f32)
    unit_columns = columns(low(inputs * rms_scale(inputs)))
    gate_own, up_own = gate_weight.T, up_weight.T
    down_near = gather_near(down_weight) if near else ()
    small = jnp.concatenate([first_gain, second_gain, query_bias, key_bias, value_bias])
    devices = lax.axis_size(EVERY)
    device_here = lax.axis_index(EVERY)
    small_all = sum_everywhere(
        lax.dynamic_update_slice_in_dim(
            jnp.zeros((devices, small.shape[0]), jnp.float32),
            small.astype(jnp.float32)[None],
            device_here,
            0,
        )
    )
    down_pieces = gather_far(down_weight, down_near) if near else ()
    qkv_rows = after(qkv_rows, small_all, unit_columns, *down_pieces)
    weight_qkv = gather_weight(qkv_rows)
    own = width // devices
    kv_own = k_width // devices
    gain_one = small_all[:, :own].reshape(1, width)
    gain_two = small_all[:, own : 2 * own].reshape(1, width)
    bias_qkv = jnp.concatenate(
        [
            small_all[:, 2 * own : 3 * own].reshape(q_width),
            small_all[:, 3 * own : 3 * own + kv_own].reshape(k_width),
            small_all[:, 3 * own + kv_own :].reshape(k_width),
        ]
    ).reshape(1, -1)
    output_rows = gather_rows(output_weight, qkv_rows)
    weight_output = gather_weight(after(output_rows, *weight_qkv[2]))
    cotangent_all = lax.all_gather(cotangent, TP_AXES, axis=0, tiled=True)

    cosine, sine = rope_tables(own_places)
    normed, queries, pairs_local = call(
        lambda *refs: project_kernel(weight_qkv, refs),
        [((rows, width), bf16), ((H * rows, HD), bf16), ((rows, 2 * k_width), bf16)],
        [hidden, gain_one, bias_qkv, cosine, sine],
        weight_args(weight_qkv),
        weight_scratch(weight_qkv, (width, q_width + 2 * k_width)),
    )
    pairs = gather_small(pairs_local)
    blocks = len(pairs)
    length = blocks * rows
    places = positions.reshape(-1, rows)
    steps = jnp.arange(places.shape[0], dtype=jnp.int32)
    from_ctx = ctx_here ^ jnp.concatenate([steps[0::2], steps[1::2]])
    matches = from_ctx[:, None] == steps[None, :]
    key_places = jnp.sum(jnp.where(matches[:, :, None], places[None], 0), axis=1).reshape(1, length)
    query_places = own_places.reshape(rows, 1)
    pair_scratch = [
        pltpu.VMEM((length, 2 * k_width), bf16),
        pltpu.SemaphoreType.DMA((blocks,)),
    ]
    mixed_low, log_sums = call(
        lambda *refs: attend_kernel(blocks, refs),
        [((rows, q_width), bf16), ((H * rows, 1), f32)],
        [queries, key_places, query_places],
        pairs,
        pair_scratch,
    )
    gate_near = gather_near(after(gate_own, *weight_output[2][2:])) if near else ()
    middle, normed_two = call(
        lambda *refs: output_kernel(weight_output, refs),
        [((rows, width), f32), ((rows, width), bf16)],
        [mixed_low, hidden, gain_two],
        weight_args(weight_output),
        weight_scratch(weight_output, (q_width, width)),
    )
    normed_two = after(normed_two, *gate_near)

    up_near = gather_near(after(up_own, *gate_near)) if near else ()

    normed_all = lax.all_gather(normed_two, TP_AXES, axis=0, tiled=True)
    if near:
        down_rows = join(down_pieces)
    else:
        down_rows = gather_group(down_weight)
    active_delta = low(matmul_nt(cotangent_all, down_rows))
    if near:
        gate_pieces = gather_far(gate_own, gate_near)
        up_pieces = gather_far(up_own, up_near)
        active, gate_delta, up_delta, normed_two_part = forward_back(
            normed_all, active_delta, gate_pieces, up_pieces
        )
    else:
        gate_rows, up_rows = gather_group(gate_own), gather_group(up_own)
        gate = matmul_nt(normed_all, gate_rows)
        upward = matmul_nt(normed_all, up_rows)
        delta = active_delta.astype(f32)
        sigmoid = 1.0 / (1.0 + jnp.exp(-gate))
        silu = gate * sigmoid
        active = low(silu * upward)
        gate_delta = low(delta * upward * (sigmoid * (1.0 + gate * (1.0 - sigmoid))))
        up_delta = low(delta * silu)
        normed_two_part = low(matmul(gate_delta, gate_rows) + matmul(up_delta, up_rows))
    normed_two_delta = lax.psum_scatter(
        normed_two_part, TP_AXES, scatter_dimension=0, tiled=True
    )
    mixed_columns = columns(after(mixed_low, normed_two_part))
    out_part = matmul(active, down_rows)
    out_sum = lax.psum_scatter(low(out_part), TP_AXES, scatter_dimension=0, tiled=True)
    gate_grad_sums = inner(gate_delta, normed_all)
    up_grad_sums = inner(up_delta, normed_all)
    down_grad_sums = inner(active, cotangent_all)

    middle_delta, attention_low, mixed_delta, second_gain_part = call(
        lambda *refs: middle_kernel(weight_output, refs),
        [
            ((rows, width), f32),
            ((rows, width), bf16),
            ((H * rows, HD), bf16),
            ((1, width), f32),
        ],
        [normed_two_delta, middle, cotangent, gain_two],
        weight_args(weight_output),
        weight_scratch(weight_output, (q_width, width)),
    )
    query_delta, query_bias_part, pair_mine, pair_other = call(
        lambda *refs: attend_back_kernel(blocks, refs),
        [
            ((rows, q_width), bf16),
            ((1, q_width), f32),
            ((length // 2, 2 * k_width), f32),
            ((length // 2, 2 * k_width), bf16),
        ],
        [queries, mixed_delta, log_sums, key_places, query_places, cosine, -sine],
        pairs,
        pair_scratch,
    )
    cuts = call(
        lambda *refs: pair_split_kernel(refs),
        [((rows, 2 * k_width), f32)] + [((rows, 2 * k_width), bf16)] * (blocks // 2 - 1),
        [pair_mine, other_core(pair_other)],
    )
    pair_delta, pair_bias_part = call(
        lambda *refs: pair_sum_kernel(blocks // 2 - 1, refs),
        [((rows, 2 * k_width), bf16), ((1, 2 * k_width), f32)],
        [cuts[0]] + [exchange(cut, i) for i, cut in enumerate(cuts[1:], 1)] + [cosine, -sine],
    )
    output_grad = weight_grad(mixed_columns, gather_plane(attention_low))
    pair_pieces = gather_small(pair_delta)
    unit_grad = weight_grad(unit_columns, gather_plane(query_delta), pair_pieces)
    (input_delta,) = call(
        lambda *refs: finish_kernel(weight_qkv, refs),
        [((rows, width), f32)],
        [query_delta, pair_delta, hidden, middle_delta, gain_one],
        weight_args(weight_qkv),
        weight_scratch(weight_qkv, (width, q_width + 2 * k_width)),
    )
    first_gain_grad = jnp.sum(unit_grad * projections.astype(f32), axis=1)
    scaled_grad = unit_grad * first_gain.astype(f32)[:, None]

    unit_rows = down_weight.shape[0]
    down_grad = scatter_group(down_grad_sums, unit_rows)
    gate_grad = scatter_group(gate_grad_sums, unit_rows, *pair_pieces).T
    up_grad = scatter_group(up_grad_sums, unit_rows, *pair_pieces).T
    layer_out = low(middle + after(out_sum, pair_delta).astype(f32))

    small_sum = sum_everywhere(
        jnp.concatenate([second_gain_part, query_bias_part, pair_bias_part], axis=1)
    )[0]

    def own_part(start, size):
        return lax.dynamic_slice_in_dim(small_sum, start + device_here * size, size)

    return (
        layer_out,
        input_delta,
        first_gain_grad,
        scaled_grad[:, :q_width],
        scaled_grad[:, q_width : q_width + k_width],
        scaled_grad[:, q_width + k_width :],
        own_part(width, own),
        own_part(width + q_width, kv_own),
        own_part(width + q_width + k_width, kv_own),
        output_grad,
        own_part(0, own),
        gate_grad,
        up_grad,
        down_grad,
    )


def solution(mesh):
    cores = 2
    ctx, fsdp = mesh.shape["ctx"], mesh.shape["fsdp"]
    split = Mesh(mesh.devices.reshape(ctx // cores, cores, fsdp), EVERY)
    tokens = P(("fsdp", "grp", "core"), None)
    in_specs = (
        tokens,
        P("fsdp"),
        P(EVERY),
        P(EVERY, None),
        P(EVERY, None),
        P(EVERY, None),
        P(EVERY),
        P(EVERY),
        P(EVERY),
        P(EVERY, None),
        P(EVERY),
        P(None, EVERY),
        P(None, EVERY),
        P(EVERY, None),
        tokens,
    )
    out_specs = (
        tokens,
        tokens,
        P(EVERY),
        P(EVERY, None),
        P(EVERY, None),
        P(EVERY, None),
        P(EVERY),
        P(EVERY),
        P(EVERY),
        P(EVERY, None),
        P(EVERY),
        P(None, EVERY),
        P(None, EVERY),
        P(EVERY, None),
    )
    return jax.shard_map(local, mesh=split, in_specs=in_specs, out_specs=out_specs, check_vma=False)
```

```python
import jax
import jax.numpy as jnp
from jax import lax
from jax.experimental import pallas as pl
from jax.experimental.pallas import tpu as pltpu
from jax.sharding import Mesh
from jax.sharding import PartitionSpec as P

H = 12
KV = 2
HD = 128

epsilon = 1e-06
rope_base = 1000000.0
neg_large = -1e30

bf16 = jnp.bfloat16
f32 = jnp.float32
VMEM_BYTES = 56 * 2**20

EVERY = ("grp", "core", "fsdp")
SEQ_AXES = ("grp", "core")
TP_AXES = ("fsdp", "core")


def rms_scale(values):
    return lax.rsqrt(jnp.mean(values * values, axis=-1, keepdims=True) + epsilon)


def rope_tables(places):
    half_width = HD // 2
    frequency = rope_base ** (-2.0 * jnp.arange(half_width, dtype=jnp.float32) / HD)
    angles = places.astype(jnp.float32)[:, None] * frequency[None, :]
    cosine, sine = jnp.cos(angles), jnp.sin(angles)
    return jnp.concatenate([cosine, cosine], axis=1), jnp.concatenate([-sine, sine], axis=1)


def matmul(left, right):
    return jnp.dot(left, right, preferred_element_type=jnp.float32)


def matmul_nt(left, right):
    return lax.dot_general(
        left, right, (((1,), (1,)), ((), ())), preferred_element_type=jnp.float32
    )


def inner(left, right):
    return lax.dot_general(
        left, right, (((0,), (0,)), ((), ())), preferred_element_type=jnp.float32
    )


def low(values):
    return values.astype(jnp.bfloat16)


def after(values, *others):
    return lax.optimization_barrier((values, others))[0]


def exchange(values, bit):
    count = lax.axis_size("grp")
    return lax.ppermute(values, "grp", [(i, i ^ bit) for i in range(count)])


def other_core(values):
    return lax.ppermute(values, "core", [(0, 1), (1, 0)])


def gather_group(block):
    count = lax.axis_size("grp")
    if count != 4:
        bit = 1
        while bit < count:
            block = jnp.concatenate([block, exchange(block, bit)], axis=0)
            bit *= 2
        return block
    half = block.shape[1] // 2
    from_x = exchange(block, 1)
    from_y = exchange(block, 2)
    left = exchange(from_x[:, :half], 2)
    right = exchange(from_y[:, half:], 1)
    corner = jnp.concatenate([left, right], axis=1)
    return jnp.concatenate([block, from_x, from_y, corner], axis=0)


def gather_near(block):
    return exchange(block, 1), exchange(block, 2)


def gather_far(block, near, *before):
    from_x, from_y = near
    half = block.shape[-1] // 2
    left = exchange(after(from_x, *before)[..., :half], 2)
    right = exchange(after(from_y, *before)[..., half:], 1)
    return block, from_x, from_y, left, right


def join(pieces):
    rows, width = pieces[0].shape
    spare = jnp.zeros((-rows % 16, width), bf16)
    corner = jnp.concatenate(pieces[3:], axis=1)
    slots = []
    for piece in (*pieces[:3], corner):
        slots += [piece, spare]
    return jnp.concatenate(slots, axis=0)


def scatter_group(parts, rows, *before):
    count = lax.axis_size("grp")
    slot = parts.shape[0] // count
    if count != 4:
        bit = count // 2
        parts = parts.astype(jnp.float32)
        while bit:
            keep, give = parts[: bit * rows], parts[bit * rows :]
            parts = keep + exchange(low(give), bit).astype(jnp.float32)
            bit //= 2
        return after(parts, *before)
    half = parts.shape[1] // 2
    own, for_x, for_y, corner = (
        parts[i * slot : i * slot + rows].astype(jnp.float32) for i in range(4)
    )
    corner = low(corner)
    from_x = exchange(corner[:, :half], 1).astype(jnp.float32)
    from_y = exchange(corner[:, half:], 2).astype(jnp.float32)
    for_y = jnp.concatenate([for_y[:, :half] + from_x, for_y[:, half:]], axis=1)
    for_x = jnp.concatenate([for_x[:, :half], for_x[:, half:] + from_y], axis=1)
    from_x = exchange(after(low(for_x), *before), 1).astype(jnp.float32)
    from_y = exchange(after(low(for_y), *before), 2).astype(jnp.float32)
    return own + from_x + from_y


def gather_chips(block):
    return [block] + [exchange(block, step) for step in range(1, lax.axis_size("grp"))]


def gather_small(block):
    mine = gather_chips(block)
    return mine + [other_core(piece) for piece in mine]


def plane_spots(pieces):
    if len(pieces) > lax.axis_size("grp"):
        return (0, 0), (1, 0), (2, 0), (3, 0), (3, pieces[3].shape[1])
    return tuple((i, 0) for i in range(len(pieces)))


def gather_plane(block, *before):
    part = block.shape[1] // 2
    if lax.axis_size("grp") != 4 or part < 512:
        return gather_chips(block)
    from_x, from_y = gather_near(block)
    left = exchange(after(from_x, *before)[:, :part], 2)
    right = exchange(after(from_y, *before)[:, part:], 1)
    return [block, from_x, from_y, left, right]


def gather_rows(block, *before):
    return lax.all_gather(after(block, *before), ("core", "fsdp"), axis=0, tiled=True)


def weight_near(rows):
    half = rows.shape[1] // 2
    own = lax.dynamic_slice_in_dim(rows, lax.axis_index("core") * half, half, 1)
    return (own, *gather_near(own)) if lax.axis_size("grp") == 4 else (own,)


def gather_weight(rows, near, before=(), late=()):
    count = lax.axis_size("grp")
    height, half = rows.shape[0], rows.shape[1] // 2
    if count == 4:
        part = half // 2
        own, from_x, from_y = near
        left = exchange(after(from_x, *before)[:, :part], 2)
        right = exchange(after(from_y, *before)[:, part:], 1)
        spots = ((1, 0), (2, 0), (3, 0), (3, part))
        mine = (from_x, from_y, left, right)
        other = tuple(other_core(piece) for piece in mine[:2])
        other += tuple(other_core(after(piece, *late)) for piece in mine[2:])
        return spots, rows, mine, other
    else:
        blocks = gather_group(near[0])
        spots = tuple((i, 0) for i in range(1, count))
        mine = tuple(blocks[i * height : (i + 1) * height] for i in range(1, count))
    return spots, rows, mine, tuple(other_core(piece) for piece in mine)


def gather_stacked(pieces, *before):
    stack = after(jnp.stack(pieces), *before)
    return (), lax.all_gather(stack, ("core", "fsdp"), axis=0, tiled=False), (), ()


def assemble(spots, own_ref, mine_refs, other_refs, full_ref, sems):
    grp, core = lax.axis_index("grp"), lax.axis_index("core")
    if len(own_ref.shape) == 4:
        count = own_ref.shape[1]
        copies = [
            pltpu.make_async_copy(own_ref.at[:, i], full_ref.at[grp ^ i], sems.at[i])
            for i in range(count)
        ]
        for copy in copies:
            copy.start()
        return copies
    height, half = own_ref.shape[0], full_ref.shape[1] // 2

    def rows_of(step):
        return pl.ds(pl.multiple_of((grp ^ step) * height, height), height)

    copies = [pltpu.make_async_copy(own_ref, full_ref.at[rows_of(0), :], sems.at[0])]
    for place, (step, offset) in enumerate(spots):
        for side, refs in ((core, mine_refs), (1 - core, other_refs)):
            width = refs[place].shape[1]
            start = pl.multiple_of(side * half + offset, 128)
            copies.append(
                pltpu.make_async_copy(
                    refs[place],
                    full_ref.at[rows_of(step), pl.ds(start, width)],
                    sems.at[len(copies)],
                )
            )
    for copy in copies:
        copy.start()
    return copies


def call(kernel, outs, ins, anys=(), scratch=()):
    whole = pl.BlockSpec(memory_space=pltpu.VMEM)
    left = pl.BlockSpec(memory_space=pl.ANY)
    return pl.pallas_call(
        kernel,
        out_shape=[jax.ShapeDtypeStruct(shape, dtype) for shape, dtype in outs],
        in_specs=[whole] * len(ins) + [left] * len(anys),
        out_specs=[whole] * len(outs),
        scratch_shapes=list(scratch),
        compiler_params=pltpu.CompilerParams(vmem_limit_bytes=VMEM_BYTES),
    )(*ins, *anys)


def weight_scratch(gathered, shape):
    spots, own, mine, other = gathered
    if len(own.shape) == 4:
        parts, count, rows, width = own.shape
        return [
            pltpu.VMEM((count, parts, rows, width), bf16),
            pltpu.SemaphoreType.DMA((count,)),
        ]
    return [
        pltpu.VMEM(shape, bf16),
        pltpu.SemaphoreType.DMA((1 + 2 * len(mine),)),
    ]


def weight_args(gathered):
    spots, own, mine, other = gathered
    return [own, *mine, *other]


def weight_refs(gathered, refs):
    count = len(gathered[2])
    return gathered[0], refs[0], refs[1 : 1 + count], refs[1 + count : 1 + 2 * count]


def rope(values, cosine, sine):
    return values * cosine + pltpu.roll(values, HD // 2, 1) * sine


def project_kernel(gathered, refs):
    hidden, gain, bias, cosine, sine = refs[:5]
    count = 1 + 2 * len(gathered[2])
    pieces = refs[5 : 5 + count]
    normed, queries, pairs, weight, sems = refs[5 + count :]
    copies = assemble(*weight_refs(gathered, pieces), weight, sems)
    inputs = hidden[...].astype(f32)
    normed[...] = low(inputs * rms_scale(inputs) * gain[...])
    for copy in copies:
        copy.wait()
    rows = hidden.shape[0]
    half = weight.shape[1] // 2
    heads_half = half // HD
    for side in range(2):
        lin = (
            matmul(normed[...], weight[:, side * half : (side + 1) * half])
            + bias[:, side * half : (side + 1) * half]
        )
        for spot in range(heads_half):
            head = side * heads_half + spot
            part = lin[:, spot * HD : (spot + 1) * HD]
            if head < H + KV:
                part = rope(part, cosine[...], sine[...])
            if head < H:
                queries[head * rows : (head + 1) * rows, :] = low(part)
            else:
                pairs[:, (head - H) * HD : (head - H + 1) * HD] = low(part)


def fetch_pairs(refs, full_ref, sems):
    rows = refs[0].shape[0]
    copies = [
        pltpu.make_async_copy(ref, full_ref.at[pl.ds(i * rows, rows), :], sems.at[i])
        for i, ref in enumerate(refs)
    ]
    for copy in copies:
        copy.start()
    return copies


def attend_kernel(blocks, refs):
    queries, key_places, own_places = refs[:3]
    pair_refs = refs[3 : 3 + blocks]
    mixed, log_sums, pairs, pair_sems = refs[3 + blocks :]
    for copy in fetch_pairs(pair_refs, pairs, pair_sems):
        copy.wait()
    rows = own_places.shape[0]
    allowed = key_places[...] <= own_places[...]
    scale = HD ** (-0.5)
    for head in range(H):
        group = head // (H // KV)
        keys = pairs[:, group * HD : (group + 1) * HD]
        values = pairs[:, (KV + group) * HD : (KV + group + 1) * HD]
        span = slice(head * rows, (head + 1) * rows)
        scores = jnp.where(allowed, matmul_nt(queries[span, :], keys) * scale, neg_large)
        top = jnp.max(scores, axis=1, keepdims=True)
        terms = jnp.exp(scores - top)
        total = jnp.sum(terms, axis=1, keepdims=True)
        log_sums[span, :] = top + jnp.log(total)
        probs = low(terms * (1.0 / total))
        mixed[:, head * HD : (head + 1) * HD] = low(matmul(probs, values))


def output_kernel(gathered, refs):
    mixed, hidden, gain = refs[:3]
    count = 1 + 2 * len(gathered[2])
    pieces = refs[3 : 3 + count]
    middle, normed_two, weight, sems = refs[3 + count :]
    for copy in assemble(*weight_refs(gathered, pieces), weight, sems):
        copy.wait()
    full = weight[...].reshape(mixed.shape[1], -1)
    result = hidden[...].astype(f32) + matmul(mixed[...], full)
    middle[...] = result
    normed_two[...] = low(result * rms_scale(result) * gain[...])


def norm_back(delta, values, gain):
    scale = rms_scale(values)
    unit = values * scale
    scaled = delta * gain
    return scale * (scaled - unit * jnp.mean(scaled * unit, axis=-1, keepdims=True)), unit


def middle_kernel(gathered, refs):
    normed_delta, middle, cotangent, gain = refs[:4]
    count = 1 + 2 * len(gathered[2])
    pieces = refs[4 : 4 + count]
    middle_delta, attention_low, mixed_delta, gain_part, weight, sems = refs[4 + count :]
    copies = assemble(*weight_refs(gathered, pieces), weight, sems)
    delta = normed_delta[...].astype(f32)
    term, unit = norm_back(delta, middle[...], gain[...])
    gain_part[...] = jnp.sum(delta * unit, axis=0, keepdims=True)
    result = cotangent[...].astype(f32) + term
    middle_delta[...] = result
    attention_low[...] = low(result)
    for copy in copies:
        copy.wait()
    rows = middle.shape[0]
    mixed = matmul_nt(low(result), weight[...].reshape(-1, result.shape[1]))
    for head in range(H):
        mixed_delta[head * rows : (head + 1) * rows, :] = low(mixed[:, head * HD : (head + 1) * HD])


def attend_back_kernel(blocks, refs):
    queries, mixed_delta, log_sums, key_places, own_places, cosine, sine, attention_low = refs[:8]
    pair_refs = refs[8 : 8 + blocks]
    deltas, bias_part, pair_mine, pair_other, pairs, pair_sems = refs[8 + blocks :]
    split = attention_low.shape[1]
    deltas[:, :split] = attention_low[...]
    for copy in fetch_pairs(pair_refs, pairs, pair_sems):
        copy.wait()
    rows = own_places.shape[0]
    half = pair_mine.shape[0]
    allowed = key_places[...] <= own_places[...]
    scale = HD ** (-0.5)
    group_size = H // KV
    for group in range(KV):
        key_span = slice(group * HD, (group + 1) * HD)
        value_span = slice((KV + group) * HD, (KV + group + 1) * HD)
        keys, values = pairs[:, key_span], pairs[:, value_span]
        key_sum = value_sum = None
        for head in range(group * group_size, (group + 1) * group_size):
            span = slice(head * rows, (head + 1) * rows)
            query = queries[span, :]
            mixed = mixed_delta[span, :]
            scores = matmul_nt(query, keys) * scale
            probs = jnp.where(allowed, jnp.exp(scores - log_sums[span, :]), 0.0)
            prob_delta = matmul_nt(mixed, values)
            dots = jnp.sum(probs * prob_delta, axis=1, keepdims=True)
            score_delta = low(probs * (prob_delta - dots))
            turned = low(rope(matmul(score_delta, keys) * scale, cosine[...], sine[...]))
            deltas[:, split + head * HD : split + (head + 1) * HD] = turned
            bias_part[:, head * HD : (head + 1) * HD] = jnp.sum(
                turned.astype(f32), axis=0, keepdims=True
            )
            key_part = inner(score_delta, query)
            value_part = inner(low(probs), mixed)
            key_sum = key_part if key_sum is None else key_sum + key_part
            value_sum = value_part if value_sum is None else value_sum + value_part
        key_sum = key_sum * scale
        pair_mine[:, key_span] = key_sum[:half]
        pair_mine[:, value_span] = value_sum[:half]
        pair_other[:, key_span] = low(key_sum[half:])
        pair_other[:, value_span] = low(value_sum[half:])


def pair_split_kernel(refs):
    mine, received, own = refs[:3]
    rows = own.shape[0]
    own[...] = mine[:rows] + received[:rows].astype(f32)
    for place, part in enumerate(refs[3:], 1):
        span = slice(place * rows, (place + 1) * rows)
        part[...] = low(mine[span] + received[span].astype(f32))


def pair_sum_kernel(parts, refs):
    own = refs[0]
    cosine, sine, pair_delta, bias_part = refs[1 + parts :]
    total = own[...]
    for part in refs[1 : 1 + parts]:
        total = total + part[...].astype(f32)
    for spot in range(2 * KV):
        span = slice(spot * HD, (spot + 1) * HD)
        part = total[:, span]
        if spot < KV:
            part = rope(part, cosine[...], sine[...])
        part = low(part)
        pair_delta[:, span] = part
        bias_part[:, span] = jnp.sum(part.astype(f32), axis=0, keepdims=True)


def weight_grad_kernel(places, split, refs):
    mixed, unit = refs[:2]
    pieces = refs[2 : 2 + len(places)]
    result, deltas, sems = refs[2 + len(places) :]
    grp = lax.axis_index("grp")
    copies = []
    for place, piece in enumerate(pieces):
        step, start = places[place]
        rows, width = piece.shape
        row = pl.multiple_of((grp ^ step) * rows, rows)
        copies.append(
            pltpu.make_async_copy(
                piece, deltas.at[pl.ds(row, rows), pl.ds(start, width)], sems.at[place]
            )
        )
    for copy in copies:
        copy.start()
    for copy in copies:
        copy.wait()
    parts = low(inner(mixed[...], deltas[:, :split])), low(inner(unit[...], deltas[:, split:]))
    cores, devices = 2, lax.axis_size("fsdp")
    rows = result.shape[0] // (cores * devices)
    if rows % 16:
        result[:, :split], result[:, split:] = parts
        return
    for device in range(devices):
        for core in range(cores):
            here = (device * cores + core) * rows
            there = (core * devices + device) * rows
            for part, span in zip(parts, (slice(0, split), slice(split, None))):
                result[here : here + rows, span] = part[there : there + rows]


def weight_grad(mixed, unit, split, *gathered):
    places, pieces, start = [], [], 0
    for group in gathered:
        places += [(step, start + offset) for step, offset in plane_spots(group)]
        pieces += group
        start += group[0].shape[1]
    (part,) = call(
        lambda *refs: weight_grad_kernel(places, split, refs),
        [((unit.shape[1], start), bf16)],
        [mixed, unit],
        pieces,
        [pltpu.VMEM((unit.shape[0], start), bf16), pltpu.SemaphoreType.DMA((len(pieces),))],
    )
    return part


def forward_back_kernel(count, refs):
    normed, active_delta = refs[:2]
    pieces = refs[2 : 2 + 2 * (count + 1)]
    active, deltas, normed_delta, weights, sems = refs[2 + 2 * (count + 1) :]
    rows, width = pieces[0].shape
    slot = weights.shape[1] // count

    @pl.when(pl.program_id(0) == 0)
    def fetch():
        copies = []
        for which in range(2):
            for place in range(count + 1):
                piece = pieces[which * (count + 1) + place]
                step = min(place, count - 1)
                start = width // 2 if place == count else 0
                copies.append(
                    pltpu.make_async_copy(
                        piece,
                        weights.at[which, pl.ds(step * slot, rows), pl.ds(start, piece.shape[1])],
                        sems.at[len(copies)],
                    )
                )
        for copy in copies:
            copy.start()
        for copy in copies:
            copy.wait()
        if slot > rows:
            for which in range(2):
                for step in range(count):
                    spare = slice(step * slot + rows, (step + 1) * slot)
                    weights[which, spare, :] = jnp.zeros((slot - rows, width), bf16)

    gate = matmul_nt(normed[...], weights[0])
    upward = matmul_nt(normed[...], weights[1])
    delta = active_delta[...].astype(f32)
    sigmoid = 1.0 / (1.0 + jnp.exp(-gate))
    silu = gate * sigmoid
    active[0] = low(silu * upward)
    gate_low = low(delta * upward * (sigmoid * (1.0 + gate * (1.0 - sigmoid))))
    up_low = low(delta * silu)
    deltas[0] = gate_low
    deltas[1] = up_low
    normed_delta[...] = low(matmul(gate_low, weights[0]) + matmul(up_low, weights[1]))


def forward_back(normed_all, active_delta, pieces):
    tokens, width = normed_all.shape
    units = active_delta.shape[1]
    tile = 256

    def tiles(columns):
        return pl.BlockSpec((tile, columns), lambda i: (i, 0))

    count = len(pieces) // 2 - 1
    return pl.pallas_call(
        lambda *refs: forward_back_kernel(count, refs),
        grid=(tokens // tile,),
        out_shape=[
            jax.ShapeDtypeStruct((1, tokens, units), bf16),
            jax.ShapeDtypeStruct((2, tokens, units), bf16),
            jax.ShapeDtypeStruct((tokens, width), bf16),
        ],
        in_specs=[tiles(width), tiles(units)] + [pl.BlockSpec(memory_space=pl.ANY)] * len(pieces),
        out_specs=[
            pl.BlockSpec((1, tile, units), lambda i: (0, i, 0)),
            pl.BlockSpec((2, tile, units), lambda i: (0, i, 0)),
            tiles(width),
        ],
        scratch_shapes=[
            pltpu.VMEM((2, units, width), bf16),
            pltpu.SemaphoreType.DMA((len(pieces),)),
        ],
        compiler_params=pltpu.CompilerParams(vmem_limit_bytes=VMEM_BYTES),
    )(normed_all, active_delta, *pieces)


def outer_kernel(refs):
    left, right, own, for_x, for_y, far_left, far_right = refs
    rows = own.shape[1]
    slot = left.shape[2] // 4
    total = inner(left[0], right[...])
    for place, part in enumerate((own, for_x, for_y)):
        part[0] = low(total[place * slot : place * slot + rows])
    far = low(total[3 * slot : 3 * slot + rows])

    @pl.when(pl.program_id(1) == 0)
    def first():
        far_left[0] = far

    @pl.when(pl.program_id(1) == 1)
    def second():
        far_right[0] = far


def outer(left, right, rows):
    stack, tokens, units = left.shape
    half = right.shape[1] // 2
    wide = jax.ShapeDtypeStruct((stack, rows, 2 * half), bf16)
    narrow = jax.ShapeDtypeStruct((stack, rows, half), bf16)
    by_half = pl.BlockSpec((1, rows, half), lambda i, j: (i, 0, j))
    whole = pl.BlockSpec((1, rows, half), lambda i, j: (i, 0, 0))
    return pl.pallas_call(
        lambda *refs: outer_kernel(refs),
        grid=(stack, 2),
        out_shape=[wide, wide, wide, narrow, narrow],
        in_specs=[
            pl.BlockSpec((1, tokens, units), lambda i, j: (i, 0, 0)),
            pl.BlockSpec((tokens, half), lambda i, j: (0, j)),
        ],
        out_specs=[by_half, by_half, by_half, whole, whole],
        compiler_params=pltpu.CompilerParams(vmem_limit_bytes=VMEM_BYTES),
    )(left, right)


def scatter_far(parts):
    own, for_x, for_y, far_left, far_right = parts
    from_x = exchange(far_left, 1)
    from_y = exchange(far_right, 2)
    spare = jnp.zeros_like(from_x)
    to_y = low(for_y.astype(f32) + jnp.concatenate([from_x, spare], axis=2).astype(f32))
    to_x = low(for_x.astype(f32) + jnp.concatenate([spare, from_y], axis=2).astype(f32))
    return to_x, to_y


def scatter_near(own, from_x, from_y, late):
    return own.astype(f32) + after(from_x, late).astype(f32) + after(from_y, late).astype(f32)


def finish_kernel(gathered, refs):
    deltas, pair_delta, hidden, middle_delta, gain = refs[:5]
    count = 1 + 2 * len(gathered[2])
    pieces = refs[5 : 5 + count]
    input_delta, weight, sems = refs[5 + count :]
    copies = assemble(*weight_refs(gathered, pieces), weight, sems)
    for copy in copies:
        copy.wait()
    split = weight.shape[1] - pair_delta.shape[1]
    delta = matmul_nt(deltas[:, -split:], weight[:, :split]) + matmul_nt(
        pair_delta[...], weight[:, split:]
    )
    term, unit = norm_back(delta, hidden[...].astype(f32), gain[...])
    input_delta[...] = middle_delta[...] + term


def sum_over(values, *axes):
    for axis in axes:
        count = lax.axis_size(axis)
        bit = 1
        while bit < count:
            values = values + lax.ppermute(values, axis, [(i, i ^ bit) for i in range(count)])
            bit *= 2
    return values


def local(
    hidden,
    positions,
    first_gain,
    query_weight,
    key_weight,
    value_weight,
    query_bias,
    key_bias,
    value_bias,
    output_weight,
    second_gain,
    gate_weight,
    up_weight,
    down_weight,
    cotangent,
):
    rows = hidden.shape[0]
    width = hidden.shape[1]
    ctx_here = lax.axis_index("grp") * lax.axis_size("core") + lax.axis_index("core")
    own_places = lax.dynamic_slice_in_dim(positions, ctx_here * rows, rows)
    q_width, k_width = H * HD, KV * HD

    near = lax.axis_size("grp") == 4 and gate_weight.shape[1] % 8 == 0
    projections = jnp.concatenate([query_weight, key_weight, value_weight], axis=1)
    qkv_rows = gather_rows(projections)

    def columns(values):
        return lax.all_to_all(values, "grp", split_axis=1, concat_axis=0, tiled=True)

    inputs = hidden.astype(f32)
    unit = low(inputs * rms_scale(inputs))
    gate_own, up_own = gate_weight.T, up_weight.T
    small = jnp.concatenate([first_gain, second_gain, query_bias, key_bias, value_bias])
    devices = lax.axis_size(EVERY)
    device_here = lax.axis_index(EVERY)
    small_plane = sum_over(
        lax.dynamic_update_slice_in_dim(
            jnp.zeros((devices, small.shape[0]), jnp.float32),
            small.astype(jnp.float32)[None],
            device_here,
            0,
        ),
        "grp",
    )
    output_chips = gather_chips(output_weight)
    small_all = sum_over(small_plane, "core", "fsdp")
    down_near = gather_near(after(down_weight, small_plane, *output_chips[1:])) if near else ()
    down_pieces = gather_far(down_weight, down_near, small_all) if near else ()
    qkv_rows = after(qkv_rows, small_all, *down_near)
    qkv_near = weight_near(qkv_rows)
    own = width // devices
    kv_own = k_width // devices
    gain_one = small_all[:, :own].reshape(1, width)
    gain_two = small_all[:, own : 2 * own].reshape(1, width)
    bias_qkv = jnp.concatenate(
        [
            small_all[:, 2 * own : 3 * own].reshape(q_width),
            small_all[:, 3 * own : 3 * own + kv_own].reshape(k_width),
            small_all[:, 3 * own + kv_own :].reshape(k_width),
        ]
    ).reshape(1, -1)
    cotangent_all = lax.all_gather(cotangent, TP_AXES, axis=0, tiled=True)

    cosine, sine = rope_tables(own_places)
    places = positions.reshape(-1, rows)
    steps = jnp.arange(places.shape[0], dtype=jnp.int32)
    from_ctx = ctx_here ^ jnp.concatenate([steps[0::2], steps[1::2]])
    matches = from_ctx[:, None] == steps[None, :]
    key_places = jnp.sum(jnp.where(matches[:, :, None], places[None], 0), axis=1).reshape(1, -1)
    unit_columns = columns(unit)
    ready = (*down_pieces[3:], unit_columns, gain_one, gain_two, bias_qkv, cosine, sine, key_places)
    weight_qkv = gather_weight(qkv_rows, qkv_near, ready)
    if output_weight.shape[0] % 16:
        output_rows = gather_rows(output_weight, qkv_rows)
        weight_output = gather_weight(output_rows, weight_near(output_rows))
    else:
        weight_output = gather_stacked(output_chips, qkv_rows)

    normed, queries, pairs_local = call(
        lambda *refs: project_kernel(weight_qkv, refs),
        [((rows, width), bf16), ((H * rows, HD), bf16), ((rows, 2 * k_width), bf16)],
        [hidden, gain_one, bias_qkv, cosine, sine],
        weight_args(weight_qkv),
        weight_scratch(weight_qkv, (width, q_width + 2 * k_width)),
    )
    pairs = gather_small(pairs_local)
    blocks = len(pairs)
    length = blocks * rows
    query_places = own_places.reshape(rows, 1)
    pair_scratch = [
        pltpu.VMEM((length, 2 * k_width), bf16),
        pltpu.SemaphoreType.DMA((blocks,)),
    ]
    mixed_low, log_sums = call(
        lambda *refs: attend_kernel(blocks, refs),
        [((rows, q_width), bf16), ((H * rows, 1), f32)],
        [queries, key_places, query_places],
        pairs,
        pair_scratch,
    )
    arrived = pairs[1 : blocks // 2]
    gate_near = gather_near(after(gate_own, *arrived)) if near else ()
    up_near = gather_near(after(up_own, *gate_near)) if near else ()
    middle, normed_two = call(
        lambda *refs: output_kernel(weight_output, refs),
        [((rows, width), f32), ((rows, width), bf16)],
        [mixed_low, hidden, gain_two],
        weight_args(weight_output),
        weight_scratch(weight_output, (q_width, width)),
    )
    normed_two = after(normed_two, *gate_near)


    normed_all = lax.all_gather(normed_two, TP_AXES, axis=0, tiled=True)
    if near:
        down_rows = join(down_pieces)
    else:
        down_rows = gather_group(down_weight)
    active_delta = low(matmul_nt(cotangent_all, down_rows))
    if near:
        active, unit_deltas, normed_two_part = forward_back(
            normed_all,
            active_delta,
            gather_far(gate_own, gate_near) + gather_far(up_own, up_near),
        )
    else:
        gate_rows, up_rows = gather_group(gate_own), gather_group(up_own)
        gate = matmul_nt(normed_all, gate_rows)
        upward = matmul_nt(normed_all, up_rows)
        delta = active_delta.astype(f32)
        sigmoid = 1.0 / (1.0 + jnp.exp(-gate))
        silu = gate * sigmoid
        active = low(silu * upward)
        gate_delta = low(delta * upward * (sigmoid * (1.0 + gate * (1.0 - sigmoid))))
        up_delta = low(delta * silu)
        normed_two_part = low(matmul(gate_delta, gate_rows) + matmul(up_delta, up_rows))
    normed_two_delta = lax.psum_scatter(
        normed_two_part, TP_AXES, scatter_dimension=0, tiled=True
    )
    mixed_columns = columns(after(mixed_low, normed_two_part))
    unit_rows = down_weight.shape[0]
    if near:
        down_parts = outer(active, cotangent_all, unit_rows)
        down_to = scatter_far(down_parts)
        both_parts = outer(after(unit_deltas, down_parts[0]), normed_all, unit_rows)
        both_to = scatter_far(both_parts)
        active = after(active[0], both_parts[0])
    out_part = matmul(active, down_rows)
    if near:
        normed_two_delta = after(normed_two_delta, out_part, *down_to)
    out_sum = lax.psum_scatter(low(out_part), TP_AXES, scatter_dimension=0, tiled=True)

    middle_delta, attention_low, mixed_delta, second_gain_part = call(
        lambda *refs: middle_kernel(weight_output, refs),
        [
            ((rows, width), f32),
            ((rows, width), bf16),
            ((H * rows, HD), bf16),
            ((1, width), f32),
        ],
        [normed_two_delta, middle, cotangent, gain_two],
        weight_args(weight_output),
        weight_scratch(weight_output, (q_width, width)),
    )
    deltas, query_bias_part, pair_mine, pair_other = call(
        lambda *refs: attend_back_kernel(blocks, refs),
        [
            ((rows, width + q_width), bf16),
            ((1, q_width), f32),
            ((length // 2, 2 * k_width), f32),
            ((length // 2, 2 * k_width), bf16),
        ],
        [
            queries,
            mixed_delta,
            log_sums,
            key_places,
            query_places,
            cosine,
            -sine,
            attention_low,
        ],
        pairs,
        pair_scratch,
    )
    if near:
        down_from = exchange(down_to[0], 1), exchange(down_to[1], 2)
        pair_mine = after(pair_mine, *both_to)
    cuts = call(
        lambda *refs: pair_split_kernel(refs),
        [((rows, 2 * k_width), f32)] + [((rows, 2 * k_width), bf16)] * (blocks // 2 - 1),
        [pair_mine, other_core(pair_other)],
    )
    pair_delta, pair_bias_part = call(
        lambda *refs: pair_sum_kernel(blocks // 2 - 1, refs),
        [((rows, 2 * k_width), bf16), ((1, 2 * k_width), f32)],
        [cuts[0]] + [exchange(cut, i) for i, cut in enumerate(cuts[1:], 1)] + [cosine, -sine],
    )
    small_plane = sum_over(
        jnp.concatenate([second_gain_part, query_bias_part, pair_bias_part], axis=1), "grp"
    )
    delta_pieces, pair_pieces = gather_plane(deltas), gather_chips(pair_delta)
    grad_part = weight_grad(mixed_columns, unit_columns, width, delta_pieces, pair_pieces)
    order = ("core", "fsdp") if output_weight.shape[0] % 16 else TP_AXES
    grads = lax.psum_scatter(grad_part, order, scatter_dimension=0, tiled=True).astype(f32)
    output_grad, unit_grad = grads[:, :width], grads[:, width:]
    (input_delta,) = call(
        lambda *refs: finish_kernel(weight_qkv, refs),
        [((rows, width), f32)],
        [deltas, pair_delta, hidden, middle_delta, gain_one],
        weight_args(weight_qkv),
        weight_scratch(weight_qkv, (width, q_width + 2 * k_width)),
    )
    first_gain_grad = jnp.sum(unit_grad * projections.astype(f32), axis=1)
    scaled_grad = unit_grad * first_gain.astype(f32)[:, None]

    if near:
        both_to = after(both_to, *delta_pieces, *pair_pieces, small_plane)
        both_from = exchange(both_to[0], 1), exchange(both_to[1], 2)
        down_grad = scatter_near(down_parts[0], *down_from, grad_part)[0]
        both_grads = scatter_near(both_parts[0], *both_from, grad_part)
        gate_grad, up_grad = both_grads[0].T, both_grads[1].T
    else:
        down_grad = scatter_group(inner(active, cotangent_all), unit_rows)
        gate_grad = scatter_group(inner(gate_delta, normed_all), unit_rows).T
        up_grad = scatter_group(inner(up_delta, normed_all), unit_rows).T
    layer_out = low(middle + after(out_sum, pair_delta).astype(f32))

    small_sum = sum_over(small_plane, "core", "fsdp")[0]

    def own_part(start, size):
        return lax.dynamic_slice_in_dim(small_sum, start + device_here * size, size)

    return (
        layer_out,
        input_delta,
        first_gain_grad,
        scaled_grad[:, :q_width],
        scaled_grad[:, q_width : q_width + k_width],
        scaled_grad[:, q_width + k_width :],
        own_part(width, own),
        own_part(width + q_width, kv_own),
        own_part(width + q_width + k_width, kv_own),
        output_grad,
        own_part(0, own),
        gate_grad,
        up_grad,
        down_grad,
    )


def solution(mesh):
    cores = 2
    ctx, fsdp = mesh.shape["ctx"], mesh.shape["fsdp"]
    split = Mesh(mesh.devices.reshape(ctx // cores, cores, fsdp), EVERY)
    tokens = P(("fsdp", "grp", "core"), None)
    in_specs = (
        tokens,
        P("fsdp"),
        P(EVERY),
        P(EVERY, None),
        P(EVERY, None),
        P(EVERY, None),
        P(EVERY),
        P(EVERY),
        P(EVERY),
        P(EVERY, None),
        P(EVERY),
        P(None, EVERY),
        P(None, EVERY),
        P(EVERY, None),
        tokens,
    )
    out_specs = (
        tokens,
        tokens,
        P(EVERY),
        P(EVERY, None),
        P(EVERY, None),
        P(EVERY, None),
        P(EVERY),
        P(EVERY),
        P(EVERY),
        P(EVERY, None),
        P(EVERY),
        P(None, EVERY),
        P(None, EVERY),
        P(EVERY, None),
    )
    return jax.shard_map(local, mesh=split, in_specs=in_specs, out_specs=out_specs, check_vma=False)
```

```python
import jax
import jax.numpy as jnp
from jax import lax
from jax.experimental import pallas as pl
from jax.experimental.pallas import tpu as pltpu
from jax.sharding import Mesh
from jax.sharding import PartitionSpec as P

H = 12
KV = 2
HD = 128

epsilon = 1e-06
rope_base = 1000000.0
neg_large = -1e30

bf16 = jnp.bfloat16
f32 = jnp.float32
VMEM_BYTES = 56 * 2**20

EVERY = ("grp", "core", "fsdp")
SEQ_AXES = ("grp", "core")
TP_AXES = ("fsdp", "core")


def rms_scale(values):
    return lax.rsqrt(jnp.mean(values * values, axis=-1, keepdims=True) + epsilon)


def rope_tables(places):
    half_width = HD // 2
    frequency = rope_base ** (-2.0 * jnp.arange(half_width, dtype=jnp.float32) / HD)
    angles = places.astype(jnp.float32)[:, None] * frequency[None, :]
    cosine, sine = jnp.cos(angles), jnp.sin(angles)
    return jnp.concatenate([cosine, cosine], axis=1), jnp.concatenate([-sine, sine], axis=1)


def matmul(left, right):
    return jnp.dot(left, right, preferred_element_type=jnp.float32)


def matmul_nt(left, right):
    return lax.dot_general(
        left, right, (((1,), (1,)), ((), ())), preferred_element_type=jnp.float32
    )


def inner(left, right):
    return lax.dot_general(
        left, right, (((0,), (0,)), ((), ())), preferred_element_type=jnp.float32
    )


def low(values):
    return values.astype(jnp.bfloat16)


def after(values, *others):
    return lax.optimization_barrier((values, others))[0]


def exchange(values, bit):
    count = lax.axis_size("grp")
    return lax.ppermute(values, "grp", [(i, i ^ bit) for i in range(count)])


def other_core(values):
    return lax.ppermute(values, "core", [(0, 1), (1, 0)])


def gather_group(block):
    count = lax.axis_size("grp")
    if count != 4:
        bit = 1
        while bit < count:
            block = jnp.concatenate([block, exchange(block, bit)], axis=0)
            bit *= 2
        return block
    half = block.shape[1] // 2
    from_x = exchange(block, 1)
    from_y = exchange(block, 2)
    left = exchange(from_x[:, :half], 2)
    right = exchange(from_y[:, half:], 1)
    corner = jnp.concatenate([left, right], axis=1)
    return jnp.concatenate([block, from_x, from_y, corner], axis=0)


def gather_near(block):
    return exchange(block, 1), exchange(block, 2)


def gather_far(block, near, *before):
    from_x, from_y = near
    half = block.shape[-1] // 2
    left = exchange(after(from_x, *before)[..., :half], 2)
    right = exchange(after(from_y, *before)[..., half:], 1)
    return block, from_x, from_y, left, right


def join(pieces):
    rows, width = pieces[0].shape
    spare = jnp.zeros((-rows % 16, width), bf16)
    corner = jnp.concatenate(pieces[3:], axis=1)
    slots = []
    for piece in (*pieces[:3], corner):
        slots += [piece, spare]
    return jnp.concatenate(slots, axis=0)


def scatter_group(parts, rows, *before):
    count = lax.axis_size("grp")
    slot = parts.shape[0] // count
    if count != 4:
        bit = count // 2
        parts = parts.astype(jnp.float32)
        while bit:
            keep, give = parts[: bit * rows], parts[bit * rows :]
            parts = keep + exchange(low(give), bit).astype(jnp.float32)
            bit //= 2
        return after(parts, *before)
    half = parts.shape[1] // 2
    own, for_x, for_y, corner = (
        parts[i * slot : i * slot + rows].astype(jnp.float32) for i in range(4)
    )
    corner = low(corner)
    from_x = exchange(corner[:, :half], 1).astype(jnp.float32)
    from_y = exchange(corner[:, half:], 2).astype(jnp.float32)
    for_y = jnp.concatenate([for_y[:, :half] + from_x, for_y[:, half:]], axis=1)
    for_x = jnp.concatenate([for_x[:, :half], for_x[:, half:] + from_y], axis=1)
    from_x = exchange(after(low(for_x), *before), 1).astype(jnp.float32)
    from_y = exchange(after(low(for_y), *before), 2).astype(jnp.float32)
    return own + from_x + from_y


def gather_chips(block):
    return [block] + [exchange(block, step) for step in range(1, lax.axis_size("grp"))]


def gather_small(block):
    mine = gather_chips(block)
    return mine + [other_core(piece) for piece in mine]


def plane_spots(pieces):
    if len(pieces) > lax.axis_size("grp"):
        return (0, 0), (1, 0), (2, 0), (3, 0), (3, pieces[3].shape[1])
    return tuple((i, 0) for i in range(len(pieces)))


def gather_plane(block, *before):
    part = block.shape[1] // 2
    if lax.axis_size("grp") != 4 or part < 512:
        return gather_chips(block)
    from_x, from_y = gather_near(block)
    left = exchange(after(from_x, *before)[:, :part], 2)
    right = exchange(after(from_y, *before)[:, part:], 1)
    return [block, from_x, from_y, left, right]


def gather_rows(block, *before):
    return lax.all_gather(after(block, *before), ("core", "fsdp"), axis=0, tiled=True)


def weight_near(rows):
    half = rows.shape[1] // 2
    own = lax.dynamic_slice_in_dim(rows, lax.axis_index("core") * half, half, 1)
    return (own, *gather_near(own)) if lax.axis_size("grp") == 4 else (own,)


def gather_weight(rows, near, before=(), late=()):
    count = lax.axis_size("grp")
    height, half = rows.shape[0], rows.shape[1] // 2
    if count == 4:
        part = half // 2
        own, from_x, from_y = near
        left = exchange(after(from_x, *before)[:, :part], 2)
        right = exchange(after(from_y, *before)[:, part:], 1)
        spots = ((1, 0), (2, 0), (3, 0), (3, part))
        mine = (from_x, from_y, left, right)
        other = tuple(other_core(piece) for piece in mine[:2])
        other += tuple(other_core(after(piece, *late)) for piece in mine[2:])
        return spots, rows, mine, other
    else:
        blocks = gather_group(near[0])
        spots = tuple((i, 0) for i in range(1, count))
        mine = tuple(blocks[i * height : (i + 1) * height] for i in range(1, count))
    return spots, rows, mine, tuple(other_core(piece) for piece in mine)


def gather_stacked(pieces, *before):
    stack = after(jnp.stack(pieces), *before)
    return (), lax.all_gather(stack, ("core", "fsdp"), axis=0, tiled=False), (), ()


def assemble(spots, own_ref, mine_refs, other_refs, full_ref, sems):
    grp, core = lax.axis_index("grp"), lax.axis_index("core")
    if len(own_ref.shape) == 4:
        count = own_ref.shape[1]
        copies = [
            pltpu.make_async_copy(own_ref.at[:, i], full_ref.at[grp ^ i], sems.at[i])
            for i in range(count)
        ]
        for copy in copies:
            copy.start()
        return copies
    height, half = own_ref.shape[0], full_ref.shape[1] // 2

    def rows_of(step):
        return pl.ds(pl.multiple_of((grp ^ step) * height, height), height)

    copies = [pltpu.make_async_copy(own_ref, full_ref.at[rows_of(0), :], sems.at[0])]
    for place, (step, offset) in enumerate(spots):
        for side, refs in ((core, mine_refs), (1 - core, other_refs)):
            width = refs[place].shape[1]
            start = pl.multiple_of(side * half + offset, 128)
            copies.append(
                pltpu.make_async_copy(
                    refs[place],
                    full_ref.at[rows_of(step), pl.ds(start, width)],
                    sems.at[len(copies)],
                )
            )
    for copy in copies:
        copy.start()
    return copies


def call(kernel, outs, ins, anys=(), scratch=()):
    whole = pl.BlockSpec(memory_space=pltpu.VMEM)
    left = pl.BlockSpec(memory_space=pl.ANY)
    return pl.pallas_call(
        kernel,
        out_shape=[jax.ShapeDtypeStruct(shape, dtype) for shape, dtype in outs],
        in_specs=[whole] * len(ins) + [left] * len(anys),
        out_specs=[whole] * len(outs),
        scratch_shapes=list(scratch),
        compiler_params=pltpu.CompilerParams(vmem_limit_bytes=VMEM_BYTES),
    )(*ins, *anys)


def weight_scratch(gathered, shape):
    spots, own, mine, other = gathered
    if len(own.shape) == 4:
        parts, count, rows, width = own.shape
        return [
            pltpu.VMEM((count, parts, rows, width), bf16),
            pltpu.SemaphoreType.DMA((count,)),
        ]
    return [
        pltpu.VMEM(shape, bf16),
        pltpu.SemaphoreType.DMA((1 + 2 * len(mine),)),
    ]


def weight_args(gathered):
    spots, own, mine, other = gathered
    return [own, *mine, *other]


def weight_refs(gathered, refs):
    count = len(gathered[2])
    return gathered[0], refs[0], refs[1 : 1 + count], refs[1 + count : 1 + 2 * count]


def rope(values, cosine, sine):
    return values * cosine + pltpu.roll(values, HD // 2, 1) * sine


def half_span(run, rows):
    return slice(run * rows // 2, (run + 1) * rows // 2)


def run_span(run, head, heads, rows):
    start = (run * H + head) * (rows // 2)
    return slice(start, start + heads * (rows // 2))


def project_kernel(gathered, refs):
    hidden, gain, bias, cosine, sine = refs[:5]
    count = 1 + 2 * len(gathered[2])
    pieces = refs[5 : 5 + count]
    normed, queries, pairs, weight, sems = refs[5 + count :]
    copies = assemble(*weight_refs(gathered, pieces), weight, sems)
    inputs = hidden[...].astype(f32)
    normed[...] = low(inputs * rms_scale(inputs) * gain[...])
    for copy in copies:
        copy.wait()
    rows = hidden.shape[0]
    half = weight.shape[1] // 2
    heads_half = half // HD
    for side in range(2):
        lin = (
            matmul(normed[...], weight[:, side * half : (side + 1) * half])
            + bias[:, side * half : (side + 1) * half]
        )
        for spot in range(heads_half):
            head = side * heads_half + spot
            part = lin[:, spot * HD : (spot + 1) * HD]
            if head < H + KV:
                part = rope(part, cosine[...], sine[...])
            if head < H:
                for run in range(2):
                    queries[run_span(run, head, 1, rows), :] = low(part)[half_span(run, rows)]
            else:
                pairs[:, (head - H) * HD : (head - H + 1) * HD] = low(part)


def fetch_pairs(refs, full_ref, sems):
    half = refs[0].shape[0] // 2
    copies = []
    for run in range(2):
        for i, ref in enumerate(refs):
            place = run * len(refs) + i
            copies.append(
                pltpu.make_async_copy(
                    ref.at[pl.ds(run * half, half), :],
                    full_ref.at[pl.ds(place * half, half), :],
                    sems.at[place],
                )
            )
    for copy in copies:
        copy.start()
    return copies


def allowed_keys(run, key_places, own_places):
    extent = key_places.shape[1] // 2 * (run + 1)
    own = own_places[half_span(run, own_places.shape[0]), :]
    own = jnp.concatenate([own] * (H // KV), axis=0)
    return extent, key_places[:, :extent] <= own


def attend_kernel(blocks, refs):
    queries, key_places, own_places = refs[:3]
    pair_refs = refs[3 : 3 + blocks]
    mixed, log_sums, pairs, pair_sems = refs[3 + blocks :]
    for copy in fetch_pairs(pair_refs, pairs, pair_sems):
        copy.wait()
    rows = own_places.shape[0]
    half = rows // 2
    scale = HD ** (-0.5)
    group_size = H // KV
    for run in range(2):
        extent, allowed = allowed_keys(run, key_places, own_places)
        for group in range(KV):
            keys = pairs[:extent, group * HD : (group + 1) * HD]
            values = pairs[:extent, (KV + group) * HD : (KV + group + 1) * HD]
            span = run_span(run, group * group_size, group_size, rows)
            scores = jnp.where(allowed, matmul_nt(queries[span, :], keys) * scale, neg_large)
            top = jnp.max(scores, axis=1, keepdims=True)
            terms = jnp.exp(scores - top)
            total = jnp.sum(terms, axis=1, keepdims=True)
            log_sums[span, :] = top + jnp.log(total)
            result = low(matmul(low(terms * (1.0 / total)), values))
            for spot in range(group_size):
                head = group * group_size + spot
                mixed[half_span(run, rows), head * HD : (head + 1) * HD] = result[
                    spot * half : (spot + 1) * half
                ]


def output_kernel(gathered, refs):
    mixed, hidden, gain = refs[:3]
    count = 1 + 2 * len(gathered[2])
    pieces = refs[3 : 3 + count]
    middle, normed_two, weight, sems = refs[3 + count :]
    for copy in assemble(*weight_refs(gathered, pieces), weight, sems):
        copy.wait()
    full = weight[...].reshape(mixed.shape[1], -1)
    result = hidden[...].astype(f32) + matmul(mixed[...], full)
    middle[...] = result
    normed_two[...] = low(result * rms_scale(result) * gain[...])


def norm_back(delta, values, gain):
    scale = rms_scale(values)
    unit = values * scale
    scaled = delta * gain
    return scale * (scaled - unit * jnp.mean(scaled * unit, axis=-1, keepdims=True)), unit


def middle_kernel(gathered, refs):
    normed_delta, middle, cotangent, gain = refs[:4]
    count = 1 + 2 * len(gathered[2])
    pieces = refs[4 : 4 + count]
    middle_delta, attention_low, mixed_delta, gain_part, weight, sems = refs[4 + count :]
    copies = assemble(*weight_refs(gathered, pieces), weight, sems)
    delta = normed_delta[...].astype(f32)
    term, unit = norm_back(delta, middle[...], gain[...])
    gain_part[...] = jnp.sum(delta * unit, axis=0, keepdims=True)
    result = cotangent[...].astype(f32) + term
    middle_delta[...] = result
    attention_low[...] = low(result)
    for copy in copies:
        copy.wait()
    rows = middle.shape[0]
    mixed = matmul_nt(low(result), weight[...].reshape(-1, result.shape[1]))
    for head in range(H):
        part = low(mixed[:, head * HD : (head + 1) * HD])
        for run in range(2):
            mixed_delta[run_span(run, head, 1, rows), :] = part[half_span(run, rows)]


def attend_back_kernel(blocks, refs):
    queries, mixed_delta, log_sums, key_places, own_places, cosine, sine, attention_low = refs[:8]
    pair_refs = refs[8 : 8 + blocks]
    deltas, bias_part, pair_mine, pair_other, pairs, pair_sems = refs[8 + blocks :]
    split = attention_low.shape[1]
    deltas[:, :split] = attention_low[...]
    for copy in fetch_pairs(pair_refs, pairs, pair_sems):
        copy.wait()
    rows = own_places.shape[0]
    half = rows // 2
    scale = HD ** (-0.5)
    group_size = H // KV
    for group in range(KV):
        key_span = slice(group * HD, (group + 1) * HD)
        value_span = slice((KV + group) * HD, (KV + group + 1) * HD)
        sums = []
        for run in range(2):
            extent, allowed = allowed_keys(run, key_places, own_places)
            keys, values = pairs[:extent, key_span], pairs[:extent, value_span]
            span = run_span(run, group * group_size, group_size, rows)
            query, mixed = queries[span, :], mixed_delta[span, :]
            scores = matmul_nt(query, keys) * scale
            probs = jnp.where(allowed, jnp.exp(scores - log_sums[span, :]), 0.0)
            prob_delta = matmul_nt(mixed, values)
            dots = jnp.sum(probs * prob_delta, axis=1, keepdims=True)
            score_delta = low(probs * (prob_delta - dots))
            turn = matmul(score_delta, keys) * scale
            here = half_span(run, rows)
            for spot in range(group_size):
                head = group * group_size + spot
                head_span = slice(head * HD, (head + 1) * HD)
                part = turn[spot * half : (spot + 1) * half]
                part = low(rope(part, cosine[here, :], sine[here, :]))
                deltas[here, split + head * HD : split + (head + 1) * HD] = part
                bias = jnp.sum(part.astype(f32), axis=0, keepdims=True)
                bias_part[:, head_span] = bias if run == 0 else bias_part[:, head_span] + bias
            sums.append((inner(score_delta, query) * scale, inner(low(probs), mixed)))
        early = sums[1][0].shape[0] // 2
        for which, to in enumerate((key_span, value_span)):
            first = sums[0][which] + sums[1][which][:early]
            for run, part in enumerate((first, sums[1][which][early:])):
                for block in range(blocks):
                    piece = part[block * half : (block + 1) * half]
                    start = block % (blocks // 2) * rows + run * half
                    if block < blocks // 2:
                        pair_mine[start : start + half, to] = piece
                    else:
                        pair_other[start : start + half, to] = low(piece)


def pair_split_kernel(refs):
    mine, received, own = refs[:3]
    rows = own.shape[0]
    own[...] = mine[:rows] + received[:rows].astype(f32)
    for place, part in enumerate(refs[3:], 1):
        span = slice(place * rows, (place + 1) * rows)
        part[...] = low(mine[span] + received[span].astype(f32))


def pair_sum_kernel(parts, refs):
    own = refs[0]
    cosine, sine, pair_delta, bias_part = refs[1 + parts :]
    total = own[...]
    for part in refs[1 : 1 + parts]:
        total = total + part[...].astype(f32)
    for spot in range(2 * KV):
        span = slice(spot * HD, (spot + 1) * HD)
        part = total[:, span]
        if spot < KV:
            part = rope(part, cosine[...], sine[...])
        part = low(part)
        pair_delta[:, span] = part
        bias_part[:, span] = jnp.sum(part.astype(f32), axis=0, keepdims=True)


def weight_grad_kernel(places, split, refs):
    mixed, unit = refs[:2]
    pieces = refs[2 : 2 + len(places)]
    result, deltas, sems = refs[2 + len(places) :]
    grp = lax.axis_index("grp")
    copies = []
    for place, piece in enumerate(pieces):
        step, start = places[place]
        rows, width = piece.shape
        row = pl.multiple_of((grp ^ step) * rows, rows)
        copies.append(
            pltpu.make_async_copy(
                piece, deltas.at[pl.ds(row, rows), pl.ds(start, width)], sems.at[place]
            )
        )
    for copy in copies:
        copy.start()
    for copy in copies:
        copy.wait()
    parts = low(inner(mixed[...], deltas[:, :split])), low(inner(unit[...], deltas[:, split:]))
    cores, devices = 2, lax.axis_size("fsdp")
    rows = result.shape[0] // (cores * devices)
    if rows % 16:
        result[:, :split], result[:, split:] = parts
        return
    for device in range(devices):
        for core in range(cores):
            here = (device * cores + core) * rows
            there = (core * devices + device) * rows
            for part, span in zip(parts, (slice(0, split), slice(split, None))):
                result[here : here + rows, span] = part[there : there + rows]


def weight_grad(mixed, unit, split, *gathered):
    places, pieces, start = [], [], 0
    for group in gathered:
        places += [(step, start + offset) for step, offset in plane_spots(group)]
        pieces += group
        start += group[0].shape[1]
    (part,) = call(
        lambda *refs: weight_grad_kernel(places, split, refs),
        [((unit.shape[1], start), bf16)],
        [mixed, unit],
        pieces,
        [pltpu.VMEM((unit.shape[0], start), bf16), pltpu.SemaphoreType.DMA((len(pieces),))],
    )
    return part


def forward_back_kernel(count, refs):
    normed, active_delta = refs[:2]
    pieces = refs[2 : 2 + 2 * (count + 1)]
    active, deltas, normed_delta, weights, sems = refs[2 + 2 * (count + 1) :]
    rows, width = pieces[0].shape
    slot = weights.shape[1] // count

    @pl.when(pl.program_id(0) == 0)
    def fetch():
        copies = []
        for which in range(2):
            for place in range(count + 1):
                piece = pieces[which * (count + 1) + place]
                step = min(place, count - 1)
                start = width // 2 if place == count else 0
                copies.append(
                    pltpu.make_async_copy(
                        piece,
                        weights.at[which, pl.ds(step * slot, rows), pl.ds(start, piece.shape[1])],
                        sems.at[len(copies)],
                    )
                )
        for copy in copies:
            copy.start()
        for copy in copies:
            copy.wait()
        if slot > rows:
            for which in range(2):
                for step in range(count):
                    spare = slice(step * slot + rows, (step + 1) * slot)
                    weights[which, spare, :] = jnp.zeros((slot - rows, width), bf16)

    gate = matmul_nt(normed[...], weights[0])
    upward = matmul_nt(normed[...], weights[1])
    delta = active_delta[...].astype(f32)
    sigmoid = 1.0 / (1.0 + jnp.exp(-gate))
    silu = gate * sigmoid
    active[0] = low(silu * upward)
    gate_low = low(delta * upward * (sigmoid * (1.0 + gate * (1.0 - sigmoid))))
    up_low = low(delta * silu)
    deltas[0] = gate_low
    deltas[1] = up_low
    normed_delta[...] = low(matmul(gate_low, weights[0]) + matmul(up_low, weights[1]))


def forward_back(normed_all, active_delta, pieces):
    tokens, width = normed_all.shape
    units = active_delta.shape[1]
    tile = 256

    def tiles(columns):
        return pl.BlockSpec((tile, columns), lambda i: (i, 0))

    count = len(pieces) // 2 - 1
    return pl.pallas_call(
        lambda *refs: forward_back_kernel(count, refs),
        grid=(tokens // tile,),
        out_shape=[
            jax.ShapeDtypeStruct((1, tokens, units), bf16),
            jax.ShapeDtypeStruct((2, tokens, units), bf16),
            jax.ShapeDtypeStruct((tokens, width), bf16),
        ],
        in_specs=[tiles(width), tiles(units)] + [pl.BlockSpec(memory_space=pl.ANY)] * len(pieces),
        out_specs=[
            pl.BlockSpec((1, tile, units), lambda i: (0, i, 0)),
            pl.BlockSpec((2, tile, units), lambda i: (0, i, 0)),
            tiles(width),
        ],
        scratch_shapes=[
            pltpu.VMEM((2, units, width), bf16),
            pltpu.SemaphoreType.DMA((len(pieces),)),
        ],
        compiler_params=pltpu.CompilerParams(vmem_limit_bytes=VMEM_BYTES),
    )(normed_all, active_delta, *pieces)


def outer_kernel(refs):
    left, right, own, for_x, for_y, far_left, far_right = refs
    rows = own.shape[1]
    slot = left.shape[2] // 4
    total = inner(left[0], right[...])
    for place, part in enumerate((own, for_x, for_y)):
        part[0] = low(total[place * slot : place * slot + rows])
    far = low(total[3 * slot : 3 * slot + rows])

    @pl.when(pl.program_id(1) == 0)
    def first():
        far_left[0] = far

    @pl.when(pl.program_id(1) == 1)
    def second():
        far_right[0] = far


def outer(left, right, rows):
    stack, tokens, units = left.shape
    half = right.shape[1] // 2
    wide = jax.ShapeDtypeStruct((stack, rows, 2 * half), bf16)
    narrow = jax.ShapeDtypeStruct((stack, rows, half), bf16)
    by_half = pl.BlockSpec((1, rows, half), lambda i, j: (i, 0, j))
    whole = pl.BlockSpec((1, rows, half), lambda i, j: (i, 0, 0))
    return pl.pallas_call(
        lambda *refs: outer_kernel(refs),
        grid=(stack, 2),
        out_shape=[wide, wide, wide, narrow, narrow],
        in_specs=[
            pl.BlockSpec((1, tokens, units), lambda i, j: (i, 0, 0)),
            pl.BlockSpec((tokens, half), lambda i, j: (0, j)),
        ],
        out_specs=[by_half, by_half, by_half, whole, whole],
        compiler_params=pltpu.CompilerParams(vmem_limit_bytes=VMEM_BYTES),
    )(left, right)


def scatter_far(parts):
    own, for_x, for_y, far_left, far_right = parts
    from_x = exchange(far_left, 1)
    from_y = exchange(far_right, 2)
    spare = jnp.zeros_like(from_x)
    to_y = low(for_y.astype(f32) + jnp.concatenate([from_x, spare], axis=2).astype(f32))
    to_x = low(for_x.astype(f32) + jnp.concatenate([spare, from_y], axis=2).astype(f32))
    return to_x, to_y


def scatter_near(own, from_x, from_y, late):
    from_x, from_y = after((from_x, from_y), late)
    return own.astype(f32) + from_x.astype(f32) + from_y.astype(f32)


def finish_kernel(gathered, refs):
    deltas, pair_delta, hidden, middle_delta, gain = refs[:5]
    count = 1 + 2 * len(gathered[2])
    pieces = refs[5 : 5 + count]
    input_delta, weight, sems = refs[5 + count :]
    copies = assemble(*weight_refs(gathered, pieces), weight, sems)
    for copy in copies:
        copy.wait()
    split = weight.shape[1] - pair_delta.shape[1]
    delta = matmul_nt(deltas[:, -split:], weight[:, :split]) + matmul_nt(
        pair_delta[...], weight[:, split:]
    )
    term, unit = norm_back(delta, hidden[...].astype(f32), gain[...])
    input_delta[...] = middle_delta[...] + term


def sum_over(values, *axes):
    for axis in axes:
        count = lax.axis_size(axis)
        bit = 1
        while bit < count:
            values = values + lax.ppermute(values, axis, [(i, i ^ bit) for i in range(count)])
            bit *= 2
    return values


def local(
    hidden,
    positions,
    first_gain,
    query_weight,
    key_weight,
    value_weight,
    query_bias,
    key_bias,
    value_bias,
    output_weight,
    second_gain,
    gate_weight,
    up_weight,
    down_weight,
    cotangent,
):
    rows = hidden.shape[0]
    width = hidden.shape[1]
    ctx_here = lax.axis_index("grp") * lax.axis_size("core") + lax.axis_index("core")
    own_places = lax.dynamic_slice_in_dim(positions, ctx_here * rows, rows)
    q_width, k_width = H * HD, KV * HD

    near = lax.axis_size("grp") == 4 and gate_weight.shape[1] % 8 == 0
    projections = jnp.concatenate([query_weight, key_weight, value_weight], axis=1)
    qkv_rows = gather_rows(projections)

    def columns(values):
        return lax.all_to_all(values, "grp", split_axis=1, concat_axis=0, tiled=True)

    inputs = hidden.astype(f32)
    unit = low(inputs * rms_scale(inputs))
    gate_own, up_own = gate_weight.T, up_weight.T
    small = jnp.concatenate([first_gain, second_gain, query_bias, key_bias, value_bias])
    devices = lax.axis_size(EVERY)
    device_here = lax.axis_index(EVERY)
    small_plane = sum_over(
        lax.dynamic_update_slice_in_dim(
            jnp.zeros((devices, small.shape[0]), jnp.float32),
            small.astype(jnp.float32)[None],
            device_here,
            0,
        ),
        "grp",
    )
    output_chips = gather_chips(output_weight)
    small_all = sum_over(small_plane, "core", "fsdp")
    down_near = gather_near(after(down_weight, small_plane, *output_chips[1:])) if near else ()
    down_pieces = gather_far(down_weight, down_near, small_all) if near else ()
    qkv_rows = after(qkv_rows, small_all, *down_near)
    qkv_near = weight_near(qkv_rows)
    own = width // devices
    kv_own = k_width // devices
    gain_one = small_all[:, :own].reshape(1, width)
    gain_two = small_all[:, own : 2 * own].reshape(1, width)
    bias_qkv = jnp.concatenate(
        [
            small_all[:, 2 * own : 3 * own].reshape(q_width),
            small_all[:, 3 * own : 3 * own + kv_own].reshape(k_width),
            small_all[:, 3 * own + kv_own :].reshape(k_width),
        ]
    ).reshape(1, -1)
    cotangent_all = lax.all_gather(cotangent, TP_AXES, axis=0, tiled=True)

    cosine, sine = rope_tables(own_places)
    places = positions.reshape(-1, rows)
    steps = jnp.arange(places.shape[0], dtype=jnp.int32)
    from_ctx = ctx_here ^ jnp.concatenate([steps[0::2], steps[1::2]])
    matches = from_ctx[:, None] == steps[None, :]
    key_places = jnp.sum(jnp.where(matches[:, :, None], places[None], 0), axis=1)
    key_places = key_places.reshape(-1, 2, rows // 2).transpose(1, 0, 2).reshape(1, -1)
    unit_columns = columns(unit)
    ready = (unit_columns, gain_one, gain_two, bias_qkv, cosine, sine, key_places)
    weight_qkv = gather_weight(qkv_rows, qkv_near, ready)
    if output_weight.shape[0] % 16:
        output_rows = gather_rows(output_weight, qkv_rows)
        weight_output = gather_weight(output_rows, weight_near(output_rows))
    else:
        weight_output = gather_stacked(output_chips, qkv_rows)

    normed, queries, pairs_local = call(
        lambda *refs: project_kernel(weight_qkv, refs),
        [((rows, width), bf16), ((H * rows, HD), bf16), ((rows, 2 * k_width), bf16)],
        [hidden, gain_one, bias_qkv, cosine, sine],
        weight_args(weight_qkv),
        weight_scratch(weight_qkv, (width, q_width + 2 * k_width)),
    )
    pairs = gather_small(pairs_local)
    blocks = len(pairs)
    length = blocks * rows
    query_places = own_places.reshape(rows, 1)
    pair_scratch = [
        pltpu.VMEM((length, 2 * k_width), bf16),
        pltpu.SemaphoreType.DMA((2 * blocks,)),
    ]
    mixed_low, log_sums = call(
        lambda *refs: attend_kernel(blocks, refs),
        [((rows, q_width), bf16), ((H * rows, 1), f32)],
        [queries, key_places, query_places],
        pairs,
        pair_scratch,
    )
    arrived = pairs[1 : blocks // 2]
    gate_near = gather_near(after(gate_own, *arrived)) if near else ()
    up_near = gather_near(after(up_own, *gate_near)) if near else ()
    middle, normed_two = call(
        lambda *refs: output_kernel(weight_output, refs),
        [((rows, width), f32), ((rows, width), bf16)],
        [mixed_low, hidden, gain_two],
        weight_args(weight_output),
        weight_scratch(weight_output, (q_width, width)),
    )
    normed_two = after(normed_two, *gate_near)


    normed_all = lax.all_gather(normed_two, TP_AXES, axis=0, tiled=True)
    if near:
        down_rows = join(down_pieces)
    else:
        down_rows = gather_group(down_weight)
    active_delta = low(matmul_nt(cotangent_all, down_rows))
    if near:
        active, unit_deltas, normed_two_part = forward_back(
            normed_all,
            active_delta,
            gather_far(gate_own, gate_near) + gather_far(up_own, up_near),
        )
    else:
        gate_rows, up_rows = gather_group(gate_own), gather_group(up_own)
        gate = matmul_nt(normed_all, gate_rows)
        upward = matmul_nt(normed_all, up_rows)
        delta = active_delta.astype(f32)
        sigmoid = 1.0 / (1.0 + jnp.exp(-gate))
        silu = gate * sigmoid
        active = low(silu * upward)
        gate_delta = low(delta * upward * (sigmoid * (1.0 + gate * (1.0 - sigmoid))))
        up_delta = low(delta * silu)
        normed_two_part = low(matmul(gate_delta, gate_rows) + matmul(up_delta, up_rows))
    normed_two_delta = lax.psum_scatter(
        normed_two_part, TP_AXES, scatter_dimension=0, tiled=True
    )
    mixed_columns = columns(after(mixed_low, normed_two_part))
    unit_rows = down_weight.shape[0]
    if near:
        down_parts = outer(active, cotangent_all, unit_rows)
        down_to = scatter_far(down_parts)
        both_parts = outer(after(unit_deltas, down_parts[0]), normed_all, unit_rows)
        both_to = scatter_far(both_parts)
        active = after(active[0], down_parts[0])
    out_part = matmul(active, down_rows)
    if near:
        normed_two_delta = after(normed_two_delta, both_parts[0], out_part, *down_to)
    out_sum = lax.psum_scatter(low(out_part), TP_AXES, scatter_dimension=0, tiled=True)

    middle_delta, attention_low, mixed_delta, second_gain_part = call(
        lambda *refs: middle_kernel(weight_output, refs),
        [
            ((rows, width), f32),
            ((rows, width), bf16),
            ((H * rows, HD), bf16),
            ((1, width), f32),
        ],
        [normed_two_delta, middle, cotangent, gain_two],
        weight_args(weight_output),
        weight_scratch(weight_output, (q_width, width)),
    )
    deltas, query_bias_part, pair_mine, pair_other = call(
        lambda *refs: attend_back_kernel(blocks, refs),
        [
            ((rows, width + q_width), bf16),
            ((1, q_width), f32),
            ((length // 2, 2 * k_width), f32),
            ((length // 2, 2 * k_width), bf16),
        ],
        [
            queries,
            mixed_delta,
            log_sums,
            key_places,
            query_places,
            cosine,
            -sine,
            attention_low,
        ],
        pairs,
        pair_scratch,
    )
    if near:
        down_from = exchange(down_to[0], 1), exchange(down_to[1], 2)
        pair_mine = after(pair_mine, *both_to, *down_from)
    cuts = call(
        lambda *refs: pair_split_kernel(refs),
        [((rows, 2 * k_width), f32)] + [((rows, 2 * k_width), bf16)] * (blocks // 2 - 1),
        [pair_mine, other_core(pair_other)],
    )
    pair_delta, pair_bias_part = call(
        lambda *refs: pair_sum_kernel(blocks // 2 - 1, refs),
        [((rows, 2 * k_width), bf16), ((1, 2 * k_width), f32)],
        [cuts[0]] + [exchange(cut, i) for i, cut in enumerate(cuts[1:], 1)] + [cosine, -sine],
    )
    small_plane = sum_over(
        jnp.concatenate([second_gain_part, query_bias_part, pair_bias_part], axis=1), "grp"
    )
    delta_pieces, pair_pieces = gather_plane(deltas, pair_delta), gather_chips(pair_delta)
    grad_part = weight_grad(mixed_columns, unit_columns, width, delta_pieces, pair_pieces)
    order = ("core", "fsdp") if output_weight.shape[0] % 16 else TP_AXES
    grads = lax.psum_scatter(grad_part, order, scatter_dimension=0, tiled=True).astype(f32)
    output_grad, unit_grad = grads[:, :width], grads[:, width:]
    (input_delta,) = call(
        lambda *refs: finish_kernel(weight_qkv, refs),
        [((rows, width), f32)],
        [deltas, pair_delta, hidden, middle_delta, gain_one],
        weight_args(weight_qkv),
        weight_scratch(weight_qkv, (width, q_width + 2 * k_width)),
    )
    first_gain_grad = jnp.sum(unit_grad * projections.astype(f32), axis=1)
    scaled_grad = unit_grad * first_gain.astype(f32)[:, None]

    if near:
        both_to = after(both_to, *delta_pieces, *pair_pieces, small_plane)
        both_from = exchange(both_to[0], 1), exchange(both_to[1], 2)
        down_grad = scatter_near(down_parts[0], *down_from, scaled_grad)[0]
        both_grads = scatter_near(both_parts[0], *both_from, (scaled_grad, first_gain_grad))
        gate_grad, up_grad = both_grads[0].T, both_grads[1].T
    else:
        down_grad = scatter_group(inner(active, cotangent_all), unit_rows)
        gate_grad = scatter_group(inner(gate_delta, normed_all), unit_rows).T
        up_grad = scatter_group(inner(up_delta, normed_all), unit_rows).T
    layer_out = low(middle + after(out_sum, pair_delta).astype(f32))

    small_sum = sum_over(small_plane, "core", "fsdp")[0]

    def own_part(start, size):
        return lax.dynamic_slice_in_dim(small_sum, start + device_here * size, size)

    return (
        layer_out,
        input_delta,
        first_gain_grad,
        scaled_grad[:, :q_width],
        scaled_grad[:, q_width : q_width + k_width],
        scaled_grad[:, q_width + k_width :],
        own_part(width, own),
        own_part(width + q_width, kv_own),
        own_part(width + q_width + k_width, kv_own),
        output_grad,
        own_part(0, own),
        gate_grad,
        up_grad,
        down_grad,
    )


def solution(mesh):
    cores = 2
    ctx, fsdp = mesh.shape["ctx"], mesh.shape["fsdp"]
    split = Mesh(mesh.devices.reshape(ctx // cores, cores, fsdp), EVERY)
    tokens = P(("fsdp", "grp", "core"), None)
    in_specs = (
        tokens,
        P("fsdp"),
        P(EVERY),
        P(EVERY, None),
        P(EVERY, None),
        P(EVERY, None),
        P(EVERY),
        P(EVERY),
        P(EVERY),
        P(EVERY, None),
        P(EVERY),
        P(None, EVERY),
        P(None, EVERY),
        P(EVERY, None),
        tokens,
    )
    out_specs = (
        tokens,
        tokens,
        P(EVERY),
        P(EVERY, None),
        P(EVERY, None),
        P(EVERY, None),
        P(EVERY),
        P(EVERY),
        P(EVERY),
        P(EVERY, None),
        P(EVERY),
        P(None, EVERY),
        P(None, EVERY),
        P(EVERY, None),
    )
    return jax.shard_map(local, mesh=split, in_specs=in_specs, out_specs=out_specs, check_vma=False)
```

```python
import jax
import jax.numpy as jnp
from jax import lax
from jax.experimental import pallas as pl
from jax.experimental.pallas import tpu as pltpu
from jax.sharding import Mesh
from jax.sharding import PartitionSpec as P

H = 12
KV = 2
HD = 128

epsilon = 1e-06
rope_base = 1000000.0
neg_large = -1e30

bf16 = jnp.bfloat16
f32 = jnp.float32
VMEM_BYTES = 56 * 2**20

EVERY = ("grp", "core", "fsdp")
SEQ_AXES = ("grp", "core")
TP_AXES = ("fsdp", "core")


def rms_scale(values):
    return lax.rsqrt(jnp.mean(values * values, axis=-1, keepdims=True) + epsilon)


def rope_tables(places):
    half_width = HD // 2
    frequency = rope_base ** (-2.0 * jnp.arange(half_width, dtype=jnp.float32) / HD)
    angles = places.astype(jnp.float32)[:, None] * frequency[None, :]
    cosine, sine = jnp.cos(angles), jnp.sin(angles)
    return jnp.concatenate([cosine, cosine], axis=1), jnp.concatenate([-sine, sine], axis=1)


def matmul(left, right):
    return jnp.dot(left, right, preferred_element_type=jnp.float32)


def matmul_nt(left, right):
    return lax.dot_general(
        left, right, (((1,), (1,)), ((), ())), preferred_element_type=jnp.float32
    )


def inner(left, right):
    return lax.dot_general(
        left, right, (((0,), (0,)), ((), ())), preferred_element_type=jnp.float32
    )


def low(values):
    return values.astype(jnp.bfloat16)


def after(values, *others):
    return lax.optimization_barrier((values, others))[0]


def exchange(values, bit):
    count = lax.axis_size("grp")
    return lax.ppermute(values, "grp", [(i, i ^ bit) for i in range(count)])


def other_core(values):
    return lax.ppermute(values, "core", [(0, 1), (1, 0)])


def gather_group(block):
    count = lax.axis_size("grp")
    if count != 4:
        bit = 1
        while bit < count:
            block = jnp.concatenate([block, exchange(block, bit)], axis=0)
            bit *= 2
        return block
    half = block.shape[1] // 2
    from_x = exchange(block, 1)
    from_y = exchange(block, 2)
    left = exchange(from_x[:, :half], 2)
    right = exchange(from_y[:, half:], 1)
    corner = jnp.concatenate([left, right], axis=1)
    return jnp.concatenate([block, from_x, from_y, corner], axis=0)


def gather_near(block):
    return exchange(block, 1), exchange(block, 2)


def gather_far(block, near, *before):
    from_x, from_y = near
    half = block.shape[-1] // 2
    left = exchange(after(from_x, *before)[..., :half], 2)
    right = exchange(after(from_y, *before)[..., half:], 1)
    return block, from_x, from_y, left, right


def join(pieces):
    rows, width = pieces[0].shape
    spare = jnp.zeros((-rows % 16, width), bf16)
    corner = jnp.concatenate(pieces[3:], axis=1)
    slots = []
    for piece in (*pieces[:3], corner):
        slots += [piece, spare]
    return jnp.concatenate(slots, axis=0)


def scatter_group(parts, rows, *before):
    count = lax.axis_size("grp")
    slot = parts.shape[0] // count
    if count != 4:
        bit = count // 2
        parts = parts.astype(jnp.float32)
        while bit:
            keep, give = parts[: bit * rows], parts[bit * rows :]
            parts = keep + exchange(low(give), bit).astype(jnp.float32)
            bit //= 2
        return after(parts, *before)
    half = parts.shape[1] // 2
    own, for_x, for_y, corner = (
        parts[i * slot : i * slot + rows].astype(jnp.float32) for i in range(4)
    )
    corner = low(corner)
    from_x = exchange(corner[:, :half], 1).astype(jnp.float32)
    from_y = exchange(corner[:, half:], 2).astype(jnp.float32)
    for_y = jnp.concatenate([for_y[:, :half] + from_x, for_y[:, half:]], axis=1)
    for_x = jnp.concatenate([for_x[:, :half], for_x[:, half:] + from_y], axis=1)
    from_x = exchange(after(low(for_x), *before), 1).astype(jnp.float32)
    from_y = exchange(after(low(for_y), *before), 2).astype(jnp.float32)
    return own + from_x + from_y


def gather_chips(block):
    return [block] + [exchange(block, step) for step in range(1, lax.axis_size("grp"))]


def gather_small(block):
    mine = gather_chips(block)
    return mine + [other_core(piece) for piece in mine]


def plane_spots(pieces):
    if len(pieces) > lax.axis_size("grp"):
        return (0, 0), (1, 0), (2, 0), (3, 0), (3, pieces[3].shape[1])
    return tuple((i, 0) for i in range(len(pieces)))


def gather_plane(block, *before):
    part = block.shape[1] // 2
    if lax.axis_size("grp") != 4 or part < 512:
        return gather_chips(block)
    from_x, from_y = gather_near(block)
    left = exchange(after(from_x, *before)[:, :part], 2)
    right = exchange(after(from_y, *before)[:, part:], 1)
    return [block, from_x, from_y, left, right]


def gather_rows(block, *before):
    return lax.all_gather(after(block, *before), ("core", "fsdp"), axis=0, tiled=True)


def weight_near(rows):
    half = rows.shape[1] // 2
    own = lax.dynamic_slice_in_dim(rows, lax.axis_index("core") * half, half, 1)
    return (own, *gather_near(own)) if lax.axis_size("grp") == 4 else (own,)


def gather_weight(rows, near, before=(), late=()):
    count = lax.axis_size("grp")
    height, half = rows.shape[0], rows.shape[1] // 2
    if count == 4:
        part = half // 2
        own, from_x, from_y = near
        left = exchange(after(from_x, *before)[:, :part], 2)
        right = exchange(after(from_y, *before)[:, part:], 1)
        spots = ((1, 0), (2, 0), (3, 0), (3, part))
        mine = (from_x, from_y, left, right)
        other = tuple(other_core(piece) for piece in mine[:2])
        other += tuple(other_core(after(piece, *late)) for piece in mine[2:])
        return spots, rows, mine, other
    else:
        blocks = gather_group(near[0])
        spots = tuple((i, 0) for i in range(1, count))
        mine = tuple(blocks[i * height : (i + 1) * height] for i in range(1, count))
    return spots, rows, mine, tuple(other_core(piece) for piece in mine)


def gather_stacked(pieces, *before):
    stack = after(jnp.stack(pieces), *before)
    return (), lax.all_gather(stack, ("core", "fsdp"), axis=0, tiled=False), (), ()


def assemble(spots, own_ref, mine_refs, other_refs, full_ref, sems):
    grp, core = lax.axis_index("grp"), lax.axis_index("core")
    if len(own_ref.shape) == 4:
        count = own_ref.shape[1]
        copies = [
            pltpu.make_async_copy(own_ref.at[:, i], full_ref.at[grp ^ i], sems.at[i])
            for i in range(count)
        ]
        for copy in copies:
            copy.start()
        return copies
    height, half = own_ref.shape[0], full_ref.shape[1] // 2

    def rows_of(step):
        return pl.ds(pl.multiple_of((grp ^ step) * height, height), height)

    copies = [pltpu.make_async_copy(own_ref, full_ref.at[rows_of(0), :], sems.at[0])]
    for place, (step, offset) in enumerate(spots):
        for side, refs in ((core, mine_refs), (1 - core, other_refs)):
            width = refs[place].shape[1]
            start = pl.multiple_of(side * half + offset, 128)
            copies.append(
                pltpu.make_async_copy(
                    refs[place],
                    full_ref.at[rows_of(step), pl.ds(start, width)],
                    sems.at[len(copies)],
                )
            )
    for copy in copies:
        copy.start()
    return copies


def call(kernel, outs, ins, anys=(), scratch=()):
    whole = pl.BlockSpec(memory_space=pltpu.VMEM)
    left = pl.BlockSpec(memory_space=pl.ANY)
    return pl.pallas_call(
        kernel,
        out_shape=[jax.ShapeDtypeStruct(shape, dtype) for shape, dtype in outs],
        in_specs=[whole] * len(ins) + [left] * len(anys),
        out_specs=[whole] * len(outs),
        scratch_shapes=list(scratch),
        compiler_params=pltpu.CompilerParams(vmem_limit_bytes=VMEM_BYTES),
    )(*ins, *anys)


def weight_scratch(gathered, shape):
    spots, own, mine, other = gathered
    if len(own.shape) == 4:
        parts, count, rows, width = own.shape
        return [
            pltpu.VMEM((count, parts, rows, width), bf16),
            pltpu.SemaphoreType.DMA((count,)),
        ]
    return [
        pltpu.VMEM(shape, bf16),
        pltpu.SemaphoreType.DMA((1 + 2 * len(mine),)),
    ]


def weight_args(gathered):
    spots, own, mine, other = gathered
    return [own, *mine, *other]


def weight_refs(gathered, refs):
    count = len(gathered[2])
    return gathered[0], refs[0], refs[1 : 1 + count], refs[1 + count : 1 + 2 * count]


def rope(values, cosine, sine):
    return values * cosine + pltpu.roll(values, HD // 2, 1) * sine


def half_span(run, rows):
    return slice(run * rows // 2, (run + 1) * rows // 2)


def run_span(run, head, heads, rows):
    start = (run * H + head) * (rows // 2)
    return slice(start, start + heads * (rows // 2))


def project_kernel(gathered, refs):
    hidden, gain, bias, cosine, sine = refs[:5]
    count = 1 + 2 * len(gathered[2])
    pieces = refs[5 : 5 + count]
    normed, queries, pairs, weight, sems = refs[5 + count :]
    copies = assemble(*weight_refs(gathered, pieces), weight, sems)
    inputs = hidden[...].astype(f32)
    normed[...] = low(inputs * rms_scale(inputs) * gain[...])
    for copy in copies:
        copy.wait()
    rows = hidden.shape[0]
    half = weight.shape[1] // 2
    heads_half = half // HD
    for side in range(2):
        lin = (
            matmul(normed[...], weight[:, side * half : (side + 1) * half])
            + bias[:, side * half : (side + 1) * half]
        )
        for spot in range(heads_half):
            head = side * heads_half + spot
            part = lin[:, spot * HD : (spot + 1) * HD]
            if head < H + KV:
                part = rope(part, cosine[...], sine[...])
            if head < H:
                for run in range(2):
                    queries[run_span(run, head, 1, rows), :] = low(part)[half_span(run, rows)]
            else:
                pairs[:, (head - H) * HD : (head - H + 1) * HD] = low(part)


def fetch_pairs(refs, full_ref, sems):
    half = refs[0].shape[0] // 2
    copies = []
    for run in range(2):
        for i, ref in enumerate(refs):
            place = run * len(refs) + i
            copies.append(
                pltpu.make_async_copy(
                    ref.at[pl.ds(run * half, half), :],
                    full_ref.at[pl.ds(place * half, half), :],
                    sems.at[place],
                )
            )
    for copy in copies:
        copy.start()
    return copies


def allowed_keys(run, key_places, own_places):
    extent = key_places.shape[1] // 2 * (run + 1)
    own = own_places[half_span(run, own_places.shape[0]), :]
    own = jnp.concatenate([own] * (H // KV), axis=0)
    return extent, key_places[:, :extent] <= own


def attend_kernel(blocks, refs):
    queries, key_places, own_places = refs[:3]
    pair_refs = refs[3 : 3 + blocks]
    mixed, log_sums, pairs, pair_sems = refs[3 + blocks :]
    for copy in fetch_pairs(pair_refs, pairs, pair_sems):
        copy.wait()
    rows = own_places.shape[0]
    half = rows // 2
    scale = HD ** (-0.5)
    group_size = H // KV
    for run in range(2):
        extent, allowed = allowed_keys(run, key_places, own_places)
        for group in range(KV):
            keys = pairs[:extent, group * HD : (group + 1) * HD]
            values = pairs[:extent, (KV + group) * HD : (KV + group + 1) * HD]
            span = run_span(run, group * group_size, group_size, rows)
            scores = jnp.where(allowed, matmul_nt(queries[span, :], keys) * scale, neg_large)
            top = jnp.max(scores, axis=1, keepdims=True)
            terms = jnp.exp(scores - top)
            total = jnp.sum(terms, axis=1, keepdims=True)
            log_sums[span, :] = top + jnp.log(total)
            result = low(matmul(low(terms * (1.0 / total)), values))
            for spot in range(group_size):
                head = group * group_size + spot
                mixed[half_span(run, rows), head * HD : (head + 1) * HD] = result[
                    spot * half : (spot + 1) * half
                ]


def output_kernel(gathered, refs):
    mixed, hidden, gain = refs[:3]
    count = 1 + 2 * len(gathered[2])
    pieces = refs[3 : 3 + count]
    middle, normed_two, weight, sems = refs[3 + count :]
    for copy in assemble(*weight_refs(gathered, pieces), weight, sems):
        copy.wait()
    full = weight[...].reshape(mixed.shape[1], -1)
    result = hidden[...].astype(f32) + matmul(mixed[...], full)
    middle[...] = result
    normed_two[...] = low(result * rms_scale(result) * gain[...])


def norm_back(delta, values, gain):
    scale = rms_scale(values)
    unit = values * scale
    scaled = delta * gain
    return scale * (scaled - unit * jnp.mean(scaled * unit, axis=-1, keepdims=True)), unit


def middle_kernel(gathered, refs):
    normed_delta, middle, cotangent, gain = refs[:4]
    count = 1 + 2 * len(gathered[2])
    pieces = refs[4 : 4 + count]
    middle_delta, attention_low, mixed_delta, gain_part, weight, sems = refs[4 + count :]
    copies = assemble(*weight_refs(gathered, pieces), weight, sems)
    delta = normed_delta[...].astype(f32)
    term, unit = norm_back(delta, middle[...], gain[...])
    gain_part[...] = jnp.sum(delta * unit, axis=0, keepdims=True)
    result = cotangent[...].astype(f32) + term
    middle_delta[...] = result
    attention_low[...] = low(result)
    for copy in copies:
        copy.wait()
    rows = middle.shape[0]
    mixed = matmul_nt(low(result), weight[...].reshape(-1, result.shape[1]))
    for head in range(H):
        part = low(mixed[:, head * HD : (head + 1) * HD])
        for run in range(2):
            mixed_delta[run_span(run, head, 1, rows), :] = part[half_span(run, rows)]


def attend_back_kernel(blocks, refs):
    queries, mixed_delta, log_sums, key_places, own_places, cosine, sine, attention_low = refs[:8]
    pair_refs = refs[8 : 8 + blocks]
    deltas, bias_part, pair_mine, pair_other, pairs, pair_sems = refs[8 + blocks :]
    split = attention_low.shape[1]
    deltas[:, :split] = attention_low[...]
    for copy in fetch_pairs(pair_refs, pairs, pair_sems):
        copy.wait()
    rows = own_places.shape[0]
    half = rows // 2
    scale = HD ** (-0.5)
    group_size = H // KV
    for group in range(KV):
        key_span = slice(group * HD, (group + 1) * HD)
        value_span = slice((KV + group) * HD, (KV + group + 1) * HD)
        sums = []
        for run in range(2):
            extent, allowed = allowed_keys(run, key_places, own_places)
            keys, values = pairs[:extent, key_span], pairs[:extent, value_span]
            span = run_span(run, group * group_size, group_size, rows)
            query, mixed = queries[span, :], mixed_delta[span, :]
            scores = matmul_nt(query, keys) * scale
            probs = jnp.where(allowed, jnp.exp(scores - log_sums[span, :]), 0.0)
            prob_delta = matmul_nt(mixed, values)
            dots = jnp.sum(probs * prob_delta, axis=1, keepdims=True)
            score_delta = low(probs * (prob_delta - dots))
            turn = matmul(score_delta, keys) * scale
            here = half_span(run, rows)
            for spot in range(group_size):
                head = group * group_size + spot
                head_span = slice(head * HD, (head + 1) * HD)
                part = turn[spot * half : (spot + 1) * half]
                part = low(rope(part, cosine[here, :], sine[here, :]))
                deltas[here, split + head * HD : split + (head + 1) * HD] = part
                bias = jnp.sum(part.astype(f32), axis=0, keepdims=True)
                bias_part[:, head_span] = bias if run == 0 else bias_part[:, head_span] + bias
            sums.append((inner(score_delta, query) * scale, inner(low(probs), mixed)))
        early = sums[1][0].shape[0] // 2
        for which, to in enumerate((key_span, value_span)):
            first = sums[0][which] + sums[1][which][:early]
            for run, part in enumerate((first, sums[1][which][early:])):
                for block in range(blocks):
                    piece = part[block * half : (block + 1) * half]
                    start = block % (blocks // 2) * rows + run * half
                    if block < blocks // 2:
                        pair_mine[start : start + half, to] = piece
                    else:
                        pair_other[start : start + half, to] = low(piece)


def pair_split_kernel(refs):
    mine, received, own = refs[:3]
    rows = own.shape[0]
    own[...] = mine[:rows] + received[:rows].astype(f32)
    for place, part in enumerate(refs[3:], 1):
        span = slice(place * rows, (place + 1) * rows)
        part[...] = low(mine[span] + received[span].astype(f32))


def pair_sum_kernel(parts, refs):
    own = refs[0]
    cosine, sine, pair_delta, bias_part = refs[1 + parts :]
    total = own[...]
    for part in refs[1 : 1 + parts]:
        total = total + part[...].astype(f32)
    for spot in range(2 * KV):
        span = slice(spot * HD, (spot + 1) * HD)
        part = total[:, span]
        if spot < KV:
            part = rope(part, cosine[...], sine[...])
        part = low(part)
        pair_delta[:, span] = part
        bias_part[:, span] = jnp.sum(part.astype(f32), axis=0, keepdims=True)


def weight_grad_kernel(places, split, refs):
    mixed, unit = refs[:2]
    pieces = refs[2 : 2 + len(places)]
    result, deltas, sems = refs[2 + len(places) :]
    grp = lax.axis_index("grp")
    copies = []
    for place, piece in enumerate(pieces):
        step, start = places[place]
        rows, width = piece.shape
        row = pl.multiple_of((grp ^ step) * rows, rows)
        copies.append(
            pltpu.make_async_copy(
                piece, deltas.at[pl.ds(row, rows), pl.ds(start, width)], sems.at[place]
            )
        )
    for copy in copies:
        copy.start()
    for copy in copies:
        copy.wait()
    parts = low(inner(mixed[...], deltas[:, :split])), low(inner(unit[...], deltas[:, split:]))
    cores, devices = 2, lax.axis_size("fsdp")
    rows = result.shape[0] // (cores * devices)
    if rows % 16:
        result[:, :split], result[:, split:] = parts
        return
    for device in range(devices):
        for core in range(cores):
            here = (device * cores + core) * rows
            there = (core * devices + device) * rows
            for part, span in zip(parts, (slice(0, split), slice(split, None))):
                result[here : here + rows, span] = part[there : there + rows]


def weight_grad(mixed, unit, split, *gathered):
    places, pieces, start = [], [], 0
    for group in gathered:
        places += [(step, start + offset) for step, offset in plane_spots(group)]
        pieces += group
        start += group[0].shape[1]
    (part,) = call(
        lambda *refs: weight_grad_kernel(places, split, refs),
        [((unit.shape[1], start), bf16)],
        [mixed, unit],
        pieces,
        [pltpu.VMEM((unit.shape[0], start), bf16), pltpu.SemaphoreType.DMA((len(pieces),))],
    )
    return part


def forward_back_kernel(count, refs):
    normed, active_delta = refs[:2]
    pieces = refs[2 : 2 + 2 * (count + 1)]
    active, deltas, normed_delta, weights, sems = refs[2 + 2 * (count + 1) :]
    rows, width = pieces[0].shape
    slot = weights.shape[1] // count

    @pl.when(pl.program_id(0) == 0)
    def fetch():
        copies = []
        for which in range(2):
            for place in range(count + 1):
                piece = pieces[which * (count + 1) + place]
                step = min(place, count - 1)
                start = width // 2 if place == count else 0
                copies.append(
                    pltpu.make_async_copy(
                        piece,
                        weights.at[which, pl.ds(step * slot, rows), pl.ds(start, piece.shape[1])],
                        sems.at[len(copies)],
                    )
                )
        for copy in copies:
            copy.start()
        for copy in copies:
            copy.wait()
        if slot > rows:
            for which in range(2):
                for step in range(count):
                    spare = slice(step * slot + rows, (step + 1) * slot)
                    weights[which, spare, :] = jnp.zeros((slot - rows, width), bf16)

    gate = matmul_nt(normed[...], weights[0])
    upward = matmul_nt(normed[...], weights[1])
    delta = active_delta[...].astype(f32)
    sigmoid = 1.0 / (1.0 + jnp.exp(-gate))
    silu = gate * sigmoid
    active[0] = low(silu * upward)
    gate_low = low(delta * upward * (sigmoid * (1.0 + gate * (1.0 - sigmoid))))
    up_low = low(delta * silu)
    deltas[0] = gate_low
    deltas[1] = up_low
    normed_delta[...] = low(matmul(gate_low, weights[0]) + matmul(up_low, weights[1]))


def forward_back(normed_all, active_delta, pieces):
    tokens, width = normed_all.shape
    units = active_delta.shape[1]
    tile = 256

    def tiles(columns):
        return pl.BlockSpec((tile, columns), lambda i: (i, 0))

    count = len(pieces) // 2 - 1
    return pl.pallas_call(
        lambda *refs: forward_back_kernel(count, refs),
        grid=(tokens // tile,),
        out_shape=[
            jax.ShapeDtypeStruct((1, tokens, units), bf16),
            jax.ShapeDtypeStruct((2, tokens, units), bf16),
            jax.ShapeDtypeStruct((tokens, width), bf16),
        ],
        in_specs=[tiles(width), tiles(units)] + [pl.BlockSpec(memory_space=pl.ANY)] * len(pieces),
        out_specs=[
            pl.BlockSpec((1, tile, units), lambda i: (0, i, 0)),
            pl.BlockSpec((2, tile, units), lambda i: (0, i, 0)),
            tiles(width),
        ],
        scratch_shapes=[
            pltpu.VMEM((2, units, width), bf16),
            pltpu.SemaphoreType.DMA((len(pieces),)),
        ],
        compiler_params=pltpu.CompilerParams(vmem_limit_bytes=VMEM_BYTES),
    )(normed_all, active_delta, *pieces)


def outer_kernel(refs):
    left, right, own, for_x, for_y, far_left, far_right = refs
    rows = own.shape[1]
    slot = left.shape[2] // 4
    total = inner(left[0], right[...])
    for place, part in enumerate((own, for_x, for_y)):
        part[0] = low(total[place * slot : place * slot + rows])
    far = low(total[3 * slot : 3 * slot + rows])

    @pl.when(pl.program_id(1) == 0)
    def first():
        far_left[0] = far

    @pl.when(pl.program_id(1) == 1)
    def second():
        far_right[0] = far


def outer(left, right, rows):
    stack, tokens, units = left.shape
    half = right.shape[1] // 2
    wide = jax.ShapeDtypeStruct((stack, rows, 2 * half), bf16)
    narrow = jax.ShapeDtypeStruct((stack, rows, half), bf16)
    by_half = pl.BlockSpec((1, rows, half), lambda i, j: (i, 0, j))
    whole = pl.BlockSpec((1, rows, half), lambda i, j: (i, 0, 0))
    return pl.pallas_call(
        lambda *refs: outer_kernel(refs),
        grid=(stack, 2),
        out_shape=[wide, wide, wide, narrow, narrow],
        in_specs=[
            pl.BlockSpec((1, tokens, units), lambda i, j: (i, 0, 0)),
            pl.BlockSpec((tokens, half), lambda i, j: (0, j)),
        ],
        out_specs=[by_half, by_half, by_half, whole, whole],
        compiler_params=pltpu.CompilerParams(vmem_limit_bytes=VMEM_BYTES),
    )(left, right)


def scatter_far(parts):
    own, for_x, for_y, far_left, far_right = parts
    from_x = exchange(far_left, 1)
    from_y = exchange(far_right, 2)
    spare = jnp.zeros_like(from_x)
    to_y = low(for_y.astype(f32) + jnp.concatenate([from_x, spare], axis=2).astype(f32))
    to_x = low(for_x.astype(f32) + jnp.concatenate([spare, from_y], axis=2).astype(f32))
    return to_x, to_y


def scatter_near(own, from_x, from_y, late):
    from_x, from_y = after((from_x, from_y), late)
    return own.astype(f32) + from_x.astype(f32) + from_y.astype(f32)


def turn_kernel(refs):
    own, from_x, from_y = refs[:3]
    for place, out in enumerate(refs[3:]):
        total = own[place].astype(f32) + from_x[place].astype(f32) + from_y[place].astype(f32)
        out[...] = total.T


def turned_sums(own, from_x, from_y, late):
    from_x, from_y = after((from_x, from_y), late)
    stack, rows, width = own.shape
    tile = width // 3 if width % 384 == 0 else width
    return pl.pallas_call(
        lambda *refs: turn_kernel(refs),
        grid=(width // tile,),
        out_shape=[jax.ShapeDtypeStruct((width, rows), f32)] * stack,
        in_specs=[pl.BlockSpec((stack, rows, tile), lambda i: (0, 0, i))] * 3,
        out_specs=[pl.BlockSpec((tile, rows), lambda i: (i, 0))] * stack,
        compiler_params=pltpu.CompilerParams(vmem_limit_bytes=VMEM_BYTES),
    )(own, from_x, from_y)


def finish_kernel(gathered, refs):
    deltas, pair_delta, hidden, middle_delta, gain = refs[:5]
    count = 1 + 2 * len(gathered[2])
    pieces = refs[5 : 5 + count]
    input_delta, weight, sems = refs[5 + count :]
    copies = assemble(*weight_refs(gathered, pieces), weight, sems)
    for copy in copies:
        copy.wait()
    split = weight.shape[1] - pair_delta.shape[1]
    delta = matmul_nt(deltas[:, -split:], weight[:, :split]) + matmul_nt(
        pair_delta[...], weight[:, split:]
    )
    term, unit = norm_back(delta, hidden[...].astype(f32), gain[...])
    input_delta[...] = middle_delta[...] + term


def sum_over(values, *axes):
    for axis in axes:
        count = lax.axis_size(axis)
        bit = 1
        while bit < count:
            values = values + lax.ppermute(values, axis, [(i, i ^ bit) for i in range(count)])
            bit *= 2
    return values


def local(
    hidden,
    positions,
    first_gain,
    query_weight,
    key_weight,
    value_weight,
    query_bias,
    key_bias,
    value_bias,
    output_weight,
    second_gain,
    gate_weight,
    up_weight,
    down_weight,
    cotangent,
):
    rows = hidden.shape[0]
    width = hidden.shape[1]
    ctx_here = lax.axis_index("grp") * lax.axis_size("core") + lax.axis_index("core")
    own_places = lax.dynamic_slice_in_dim(positions, ctx_here * rows, rows)
    q_width, k_width = H * HD, KV * HD

    near = lax.axis_size("grp") == 4 and gate_weight.shape[1] % 8 == 0
    projections = jnp.concatenate([query_weight, key_weight, value_weight], axis=1)
    qkv_rows = gather_rows(projections)

    def columns(values):
        return lax.all_to_all(values, "grp", split_axis=1, concat_axis=0, tiled=True)

    inputs = hidden.astype(f32)
    unit = low(inputs * rms_scale(inputs))
    gate_own, up_own = gate_weight.T, up_weight.T
    small = jnp.concatenate([first_gain, second_gain, query_bias, key_bias, value_bias])
    devices = lax.axis_size(EVERY)
    device_here = lax.axis_index(EVERY)
    small_plane = sum_over(
        lax.dynamic_update_slice_in_dim(
            jnp.zeros((devices, small.shape[0]), jnp.float32),
            small.astype(jnp.float32)[None],
            device_here,
            0,
        ),
        "grp",
    )
    output_chips = gather_chips(output_weight)
    small_all = sum_over(small_plane, "core", "fsdp")
    down_near = gather_near(after(down_weight, small_plane, *output_chips[1:])) if near else ()
    down_pieces = gather_far(down_weight, down_near, small_all) if near else ()
    qkv_rows = after(qkv_rows, small_all, *down_near)
    qkv_near = weight_near(qkv_rows)
    own = width // devices
    kv_own = k_width // devices
    gain_one = small_all[:, :own].reshape(1, width)
    gain_two = small_all[:, own : 2 * own].reshape(1, width)
    bias_qkv = jnp.concatenate(
        [
            small_all[:, 2 * own : 3 * own].reshape(q_width),
            small_all[:, 3 * own : 3 * own + kv_own].reshape(k_width),
            small_all[:, 3 * own + kv_own :].reshape(k_width),
        ]
    ).reshape(1, -1)
    cotangent_all = lax.all_gather(cotangent, TP_AXES, axis=0, tiled=True)

    cosine, sine = rope_tables(own_places)
    places = positions.reshape(-1, rows)
    steps = jnp.arange(places.shape[0], dtype=jnp.int32)
    from_ctx = ctx_here ^ jnp.concatenate([steps[0::2], steps[1::2]])
    matches = from_ctx[:, None] == steps[None, :]
    key_places = jnp.sum(jnp.where(matches[:, :, None], places[None], 0), axis=1)
    key_places = key_places.reshape(-1, 2, rows // 2).transpose(1, 0, 2).reshape(1, -1)
    unit_columns = columns(after(unit, qkv_near[0]))
    ready = (unit_columns, gain_one, gain_two, bias_qkv, cosine, sine, key_places)
    weight_qkv = gather_weight(qkv_rows, qkv_near, ready)
    if output_weight.shape[0] % 16:
        output_rows = gather_rows(output_weight, qkv_rows)
        weight_output = gather_weight(output_rows, weight_near(output_rows))
    else:
        weight_output = gather_stacked(output_chips, qkv_rows)

    normed, queries, pairs_local = call(
        lambda *refs: project_kernel(weight_qkv, refs),
        [((rows, width), bf16), ((H * rows, HD), bf16), ((rows, 2 * k_width), bf16)],
        [hidden, gain_one, bias_qkv, cosine, sine],
        weight_args(weight_qkv),
        weight_scratch(weight_qkv, (width, q_width + 2 * k_width)),
    )
    pairs = gather_small(pairs_local)
    blocks = len(pairs)
    length = blocks * rows
    query_places = own_places.reshape(rows, 1)
    pair_scratch = [
        pltpu.VMEM((length, 2 * k_width), bf16),
        pltpu.SemaphoreType.DMA((2 * blocks,)),
    ]
    mixed_low, log_sums = call(
        lambda *refs: attend_kernel(blocks, refs),
        [((rows, q_width), bf16), ((H * rows, 1), f32)],
        [queries, key_places, query_places],
        pairs,
        pair_scratch,
    )
    arrived = pairs[1 : blocks // 2]
    gate_near = gather_near(after(gate_own, *arrived)) if near else ()
    up_near = gather_near(after(up_own, *gate_near)) if near else ()
    middle, normed_two = call(
        lambda *refs: output_kernel(weight_output, refs),
        [((rows, width), f32), ((rows, width), bf16)],
        [mixed_low, hidden, gain_two],
        weight_args(weight_output),
        weight_scratch(weight_output, (q_width, width)),
    )
    normed_two = after(normed_two, *gate_near)


    normed_all = lax.all_gather(normed_two, TP_AXES, axis=0, tiled=True)
    mixed_columns = columns(after(mixed_low, normed_two))
    normed_all = after(normed_all, mixed_columns)
    if near:
        down_rows = join(down_pieces)
    else:
        down_rows = gather_group(down_weight)
    active_delta = low(matmul_nt(cotangent_all, down_rows))
    if near:
        active, unit_deltas, normed_two_part = forward_back(
            normed_all,
            active_delta,
            gather_far(gate_own, gate_near) + gather_far(up_own, up_near),
        )
    else:
        gate_rows, up_rows = gather_group(gate_own), gather_group(up_own)
        gate = matmul_nt(normed_all, gate_rows)
        upward = matmul_nt(normed_all, up_rows)
        delta = active_delta.astype(f32)
        sigmoid = 1.0 / (1.0 + jnp.exp(-gate))
        silu = gate * sigmoid
        active = low(silu * upward)
        gate_delta = low(delta * upward * (sigmoid * (1.0 + gate * (1.0 - sigmoid))))
        up_delta = low(delta * silu)
        normed_two_part = low(matmul(gate_delta, gate_rows) + matmul(up_delta, up_rows))
    normed_two_delta = lax.psum_scatter(
        normed_two_part, TP_AXES, scatter_dimension=0, tiled=True
    )
    unit_rows = down_weight.shape[0]
    if near:
        down_parts = outer(active, cotangent_all, unit_rows)
        down_to = scatter_far(down_parts)
        both_parts = outer(after(unit_deltas, down_parts[0]), normed_all, unit_rows)
        both_to = scatter_far(both_parts)
        active = after(active[0], down_parts[0])
    out_part = matmul(active, down_rows)
    if near:
        normed_two_delta = after(normed_two_delta, both_parts[0], out_part, *down_to)
    out_sum = lax.psum_scatter(low(out_part), TP_AXES, scatter_dimension=0, tiled=True)

    middle_delta, attention_low, mixed_delta, second_gain_part = call(
        lambda *refs: middle_kernel(weight_output, refs),
        [
            ((rows, width), f32),
            ((rows, width), bf16),
            ((H * rows, HD), bf16),
            ((1, width), f32),
        ],
        [normed_two_delta, middle, cotangent, gain_two],
        weight_args(weight_output),
        weight_scratch(weight_output, (q_width, width)),
    )
    deltas, query_bias_part, pair_mine, pair_other = call(
        lambda *refs: attend_back_kernel(blocks, refs),
        [
            ((rows, width + q_width), bf16),
            ((1, q_width), f32),
            ((length // 2, 2 * k_width), f32),
            ((length // 2, 2 * k_width), bf16),
        ],
        [
            queries,
            mixed_delta,
            log_sums,
            key_places,
            query_places,
            cosine,
            -sine,
            attention_low,
        ],
        pairs,
        pair_scratch,
    )
    if near:
        pair_mine = after(pair_mine, *both_to)
    cuts = call(
        lambda *refs: pair_split_kernel(refs),
        [((rows, 2 * k_width), f32)] + [((rows, 2 * k_width), bf16)] * (blocks // 2 - 1),
        [pair_mine, other_core(pair_other)],
    )
    pair_delta, pair_bias_part = call(
        lambda *refs: pair_sum_kernel(blocks // 2 - 1, refs),
        [((rows, 2 * k_width), bf16), ((1, 2 * k_width), f32)],
        [cuts[0]] + [exchange(cut, i) for i, cut in enumerate(cuts[1:], 1)] + [cosine, -sine],
    )
    small_plane = sum_over(
        jnp.concatenate([second_gain_part, query_bias_part, pair_bias_part], axis=1), "grp"
    )
    delta_pieces, pair_pieces = gather_plane(deltas, pair_delta), gather_chips(pair_delta)
    grad_part = weight_grad(mixed_columns, unit_columns, width, delta_pieces, pair_pieces)
    order = ("core", "fsdp") if output_weight.shape[0] % 16 else TP_AXES
    grads = lax.psum_scatter(grad_part, order, scatter_dimension=0, tiled=True).astype(f32)
    output_grad, unit_grad = grads[:, :width], grads[:, width:]
    (input_delta,) = call(
        lambda *refs: finish_kernel(weight_qkv, refs),
        [((rows, width), f32)],
        [deltas, pair_delta, hidden, middle_delta, gain_one],
        weight_args(weight_qkv),
        weight_scratch(weight_qkv, (width, q_width + 2 * k_width)),
    )
    first_gain_grad = jnp.sum(unit_grad * projections.astype(f32), axis=1)
    scaled_grad = unit_grad * first_gain.astype(f32)[:, None]

    if near:
        both_to = after(both_to, *delta_pieces, *pair_pieces, small_plane)
        both_from = exchange(both_to[0], 1), exchange(both_to[1], 2)
        down_to = after(down_to, pair_delta)
        down_from = exchange(down_to[0], 1), exchange(down_to[1], 2)
        down_grad = scatter_near(down_parts[0], *down_from, scaled_grad)[0]
        gate_grad, up_grad = turned_sums(both_parts[0], *both_from, (scaled_grad, first_gain_grad))
    else:
        down_grad = scatter_group(inner(active, cotangent_all), unit_rows)
        gate_grad = scatter_group(inner(gate_delta, normed_all), unit_rows).T
        up_grad = scatter_group(inner(up_delta, normed_all), unit_rows).T
    layer_out = low(middle + after(out_sum, pair_delta).astype(f32))

    small_sum = sum_over(small_plane, "core", "fsdp")[0]

    def own_part(start, size):
        return lax.dynamic_slice_in_dim(small_sum, start + device_here * size, size)

    return (
        layer_out,
        input_delta,
        first_gain_grad,
        scaled_grad[:, :q_width],
        scaled_grad[:, q_width : q_width + k_width],
        scaled_grad[:, q_width + k_width :],
        own_part(width, own),
        own_part(width + q_width, kv_own),
        own_part(width + q_width + k_width, kv_own),
        output_grad,
        own_part(0, own),
        gate_grad,
        up_grad,
        down_grad,
    )


def solution(mesh):
    cores = 2
    ctx, fsdp = mesh.shape["ctx"], mesh.shape["fsdp"]
    split = Mesh(mesh.devices.reshape(ctx // cores, cores, fsdp), EVERY)
    tokens = P(("fsdp", "grp", "core"), None)
    in_specs = (
        tokens,
        P("fsdp"),
        P(EVERY),
        P(EVERY, None),
        P(EVERY, None),
        P(EVERY, None),
        P(EVERY),
        P(EVERY),
        P(EVERY),
        P(EVERY, None),
        P(EVERY),
        P(None, EVERY),
        P(None, EVERY),
        P(EVERY, None),
        tokens,
    )
    out_specs = (
        tokens,
        tokens,
        P(EVERY),
        P(EVERY, None),
        P(EVERY, None),
        P(EVERY, None),
        P(EVERY),
        P(EVERY),
        P(EVERY),
        P(EVERY, None),
        P(EVERY),
        P(None, EVERY),
        P(None, EVERY),
        P(EVERY, None),
    )
    return jax.shard_map(local, mesh=split, in_specs=in_specs, out_specs=out_specs, check_vma=False)
```

```python
import jax
import jax.numpy as jnp
from jax import lax
from jax.experimental import pallas as pl
from jax.experimental.pallas import tpu as pltpu
from jax.sharding import Mesh
from jax.sharding import PartitionSpec as P

H = 12
KV = 2
HD = 128

epsilon = 1e-06
rope_base = 1000000.0
neg_large = -1e30

bf16 = jnp.bfloat16
f32 = jnp.float32
VMEM_BYTES = 56 * 2**20

EVERY = ("grp", "core", "fsdp")
SEQ_AXES = ("grp", "core")
TP_AXES = ("fsdp", "core")


def rms_scale(values):
    return lax.rsqrt(jnp.mean(values * values, axis=-1, keepdims=True) + epsilon)


def rope_tables(places):
    half_width = HD // 2
    frequency = rope_base ** (-2.0 * jnp.arange(half_width, dtype=jnp.float32) / HD)
    angles = places.astype(jnp.float32)[:, None] * frequency[None, :]
    cosine, sine = jnp.cos(angles), jnp.sin(angles)
    return jnp.concatenate([cosine, cosine], axis=1), jnp.concatenate([-sine, sine], axis=1)


def matmul(left, right):
    return jnp.dot(left, right, preferred_element_type=jnp.float32)


def matmul_nt(left, right):
    return lax.dot_general(
        left, right, (((1,), (1,)), ((), ())), preferred_element_type=jnp.float32
    )


def inner(left, right):
    return lax.dot_general(
        left, right, (((0,), (0,)), ((), ())), preferred_element_type=jnp.float32
    )


def low(values):
    return values.astype(jnp.bfloat16)


def after(values, *others):
    return lax.optimization_barrier((values, others))[0]


def exchange(values, bit):
    count = lax.axis_size("grp")
    return lax.ppermute(values, "grp", [(i, i ^ bit) for i in range(count)])


def other_core(values):
    return lax.ppermute(values, "core", [(0, 1), (1, 0)])


def gather_group(block):
    count = lax.axis_size("grp")
    if count != 4:
        bit = 1
        while bit < count:
            block = jnp.concatenate([block, exchange(block, bit)], axis=0)
            bit *= 2
        return block
    half = block.shape[1] // 2
    from_x = exchange(block, 1)
    from_y = exchange(block, 2)
    left = exchange(from_x[:, :half], 2)
    right = exchange(from_y[:, half:], 1)
    corner = jnp.concatenate([left, right], axis=1)
    return jnp.concatenate([block, from_x, from_y, corner], axis=0)


def gather_near(block):
    return exchange(block, 1), exchange(block, 2)


def gather_far(block, near, *before):
    from_x, from_y = near
    half = block.shape[-1] // 2
    left = exchange(after(from_x, *before)[..., :half], 2)
    right = exchange(after(from_y, *before)[..., half:], 1)
    return block, from_x, from_y, left, right


def join(pieces):
    rows, width = pieces[0].shape
    spare = jnp.zeros((-rows % 16, width), bf16)
    corner = jnp.concatenate(pieces[3:], axis=1)
    slots = []
    for piece in (*pieces[:3], corner):
        slots += [piece, spare]
    return jnp.concatenate(slots, axis=0)


def scatter_group(parts, rows, *before):
    count = lax.axis_size("grp")
    slot = parts.shape[0] // count
    if count != 4:
        bit = count // 2
        parts = parts.astype(jnp.float32)
        while bit:
            keep, give = parts[: bit * rows], parts[bit * rows :]
            parts = keep + exchange(low(give), bit).astype(jnp.float32)
            bit //= 2
        return after(parts, *before)
    half = parts.shape[1] // 2
    own, for_x, for_y, corner = (
        parts[i * slot : i * slot + rows].astype(jnp.float32) for i in range(4)
    )
    corner = low(corner)
    from_x = exchange(corner[:, :half], 1).astype(jnp.float32)
    from_y = exchange(corner[:, half:], 2).astype(jnp.float32)
    for_y = jnp.concatenate([for_y[:, :half] + from_x, for_y[:, half:]], axis=1)
    for_x = jnp.concatenate([for_x[:, :half], for_x[:, half:] + from_y], axis=1)
    from_x = exchange(after(low(for_x), *before), 1).astype(jnp.float32)
    from_y = exchange(after(low(for_y), *before), 2).astype(jnp.float32)
    return own + from_x + from_y


def gather_chips(block):
    return [block] + [exchange(block, step) for step in range(1, lax.axis_size("grp"))]


def gather_small(block):
    mine = gather_chips(block)
    return mine + [other_core(piece) for piece in mine]


def plane_spots(pieces):
    if len(pieces) > lax.axis_size("grp"):
        return (0, 0), (1, 0), (2, 0), (3, 0), (3, pieces[3].shape[1])
    return tuple((i, 0) for i in range(len(pieces)))


def gather_plane(block, *before):
    part = block.shape[1] // 2
    if lax.axis_size("grp") != 4 or part < 512:
        return gather_chips(block)
    from_x, from_y = gather_near(block)
    left = exchange(after(from_x, *before)[:, :part], 2)
    right = exchange(after(from_y, *before)[:, part:], 1)
    return [block, from_x, from_y, left, right]


def gather_rows(block, *before):
    return lax.all_gather(after(block, *before), ("core", "fsdp"), axis=0, tiled=True)


def weight_near(rows):
    half = rows.shape[1] // 2
    own = lax.dynamic_slice_in_dim(rows, lax.axis_index("core") * half, half, 1)
    return (own, *gather_near(own)) if lax.axis_size("grp") == 4 else (own,)


def gather_weight(rows, near, before=(), late=()):
    count = lax.axis_size("grp")
    height, half = rows.shape[0], rows.shape[1] // 2
    if count == 4:
        part = half // 2
        own, from_x, from_y = near
        left = exchange(after(from_x, *before)[:, :part], 2)
        right = exchange(after(from_y, *before)[:, part:], 1)
        spots = ((1, 0), (2, 0), (3, 0), (3, part))
        mine = (from_x, from_y, left, right)
        other = tuple(other_core(piece) for piece in mine[:2])
        other += tuple(other_core(after(piece, *late)) for piece in mine[2:])
        return spots, rows, mine, other
    else:
        blocks = gather_group(near[0])
        spots = tuple((i, 0) for i in range(1, count))
        mine = tuple(blocks[i * height : (i + 1) * height] for i in range(1, count))
    return spots, rows, mine, tuple(other_core(piece) for piece in mine)


def gather_stacked(pieces, *before):
    stack = after(jnp.stack(pieces), *before)
    return (), lax.all_gather(stack, ("core", "fsdp"), axis=0, tiled=False), (), ()


def assemble(spots, own_ref, mine_refs, other_refs, full_ref, sems):
    grp, core = lax.axis_index("grp"), lax.axis_index("core")
    if len(own_ref.shape) == 4:
        count = own_ref.shape[1]
        copies = [
            pltpu.make_async_copy(own_ref.at[:, i], full_ref.at[grp ^ i], sems.at[i])
            for i in range(count)
        ]
        for copy in copies:
            copy.start()
        return copies
    height, half = own_ref.shape[0], full_ref.shape[1] // 2

    def rows_of(step):
        return pl.ds(pl.multiple_of((grp ^ step) * height, height), height)

    copies = [pltpu.make_async_copy(own_ref, full_ref.at[rows_of(0), :], sems.at[0])]
    for place, (step, offset) in enumerate(spots):
        for side, refs in ((core, mine_refs), (1 - core, other_refs)):
            width = refs[place].shape[1]
            start = pl.multiple_of(side * half + offset, 128)
            copies.append(
                pltpu.make_async_copy(
                    refs[place],
                    full_ref.at[rows_of(step), pl.ds(start, width)],
                    sems.at[len(copies)],
                )
            )
    for copy in copies:
        copy.start()
    return copies


def call(kernel, outs, ins, anys=(), scratch=()):
    whole = pl.BlockSpec(memory_space=pltpu.VMEM)
    left = pl.BlockSpec(memory_space=pl.ANY)
    return pl.pallas_call(
        kernel,
        out_shape=[jax.ShapeDtypeStruct(shape, dtype) for shape, dtype in outs],
        in_specs=[whole] * len(ins) + [left] * len(anys),
        out_specs=[whole] * len(outs),
        scratch_shapes=list(scratch),
        compiler_params=pltpu.CompilerParams(vmem_limit_bytes=VMEM_BYTES),
    )(*ins, *anys)


def weight_scratch(gathered, shape):
    spots, own, mine, other = gathered
    if len(own.shape) == 4:
        parts, count, rows, width = own.shape
        return [
            pltpu.VMEM((count, parts, rows, width), bf16),
            pltpu.SemaphoreType.DMA((count,)),
        ]
    return [
        pltpu.VMEM(shape, bf16),
        pltpu.SemaphoreType.DMA((1 + 2 * len(mine),)),
    ]


def weight_args(gathered):
    spots, own, mine, other = gathered
    return [own, *mine, *other]


def weight_refs(gathered, refs):
    count = len(gathered[2])
    return gathered[0], refs[0], refs[1 : 1 + count], refs[1 + count : 1 + 2 * count]


def rope(values, cosine, sine):
    return values * cosine + pltpu.roll(values, HD // 2, 1) * sine


def half_span(run, rows):
    return slice(run * rows // 2, (run + 1) * rows // 2)


def run_span(run, head, heads, rows):
    start = (run * H + head) * (rows // 2)
    return slice(start, start + heads * (rows // 2))


def project_kernel(gathered, refs):
    hidden, gain, bias, cosine, sine = refs[:5]
    count = 1 + 2 * len(gathered[2])
    pieces = refs[5 : 5 + count]
    normed, queries, pairs, weight, sems = refs[5 + count :]
    copies = assemble(*weight_refs(gathered, pieces), weight, sems)
    inputs = hidden[...].astype(f32)
    normed[...] = low(inputs * rms_scale(inputs) * gain[...])
    for copy in copies:
        copy.wait()
    rows = hidden.shape[0]
    half = weight.shape[1] // 2
    heads_half = half // HD
    for side in range(2):
        lin = (
            matmul(normed[...], weight[:, side * half : (side + 1) * half])
            + bias[:, side * half : (side + 1) * half]
        )
        for spot in range(heads_half):
            head = side * heads_half + spot
            part = lin[:, spot * HD : (spot + 1) * HD]
            if head < H + KV:
                part = rope(part, cosine[...], sine[...])
            if head < H:
                for run in range(2):
                    queries[run_span(run, head, 1, rows), :] = low(part)[half_span(run, rows)]
            else:
                pairs[:, (head - H) * HD : (head - H + 1) * HD] = low(part)


def fetch_pairs(refs, full_ref, sems):
    half = refs[0].shape[0] // 2
    copies = []
    for run in range(2):
        for i, ref in enumerate(refs):
            place = run * len(refs) + i
            copies.append(
                pltpu.make_async_copy(
                    ref.at[pl.ds(run * half, half), :],
                    full_ref.at[pl.ds(place * half, half), :],
                    sems.at[place],
                )
            )
    for copy in copies:
        copy.start()
    return copies


def allowed_keys(run, key_places, own_places):
    extent = key_places.shape[1] // 2 * (run + 1)
    own = own_places[half_span(run, own_places.shape[0]), :]
    own = jnp.concatenate([own] * (H // KV), axis=0)
    return extent, key_places[:, :extent] <= own


def attend_kernel(blocks, refs):
    queries, key_places, own_places = refs[:3]
    pair_refs = refs[3 : 3 + blocks]
    mixed, log_sums, pairs, pair_sems = refs[3 + blocks :]
    for copy in fetch_pairs(pair_refs, pairs, pair_sems):
        copy.wait()
    rows = own_places.shape[0]
    half = rows // 2
    scale = HD ** (-0.5)
    group_size = H // KV
    for run in range(2):
        extent, allowed = allowed_keys(run, key_places, own_places)
        for group in range(KV):
            keys = pairs[:extent, group * HD : (group + 1) * HD]
            values = pairs[:extent, (KV + group) * HD : (KV + group + 1) * HD]
            span = run_span(run, group * group_size, group_size, rows)
            scores = jnp.where(allowed, matmul_nt(queries[span, :], keys) * scale, neg_large)
            top = jnp.max(scores, axis=1, keepdims=True)
            terms = jnp.exp(scores - top)
            total = jnp.sum(terms, axis=1, keepdims=True)
            log_sums[span, :] = top + jnp.log(total)
            result = low(matmul(low(terms * (1.0 / total)), values))
            for spot in range(group_size):
                head = group * group_size + spot
                mixed[half_span(run, rows), head * HD : (head + 1) * HD] = result[
                    spot * half : (spot + 1) * half
                ]


def output_kernel(gathered, refs):
    mixed, hidden, gain = refs[:3]
    count = 1 + 2 * len(gathered[2])
    pieces = refs[3 : 3 + count]
    middle, normed_two, weight, sems = refs[3 + count :]
    for copy in assemble(*weight_refs(gathered, pieces), weight, sems):
        copy.wait()
    full = weight[...].reshape(mixed.shape[1], -1)
    result = hidden[...].astype(f32) + matmul(mixed[...], full)
    middle[...] = result
    normed_two[...] = low(result * rms_scale(result) * gain[...])


def norm_back(delta, values, gain):
    scale = rms_scale(values)
    unit = values * scale
    scaled = delta * gain
    return scale * (scaled - unit * jnp.mean(scaled * unit, axis=-1, keepdims=True)), unit


def middle_kernel(gathered, refs):
    normed_delta, middle, cotangent, gain = refs[:4]
    count = 1 + 2 * len(gathered[2])
    pieces = refs[4 : 4 + count]
    middle_delta, attention_low, mixed_delta, gain_part, weight, sems = refs[4 + count :]
    copies = assemble(*weight_refs(gathered, pieces), weight, sems)
    delta = normed_delta[...].astype(f32)
    term, unit = norm_back(delta, middle[...], gain[...])
    gain_part[...] = jnp.sum(delta * unit, axis=0, keepdims=True)
    result = cotangent[...].astype(f32) + term
    middle_delta[...] = result
    attention_low[...] = low(result)
    for copy in copies:
        copy.wait()
    rows = middle.shape[0]
    mixed = matmul_nt(low(result), weight[...].reshape(-1, result.shape[1]))
    for head in range(H):
        part = low(mixed[:, head * HD : (head + 1) * HD])
        for run in range(2):
            mixed_delta[run_span(run, head, 1, rows), :] = part[half_span(run, rows)]


def attend_back_kernel(blocks, refs):
    queries, mixed_delta, log_sums, key_places, own_places, cosine, sine, attention_low = refs[:8]
    pair_refs = refs[8 : 8 + blocks]
    deltas, bias_part, pair_mine, pair_other, pairs, pair_sems = refs[8 + blocks :]
    split = attention_low.shape[1]
    deltas[:, :split] = attention_low[...]
    for copy in fetch_pairs(pair_refs, pairs, pair_sems):
        copy.wait()
    rows = own_places.shape[0]
    half = rows // 2
    scale = HD ** (-0.5)
    group_size = H // KV
    for group in range(KV):
        key_span = slice(group * HD, (group + 1) * HD)
        value_span = slice((KV + group) * HD, (KV + group + 1) * HD)
        sums = []
        for run in range(2):
            extent, allowed = allowed_keys(run, key_places, own_places)
            keys, values = pairs[:extent, key_span], pairs[:extent, value_span]
            span = run_span(run, group * group_size, group_size, rows)
            query, mixed = queries[span, :], mixed_delta[span, :]
            scores = matmul_nt(query, keys) * scale
            probs = jnp.where(allowed, jnp.exp(scores - log_sums[span, :]), 0.0)
            prob_delta = matmul_nt(mixed, values)
            dots = jnp.sum(probs * prob_delta, axis=1, keepdims=True)
            score_delta = low(probs * (prob_delta - dots))
            turn = matmul(score_delta, keys) * scale
            here = half_span(run, rows)
            for spot in range(group_size):
                head = group * group_size + spot
                head_span = slice(head * HD, (head + 1) * HD)
                part = turn[spot * half : (spot + 1) * half]
                part = low(rope(part, cosine[here, :], sine[here, :]))
                deltas[here, split + head * HD : split + (head + 1) * HD] = part
                bias = jnp.sum(part.astype(f32), axis=0, keepdims=True)
                bias_part[:, head_span] = bias if run == 0 else bias_part[:, head_span] + bias
            sums.append((inner(score_delta, query) * scale, inner(low(probs), mixed)))
        early = sums[1][0].shape[0] // 2
        for which, to in enumerate((key_span, value_span)):
            first = sums[0][which] + sums[1][which][:early]
            for run, part in enumerate((first, sums[1][which][early:])):
                for block in range(blocks):
                    piece = part[block * half : (block + 1) * half]
                    start = block % (blocks // 2) * rows + run * half
                    if block < blocks // 2:
                        pair_mine[start : start + half, to] = piece
                    else:
                        pair_other[start : start + half, to] = low(piece)


def pair_split_kernel(refs):
    mine, received, own = refs[:3]
    rows = own.shape[0]
    own[...] = mine[:rows] + received[:rows].astype(f32)
    for place, part in enumerate(refs[3:], 1):
        span = slice(place * rows, (place + 1) * rows)
        part[...] = low(mine[span] + received[span].astype(f32))


def pair_sum_kernel(parts, refs):
    own = refs[0]
    cosine, sine, pair_delta, bias_part = refs[1 + parts :]
    total = own[...]
    for part in refs[1 : 1 + parts]:
        total = total + part[...].astype(f32)
    for spot in range(2 * KV):
        span = slice(spot * HD, (spot + 1) * HD)
        part = total[:, span]
        if spot < KV:
            part = rope(part, cosine[...], sine[...])
        part = low(part)
        pair_delta[:, span] = part
        bias_part[:, span] = jnp.sum(part.astype(f32), axis=0, keepdims=True)


def weight_grad_kernel(places, split, refs):
    mixed, unit = refs[:2]
    pieces = refs[2 : 2 + len(places)]
    result, deltas, sems = refs[2 + len(places) :]
    grp = lax.axis_index("grp")
    copies = []
    for place, piece in enumerate(pieces):
        step, start = places[place]
        rows, width = piece.shape
        row = pl.multiple_of((grp ^ step) * rows, rows)
        copies.append(
            pltpu.make_async_copy(
                piece, deltas.at[pl.ds(row, rows), pl.ds(start, width)], sems.at[place]
            )
        )
    for copy in copies:
        copy.start()
    for copy in copies:
        copy.wait()
    parts = low(inner(mixed[...], deltas[:, :split])), low(inner(unit[...], deltas[:, split:]))
    cores, devices = 2, lax.axis_size("fsdp")
    rows = result.shape[0] // (cores * devices)
    if rows % 16:
        result[:, :split], result[:, split:] = parts
        return
    for device in range(devices):
        for core in range(cores):
            here = (device * cores + core) * rows
            there = (core * devices + device) * rows
            for part, span in zip(parts, (slice(0, split), slice(split, None))):
                result[here : here + rows, span] = part[there : there + rows]


def weight_grad(mixed, unit, split, *gathered):
    places, pieces, start = [], [], 0
    for group in gathered:
        places += [(step, start + offset) for step, offset in plane_spots(group)]
        pieces += group
        start += group[0].shape[1]
    (part,) = call(
        lambda *refs: weight_grad_kernel(places, split, refs),
        [((unit.shape[1], start), bf16)],
        [mixed, unit],
        pieces,
        [pltpu.VMEM((unit.shape[0], start), bf16), pltpu.SemaphoreType.DMA((len(pieces),))],
    )
    return part


def forward_back_kernel(count, refs):
    normed, active_delta = refs[:2]
    pieces = refs[2 : 2 + 2 * (count + 1)]
    active, deltas, normed_delta, weights, sems = refs[2 + 2 * (count + 1) :]
    rows, width = pieces[0].shape
    slot = weights.shape[1] // count

    @pl.when(pl.program_id(0) == 0)
    def fetch():
        copies = []
        for which in range(2):
            for place in range(count + 1):
                piece = pieces[which * (count + 1) + place]
                step = min(place, count - 1)
                start = width // 2 if place == count else 0
                copies.append(
                    pltpu.make_async_copy(
                        piece,
                        weights.at[which, pl.ds(step * slot, rows), pl.ds(start, piece.shape[1])],
                        sems.at[len(copies)],
                    )
                )
        for copy in copies:
            copy.start()
        for copy in copies:
            copy.wait()
        if slot > rows:
            for which in range(2):
                for step in range(count):
                    spare = slice(step * slot + rows, (step + 1) * slot)
                    weights[which, spare, :] = jnp.zeros((slot - rows, width), bf16)

    gate = matmul_nt(normed[...], weights[0])
    upward = matmul_nt(normed[...], weights[1])
    delta = active_delta[...].astype(f32)
    sigmoid = 1.0 / (1.0 + jnp.exp(-gate))
    silu = gate * sigmoid
    active[0] = low(silu * upward)
    gate_low = low(delta * upward * (sigmoid * (1.0 + gate * (1.0 - sigmoid))))
    up_low = low(delta * silu)
    deltas[0] = gate_low
    deltas[1] = up_low
    normed_delta[...] = low(matmul(gate_low, weights[0]) + matmul(up_low, weights[1]))


def forward_back(normed_all, active_delta, pieces):
    tokens, width = normed_all.shape
    units = active_delta.shape[1]
    tile = 256

    def tiles(columns):
        return pl.BlockSpec((tile, columns), lambda i: (i, 0))

    count = len(pieces) // 2 - 1
    return pl.pallas_call(
        lambda *refs: forward_back_kernel(count, refs),
        grid=(tokens // tile,),
        out_shape=[
            jax.ShapeDtypeStruct((1, tokens, units), bf16),
            jax.ShapeDtypeStruct((2, tokens, units), bf16),
            jax.ShapeDtypeStruct((tokens, width), bf16),
        ],
        in_specs=[tiles(width), tiles(units)] + [pl.BlockSpec(memory_space=pl.ANY)] * len(pieces),
        out_specs=[
            pl.BlockSpec((1, tile, units), lambda i: (0, i, 0)),
            pl.BlockSpec((2, tile, units), lambda i: (0, i, 0)),
            tiles(width),
        ],
        scratch_shapes=[
            pltpu.VMEM((2, units, width), bf16),
            pltpu.SemaphoreType.DMA((len(pieces),)),
        ],
        compiler_params=pltpu.CompilerParams(vmem_limit_bytes=VMEM_BYTES),
    )(normed_all, active_delta, *pieces)


def outer_kernel(refs):
    left, right, own, for_x, for_y, far_left, far_right = refs
    rows = own.shape[1]
    slot = left.shape[2] // 4
    total = inner(left[0], right[...])
    for place, part in enumerate((own, for_x, for_y)):
        part[0] = low(total[place * slot : place * slot + rows])
    far = low(total[3 * slot : 3 * slot + rows])

    @pl.when(pl.program_id(1) == 0)
    def first():
        far_left[0] = far

    @pl.when(pl.program_id(1) == 1)
    def second():
        far_right[0] = far


def outer(left, right, rows):
    stack, tokens, units = left.shape
    half = right.shape[1] // 2
    wide = jax.ShapeDtypeStruct((stack, rows, 2 * half), bf16)
    narrow = jax.ShapeDtypeStruct((stack, rows, half), bf16)
    by_half = pl.BlockSpec((1, rows, half), lambda i, j: (i, 0, j))
    whole = pl.BlockSpec((1, rows, half), lambda i, j: (i, 0, 0))
    return pl.pallas_call(
        lambda *refs: outer_kernel(refs),
        grid=(stack, 2),
        out_shape=[wide, wide, wide, narrow, narrow],
        in_specs=[
            pl.BlockSpec((1, tokens, units), lambda i, j: (i, 0, 0)),
            pl.BlockSpec((tokens, half), lambda i, j: (0, j)),
        ],
        out_specs=[by_half, by_half, by_half, whole, whole],
        compiler_params=pltpu.CompilerParams(vmem_limit_bytes=VMEM_BYTES),
    )(left, right)


def scatter_far(parts):
    own, for_x, for_y, far_left, far_right = parts
    from_x = exchange(far_left, 1)
    from_y = exchange(far_right, 2)
    spare = jnp.zeros_like(from_x)
    to_y = low(for_y.astype(f32) + jnp.concatenate([from_x, spare], axis=2).astype(f32))
    to_x = low(for_x.astype(f32) + jnp.concatenate([spare, from_y], axis=2).astype(f32))
    return to_x, to_y


def scatter_near(own, from_x, from_y, late):
    from_x, from_y = after((from_x, from_y), late)
    return own.astype(f32) + from_x.astype(f32) + from_y.astype(f32)


def turn_kernel(refs):
    own, from_x, from_y = refs[:3]
    for place, out in enumerate(refs[3:]):
        total = own[place].astype(f32) + from_x[place].astype(f32) + from_y[place].astype(f32)
        out[...] = total.T


def turned_sums(own, from_x, from_y, late):
    from_x, from_y = after((from_x, from_y), late)
    stack, rows, width = own.shape
    tile = width // 3 if width % 384 == 0 else width
    return pl.pallas_call(
        lambda *refs: turn_kernel(refs),
        grid=(width // tile,),
        out_shape=[jax.ShapeDtypeStruct((width, rows), f32)] * stack,
        in_specs=[pl.BlockSpec((stack, rows, tile), lambda i: (0, 0, i))] * 3,
        out_specs=[pl.BlockSpec((tile, rows), lambda i: (i, 0))] * stack,
        compiler_params=pltpu.CompilerParams(vmem_limit_bytes=VMEM_BYTES),
    )(own, from_x, from_y)


def finish_kernel(gathered, refs):
    deltas, pair_delta, hidden, middle_delta, gain = refs[:5]
    count = 1 + 2 * len(gathered[2])
    pieces = refs[5 : 5 + count]
    input_delta, weight, sems = refs[5 + count :]
    copies = assemble(*weight_refs(gathered, pieces), weight, sems)
    for copy in copies:
        copy.wait()
    split = weight.shape[1] - pair_delta.shape[1]
    delta = matmul_nt(deltas[:, -split:], weight[:, :split]) + matmul_nt(
        pair_delta[...], weight[:, split:]
    )
    term, unit = norm_back(delta, hidden[...].astype(f32), gain[...])
    input_delta[...] = middle_delta[...] + term


def sum_over(values, *axes):
    for axis in axes:
        count = lax.axis_size(axis)
        bit = 1
        while bit < count:
            values = values + lax.ppermute(values, axis, [(i, i ^ bit) for i in range(count)])
            bit *= 2
    return values


def local(
    hidden,
    positions,
    first_gain,
    query_weight,
    key_weight,
    value_weight,
    query_bias,
    key_bias,
    value_bias,
    output_weight,
    second_gain,
    gate_weight,
    up_weight,
    down_weight,
    cotangent,
):
    rows = hidden.shape[0]
    width = hidden.shape[1]
    ctx_here = lax.axis_index("grp") * lax.axis_size("core") + lax.axis_index("core")
    own_places = lax.dynamic_slice_in_dim(positions, ctx_here * rows, rows)
    q_width, k_width = H * HD, KV * HD

    near = lax.axis_size("grp") == 4 and gate_weight.shape[1] % 8 == 0
    projections = jnp.concatenate([query_weight, key_weight, value_weight], axis=1)
    qkv_rows = gather_rows(projections)

    def columns(values):
        return lax.all_to_all(values, "grp", split_axis=1, concat_axis=0, tiled=True)

    inputs = hidden.astype(f32)
    unit = low(inputs * rms_scale(inputs))
    gate_own, up_own = gate_weight.T, up_weight.T
    small = jnp.concatenate([first_gain, second_gain, query_bias, key_bias, value_bias])
    devices = lax.axis_size(EVERY)
    device_here = lax.axis_index(EVERY)
    small_plane = sum_over(
        lax.dynamic_update_slice_in_dim(
            jnp.zeros((devices, small.shape[0]), jnp.float32),
            small.astype(jnp.float32)[None],
            device_here,
            0,
        ),
        "grp",
    )
    output_chips = gather_chips(output_weight)
    small_all = sum_over(small_plane, "core", "fsdp")
    down_near = gather_near(after(down_weight, small_plane, *output_chips[1:])) if near else ()
    down_pieces = gather_far(down_weight, down_near, small_all) if near else ()
    qkv_rows = after(qkv_rows, small_all, *down_near)
    qkv_near = weight_near(qkv_rows)
    own = width // devices
    kv_own = k_width // devices
    gain_one = small_all[:, :own].reshape(1, width)
    gain_two = small_all[:, own : 2 * own].reshape(1, width)
    bias_qkv = jnp.concatenate(
        [
            small_all[:, 2 * own : 3 * own].reshape(q_width),
            small_all[:, 3 * own : 3 * own + kv_own].reshape(k_width),
            small_all[:, 3 * own + kv_own :].reshape(k_width),
        ]
    ).reshape(1, -1)
    cotangent_all = lax.all_gather(cotangent, TP_AXES, axis=0, tiled=True)

    cosine, sine = rope_tables(own_places)
    places = positions.reshape(-1, rows)
    steps = jnp.arange(places.shape[0], dtype=jnp.int32)
    from_ctx = ctx_here ^ jnp.concatenate([steps[0::2], steps[1::2]])
    matches = from_ctx[:, None] == steps[None, :]
    key_places = jnp.sum(jnp.where(matches[:, :, None], places[None], 0), axis=1)
    key_places = key_places.reshape(-1, 2, rows // 2).transpose(1, 0, 2).reshape(1, -1)
    unit_columns = columns(unit)
    ready = (unit_columns, gain_one, gain_two, bias_qkv, cosine, sine, key_places)
    weight_qkv = gather_weight(qkv_rows, qkv_near, ready)
    if output_weight.shape[0] % 16:
        output_rows = gather_rows(output_weight, qkv_rows)
        weight_output = gather_weight(output_rows, weight_near(output_rows))
    else:
        weight_output = gather_stacked(output_chips, qkv_rows)

    normed, queries, pairs_local = call(
        lambda *refs: project_kernel(weight_qkv, refs),
        [((rows, width), bf16), ((H * rows, HD), bf16), ((rows, 2 * k_width), bf16)],
        [hidden, gain_one, bias_qkv, cosine, sine],
        weight_args(weight_qkv),
        weight_scratch(weight_qkv, (width, q_width + 2 * k_width)),
    )
    pairs = gather_small(pairs_local)
    blocks = len(pairs)
    length = blocks * rows
    query_places = own_places.reshape(rows, 1)
    pair_scratch = [
        pltpu.VMEM((length, 2 * k_width), bf16),
        pltpu.SemaphoreType.DMA((2 * blocks,)),
    ]
    mixed_low, log_sums = call(
        lambda *refs: attend_kernel(blocks, refs),
        [((rows, q_width), bf16), ((H * rows, 1), f32)],
        [queries, key_places, query_places],
        pairs,
        pair_scratch,
    )
    arrived = pairs[1 : blocks // 2]
    gate_near = gather_near(after(gate_own, *arrived)) if near else ()
    up_near = gather_near(after(up_own, *gate_near)) if near else ()
    middle, normed_two = call(
        lambda *refs: output_kernel(weight_output, refs),
        [((rows, width), f32), ((rows, width), bf16)],
        [mixed_low, hidden, gain_two],
        weight_args(weight_output),
        weight_scratch(weight_output, (q_width, width)),
    )
    normed_two = after(normed_two, *gate_near)


    normed_all = lax.all_gather(normed_two, TP_AXES, axis=0, tiled=True)
    mixed_columns = columns(after(mixed_low, normed_two))
    normed_all = after(normed_all, mixed_columns)
    if near:
        down_rows = join(down_pieces)
    else:
        down_rows = gather_group(down_weight)
    active_delta = low(matmul_nt(cotangent_all, down_rows))
    if near:
        active, unit_deltas, normed_two_part = forward_back(
            normed_all,
            active_delta,
            gather_far(gate_own, gate_near) + gather_far(up_own, up_near),
        )
    else:
        gate_rows, up_rows = gather_group(gate_own), gather_group(up_own)
        gate = matmul_nt(normed_all, gate_rows)
        upward = matmul_nt(normed_all, up_rows)
        delta = active_delta.astype(f32)
        sigmoid = 1.0 / (1.0 + jnp.exp(-gate))
        silu = gate * sigmoid
        active = low(silu * upward)
        gate_delta = low(delta * upward * (sigmoid * (1.0 + gate * (1.0 - sigmoid))))
        up_delta = low(delta * silu)
        normed_two_part = low(matmul(gate_delta, gate_rows) + matmul(up_delta, up_rows))
    normed_two_delta = lax.psum_scatter(
        normed_two_part, TP_AXES, scatter_dimension=0, tiled=True
    )
    unit_rows = down_weight.shape[0]
    if near:
        down_parts = outer(active, cotangent_all, unit_rows)
        down_to = scatter_far(down_parts)
        both_parts = outer(after(unit_deltas, down_parts[0]), normed_all, unit_rows)
        both_to = scatter_far(both_parts)
        active = after(active[0], down_parts[0])
    out_part = matmul(active, down_rows)
    if near:
        normed_two_delta = after(normed_two_delta, both_parts[0], out_part, *down_to)
    out_sum = lax.psum_scatter(low(out_part), TP_AXES, scatter_dimension=0, tiled=True)

    middle_delta, attention_low, mixed_delta, second_gain_part = call(
        lambda *refs: middle_kernel(weight_output, refs),
        [
            ((rows, width), f32),
            ((rows, width), bf16),
            ((H * rows, HD), bf16),
            ((1, width), f32),
        ],
        [normed_two_delta, middle, cotangent, gain_two],
        weight_args(weight_output),
        weight_scratch(weight_output, (q_width, width)),
    )
    deltas, query_bias_part, pair_mine, pair_other = call(
        lambda *refs: attend_back_kernel(blocks, refs),
        [
            ((rows, width + q_width), bf16),
            ((1, q_width), f32),
            ((length // 2, 2 * k_width), f32),
            ((length // 2, 2 * k_width), bf16),
        ],
        [
            queries,
            mixed_delta,
            log_sums,
            key_places,
            query_places,
            cosine,
            -sine,
            attention_low,
        ],
        pairs,
        pair_scratch,
    )
    if near:
        pair_mine = after(pair_mine, *both_to)
    cuts = call(
        lambda *refs: pair_split_kernel(refs),
        [((rows, 2 * k_width), f32)] + [((rows, 2 * k_width), bf16)] * (blocks // 2 - 1),
        [pair_mine, other_core(pair_other)],
    )
    pair_delta, pair_bias_part = call(
        lambda *refs: pair_sum_kernel(blocks // 2 - 1, refs),
        [((rows, 2 * k_width), bf16), ((1, 2 * k_width), f32)],
        [cuts[0]] + [exchange(cut, i) for i, cut in enumerate(cuts[1:], 1)] + [cosine, -sine],
    )
    small_plane = sum_over(
        jnp.concatenate([second_gain_part, query_bias_part, pair_bias_part], axis=1), "grp"
    )
    delta_pieces, pair_pieces = gather_plane(deltas, pair_delta), gather_chips(pair_delta)
    grad_part = weight_grad(mixed_columns, unit_columns, width, delta_pieces, pair_pieces)
    order = ("core", "fsdp") if output_weight.shape[0] % 16 else TP_AXES
    grads = lax.psum_scatter(grad_part, order, scatter_dimension=0, tiled=True).astype(f32)
    output_grad, unit_grad = grads[:, :width], grads[:, width:]
    (input_delta,) = call(
        lambda *refs: finish_kernel(weight_qkv, refs),
        [((rows, width), f32)],
        [deltas, pair_delta, hidden, middle_delta, gain_one],
        weight_args(weight_qkv),
        weight_scratch(weight_qkv, (width, q_width + 2 * k_width)),
    )
    first_gain_grad = jnp.sum(unit_grad * projections.astype(f32), axis=1)
    scaled_grad = unit_grad * first_gain.astype(f32)[:, None]

    if near:
        both_to = after(both_to, *delta_pieces, *pair_pieces, small_plane)
        both_from = exchange(both_to[0], 1), exchange(both_to[1], 2)
        down_to = after(down_to, pair_delta)
        down_from = exchange(down_to[0], 1), exchange(down_to[1], 2)
        down_grad = scatter_near(down_parts[0], *down_from, scaled_grad)[0]
        gate_grad, up_grad = turned_sums(both_parts[0], *both_from, (scaled_grad, first_gain_grad))
    else:
        down_grad = scatter_group(inner(active, cotangent_all), unit_rows)
        gate_grad = scatter_group(inner(gate_delta, normed_all), unit_rows).T
        up_grad = scatter_group(inner(up_delta, normed_all), unit_rows).T
    layer_out = low(middle + after(out_sum, pair_delta).astype(f32))

    small_sum = sum_over(small_plane, "core", "fsdp")[0]

    def own_part(start, size):
        return lax.dynamic_slice_in_dim(small_sum, start + device_here * size, size)

    return (
        layer_out,
        input_delta,
        first_gain_grad,
        scaled_grad[:, :q_width],
        scaled_grad[:, q_width : q_width + k_width],
        scaled_grad[:, q_width + k_width :],
        own_part(width, own),
        own_part(width + q_width, kv_own),
        own_part(width + q_width + k_width, kv_own),
        output_grad,
        own_part(0, own),
        gate_grad,
        up_grad,
        down_grad,
    )


def solution(mesh):
    cores = 2
    ctx, fsdp = mesh.shape["ctx"], mesh.shape["fsdp"]
    split = Mesh(mesh.devices.reshape(ctx // cores, cores, fsdp), EVERY)
    tokens = P(("fsdp", "grp", "core"), None)
    in_specs = (
        tokens,
        P("fsdp"),
        P(EVERY),
        P(EVERY, None),
        P(EVERY, None),
        P(EVERY, None),
        P(EVERY),
        P(EVERY),
        P(EVERY),
        P(EVERY, None),
        P(EVERY),
        P(None, EVERY),
        P(None, EVERY),
        P(EVERY, None),
        tokens,
    )
    out_specs = (
        tokens,
        tokens,
        P(EVERY),
        P(EVERY, None),
        P(EVERY, None),
        P(EVERY, None),
        P(EVERY),
        P(EVERY),
        P(EVERY),
        P(EVERY, None),
        P(EVERY),
        P(None, EVERY),
        P(None, EVERY),
        P(EVERY, None),
    )
    return jax.shard_map(local, mesh=split, in_specs=in_specs, out_specs=out_specs, check_vma=False)
```
